256 devices in a mesh: ctx: 64 (over x, z, core), head: 4 (over y).
Axes of the slice: x: 4, y: 4, z: 8, core: 2. Of those that a mesh axis runs over, the one named last changes fastest.
Arguments:
- lin_query: bfloat16 [8192, 8192], P('ctx', 'head'), may hold values from -6 to 6
- lin_key: bfloat16 [8192, 8192], P('ctx', 'head'), may hold values from -6 to 6
- lin_value: bfloat16 [8192, 8192], P('ctx', 'head'), may hold values from -6 to 6
- log_decay: float32 [8192, 64], P('ctx', 'head'), may hold values from -1 to 0, as said below
- soft_query: bfloat16 [8192, 8192], P('ctx', 'head'), may hold values from -24 to 24
- soft_key: bfloat16 [8192, 8192], P('ctx', 'head'), may hold values from -24 to 24
- soft_value: bfloat16 [8192, 8192], P('ctx', 'head'), may hold values from -6 to 6
Outputs:
- lin_out: bfloat16 [8192, 8192], P('ctx', 'head')
- soft_out: bfloat16 [8192, 8192], P('ctx', 'head')
The draws below stay inside these ranges and needn't reach their ends.
Inputs may be any that keep to these rules, and one draw needn't show every extreme that they name: `log_decay`: never positive.
All inputs are finite; a program needn't handle non-finite values.
Results may differ from the reference program's by a relative error of at most 0.0065.
Values may be sent and summed in bfloat16 or wider, within the bound.
No kernel may reach another device: no remote copies, remote signals or barrier semaphores. Data moves between devices by JAX's collectives and lax.ppermute only.
A program may use at most 192 MiB of HBM per device.

```python
import jax
import jax.numpy as jnp
from jax import lax

HEADS = 64
HEAD_DIM = 128
TOK_DEV = 128
SEQ = 8192


def soft_pair(key):
    base_key = jax.random.fold_in(key, 11)
    key_query, key_keys = jax.random.split(base_key, 2)
    width_all = HEADS * HEAD_DIM
    queries = jnp.clip(jax.random.normal(key_query, (SEQ, width_all), jnp.float32), -4.0, 4.0)
    keys_all = jnp.clip(jax.random.normal(key_keys, (SEQ, width_all), jnp.float32), -4.0, 4.0)
    return (queries, keys_all)


def draw_soft_query(key, part):
    return soft_pair(key)[0].astype(jnp.bfloat16)


def draw_soft_key(key, part):
    return soft_pair(key)[1].astype(jnp.bfloat16)


def draw_log_decay(key, part):
    base_key = jax.random.fold_in(key, 23)
    key_kind, key_fast, key_slow, key_block, key_token, key_where, key_loss = jax.random.split(base_key, 7)
    fast_share = 0.5
    fast_heads = jax.random.uniform(key_kind, (HEADS,), jnp.float32) < fast_share
    fast_rate = jnp.exp(jax.random.uniform(key_fast, (HEADS,), jnp.float32, jnp.log(0.5), jnp.log(3.0))) / TOK_DEV
    slow_rate = jnp.exp(jax.random.uniform(key_slow, (HEADS,), jnp.float32, jnp.log(0.05), jnp.log(0.3))) / SEQ
    head_rate = jnp.where(fast_heads, fast_rate, slow_rate)
    block_width = jnp.where(fast_heads, jnp.log(4.0), jnp.log(2.0))
    block_unit = jax.random.uniform(key_block, (SEQ // TOK_DEV, HEADS), jnp.float32, -1.0, 1.0)
    block_factor = jnp.exp(block_unit * block_width[None, :])
    block_factor = jnp.repeat(block_factor, TOK_DEV, axis=0)
    token_factor = jnp.exp(jax.random.uniform(key_token, (SEQ, HEADS), jnp.float32, -jnp.log(2.0), jnp.log(2.0)))
    log_retention = jnp.maximum(-head_rate[None, :] * block_factor * token_factor, -0.45)
    third_len = SEQ // 3
    token_slots = jnp.arange(3, dtype=jnp.int32)[:, None] * third_len + jax.random.randint(key_where, (3, HEADS), 0, third_len)
    decay_losses = jax.random.uniform(key_loss, (3, HEADS), jnp.float32, 0.2, 0.4)
    token_positions = jnp.arange(SEQ)[:, None]
    for segment_index in range(3):
        log_retention = log_retention + jnp.where(token_positions == token_slots[segment_index][None, :], jnp.log(1.0 - decay_losses[segment_index])[None, :], 0.0)
    return log_retention


def level_of(stream_key, extent, shards, low, top_value):
    loudness, own = 1.0, jax.random.fold_in(stream_key, 6)
    for axis_at, parts in shards:
        heights = jnp.exp(jax.random.uniform(jax.random.fold_in(own, axis_at), (parts,), jnp.float32, low / len(shards), top_value / len(shards)))
        loudness = loudness * jnp.repeat(heights, extent[axis_at] // parts).reshape([-1 if axis == axis_at else 1 for axis in range(len(extent))])
    return loudness


def normal_values(own_key, shape, scale, most, cuts=(), kind=jnp.bfloat16):
    values = jax.random.normal(own_key, shape, jnp.float32) * scale
    if len(cuts) > 0:
        values = level_of(own_key, shape, cuts, -0.22, 0.18) * values
    return jnp.clip(values, min=-most, max=most).astype(kind)


def setup_inputs(seed: int = 0) -> dict:
    arg_keys = jax.random.split(jax.random.key(seed), 8)
    return {
        "lin_query": normal_values(arg_keys[0], (SEQ, HEADS * HEAD_DIM), 1.0, 6.0, ((0, 64), (1, 4))),
        "lin_key": normal_values(arg_keys[1], (SEQ, HEADS * HEAD_DIM), 1.0, 6.0, ((0, 64), (1, 4))),
        "lin_value": normal_values(arg_keys[2], (SEQ, HEADS * HEAD_DIM), 1.0, 6.0, ((0, 64), (1, 4))),
        "log_decay": draw_log_decay(jax.random.fold_in(arg_keys[7], 71), 0),
        "soft_query": draw_soft_query(jax.random.fold_in(arg_keys[7], 71), 0),
        "soft_key": draw_soft_key(jax.random.fold_in(arg_keys[7], 71), 0),
        "soft_value": normal_values(arg_keys[6], (SEQ, HEADS * HEAD_DIM), 1.0, 6.0, ((0, 64), (1, 4))),
    }


norm_eps = 1e-06
masked_score = -1e+30

def rounded(array):
    return lax.optimization_barrier(array.astype(jnp.bfloat16)).astype(jnp.float32)

def lightning_block(carry_state, packed):
    query_group, key_blk, value_blk, decay_blk = packed
    query_wide = query_group.astype(jnp.float32)
    key_wide = key_blk.astype(jnp.float32)
    value_wide = value_blk.astype(jnp.float32)
    count_rows = decay_blk.shape[0]
    running_sum = jnp.cumsum(decay_blk, axis=0)
    ending = running_sum[-1]
    scores = jnp.einsum('thd,shd->hts', query_wide, key_wide, precision=lax.Precision.HIGHEST)
    causal = jnp.arange(count_rows)[:, None] >= jnp.arange(count_rows)[None, :]
    spread = running_sum.T[:, :, None] - running_sum.T[:, None, :]
    decayed = rounded(jnp.where(causal[None], jnp.exp(jnp.where(causal[None], spread, 0.0)), 0.0) * scores)
    inside = jnp.einsum('hts,shd->thd', decayed, value_wide, precision=lax.Precision.HIGHEST)
    query_scaled = rounded(query_wide * jnp.exp(running_sum)[:, :, None])
    outside = jnp.einsum('thd,hde->the', query_scaled, rounded(carry_state), precision=lax.Precision.HIGHEST)
    to_end = jnp.exp(ending[None, :] - running_sum)
    key_scaled = rounded(key_wide * to_end[:, :, None])
    block_state = jnp.einsum('shd,she->hde', key_scaled, value_wide, precision=lax.Precision.HIGHEST)
    new_state = jnp.exp(ending)[:, None, None] * carry_state + block_state
    total = inside + outside
    normed = total * lax.rsqrt(lax.optimization_barrier(jnp.mean(total * total, axis=-1, keepdims=True)) + norm_eps)
    return (new_state, normed.astype(jnp.bfloat16))

def softmax_head(packed):
    query_one, key_one, value_one = packed
    scores = jnp.dot(query_one, key_one.T, preferred_element_type=jnp.float32) * HEAD_DIM ** (-0.5)
    causal = jnp.arange(SEQ)[:, None] >= jnp.arange(SEQ)[None, :]
    scores = jnp.where(causal, scores, masked_score)
    peak = lax.optimization_barrier(jnp.max(scores, axis=-1, keepdims=True))
    expo = jnp.where(causal, jnp.exp(scores - peak), 0.0)
    weights = expo.astype(jnp.bfloat16)
    numer = jnp.dot(weights, value_one, preferred_element_type=jnp.float32)
    return (numer / lax.optimization_barrier(jnp.sum(expo, axis=-1, keepdims=True))).astype(jnp.bfloat16)

def reference(lin_query, lin_key, lin_value, log_decay, soft_query, soft_key, soft_value):
    blocks_count = SEQ // TOK_DEV
    shaped = (blocks_count, TOK_DEV, HEADS, HEAD_DIM)
    packed = (lin_query.reshape(shaped), lin_key.reshape(shaped), lin_value.reshape(shaped), log_decay.reshape(blocks_count, TOK_DEV, HEADS))
    start_state = jnp.zeros((HEADS, HEAD_DIM, HEAD_DIM), jnp.float32)
    final_state, lin_blocks = lax.scan(lightning_block, start_state, packed)
    lin_out = lin_blocks.reshape(SEQ, HEADS * HEAD_DIM)

    def per_head(array):
        return array.reshape(SEQ, HEADS, HEAD_DIM).transpose(1, 0, 2)
    soft_heads = lax.map(softmax_head, (per_head(soft_query), per_head(soft_key), per_head(soft_value)))
    soft_out = soft_heads.transpose(1, 0, 2).reshape(SEQ, HEADS * HEAD_DIM)
    return (lin_out, soft_out)
```

```python
import functools
import math

import jax
import jax.numpy as jnp
import numpy as np
from jax import lax
from jax.experimental import pallas as pl
from jax.experimental.pallas import tpu as pltpu
from jax.sharding import PartitionSpec as P

HEAD_DIM = 128
TOKENS = 128
HEADS_HERE = 16
BLOCKS = 64
PIECE = 32

norm_eps = 1e-06
masked_score = -1e30
exponent_scale = HEAD_DIM ** (-0.5) * math.log2(math.e)
X_STEP = 16
QUERY_TILE = 8


def place_of(device):
    x, z, core = device // 16, device // 2 % 8, device % 2
    return 2 * z + x // 2, 2 * (x % 2) + core


def columns(head):
    return slice(head * HEAD_DIM, (head + 1) * HEAD_DIM)


def rows(quarter):
    return slice(quarter * PIECE, (quarter + 1) * PIECE)


def whole():
    return pl.BlockSpec(memory_space=pltpu.VMEM)


def dot(left, right, left_dim, right_dim, precision=None):
    return lax.dot_general(
        left,
        right,
        (((left_dim,), (right_dim,)), ((), ())),
        precision=precision,
        preferred_element_type=jnp.float32,
    )


def call(kernel, out_shape, operands, flops, scratch=(), smem=0):
    bytes_in = sum(math.prod(o.shape) * o.dtype.itemsize for o in operands)
    bytes_out = math.prod(out_shape.shape) * out_shape.dtype.itemsize
    return pl.pallas_call(
        kernel,
        out_shape=out_shape,
        in_specs=[pl.BlockSpec(memory_space=pltpu.SMEM)] * smem
        + [whole() for _ in operands[smem:]],
        out_specs=whole(),
        scratch_shapes=list(scratch),
        compiler_params=pltpu.CompilerParams(vmem_limit_bytes=48 << 20),
        cost_estimate=pl.CostEstimate(
            flops=flops, bytes_accessed=bytes_in + bytes_out, transcendentals=0
        ),
    )(*operands)


def pack_keys_kernel(key_ref, value_ref, out_ref):
    for device in range(BLOCKS):
        head, quarter = place_of(device)
        out_ref[device, 0:PIECE, :] = key_ref[rows(quarter), columns(head)]
        out_ref[device, PIECE : 2 * PIECE, :] = value_ref[rows(quarter), columns(head)]


def lower_triangle():
    shape = (TOKENS, TOKENS)
    return lax.broadcasted_iota(jnp.int32, shape, 0) >= lax.broadcasted_iota(jnp.int32, shape, 1)


def running_sums(decay):
    ones = jnp.where(lower_triangle(), 1.0, 0.0).astype(jnp.float32)
    return dot(ones, decay, 1, 0, lax.Precision.HIGHEST)


def states_kernel(key_ref, value_ref, decay_ref, query_ref, out_ref):
    running_sum = running_sums(decay_ref[...])
    part = lax.broadcasted_iota(jnp.int32, (8, HEAD_DIM), 0)
    for head in range(HEADS_HERE):
        sums = running_sum[:, head : head + 1]
        ending = running_sum[TOKENS - 1 : TOKENS, head : head + 1]
        key_wide = key_ref[:, columns(head)].astype(jnp.float32)
        key_scaled = (key_wide * jnp.exp(ending - sums)).astype(jnp.bfloat16)
        state = dot(key_scaled, value_ref[:, columns(head)], 0, 0).astype(jnp.bfloat16)
        coarse = ending.astype(jnp.bfloat16).astype(jnp.float32)
        middle = (ending - coarse).astype(jnp.bfloat16).astype(jnp.float32)
        fine = ending - coarse - middle
        parts = jnp.where(part == 0, coarse, jnp.where(part == 1, middle, fine))
        parts = parts.astype(jnp.bfloat16)
        for quarter in range(4):
            out_ref[4 * head + quarter, PIECE : 2 * PIECE, :] = state[rows(quarter), :]
            out_ref[4 * head + quarter, 2 * PIECE :, :] = parts
    for device in range(BLOCKS):
        head, quarter = place_of(device)
        out_ref[device, 0:PIECE, :] = query_ref[rows(quarter), columns(head)]


def scan_kernel(moved_ref, out_ref):
    def step(block, carry):
        out_ref[block] = carry.astype(jnp.bfloat16)
        parts = moved_ref[block, 2 * PIECE :, :].astype(jnp.float32)
        ending = parts[0:1] + parts[1:2] + parts[2:3]
        state = moved_ref[block, PIECE : 2 * PIECE, :].astype(jnp.float32)
        return jnp.exp(ending) * carry + state

    lax.fori_loop(0, BLOCKS, step, jnp.zeros((PIECE, HEAD_DIM), jnp.float32), unroll=4)


def attention_kernel(quarter_ref, query_ref, kv0, kv1, kv2, kv3, out_ref, best_ref, total_ref):
    segments = (kv0, kv1, kv2, kv3)
    mine = quarter_ref[0]
    count = QUERY_TILE * PIECE
    ones = jnp.ones((count, HEAD_DIM), jnp.bfloat16)

    def tile(index):
        return pl.ds(pl.multiple_of(index * QUERY_TILE, QUERY_TILE), QUERY_TILE)

    def positions(dim, quarter):
        row = lax.broadcasted_iota(jnp.int32, (count, count), dim)
        return (row // PIECE) * TOKENS + row % PIECE + quarter * PIECE

    def per_tile(query_tile, nothing):
        query = query_ref[tile(query_tile), 0:PIECE, :].reshape(count, HEAD_DIM)
        best_ref[...] = jnp.full_like(best_ref, masked_score)
        total_ref[...] = jnp.zeros_like(total_ref)

        def attend(key_tile, masked):
            scores = []
            for which, segment in enumerate(segments):
                key = segment[tile(key_tile), 0:PIECE, :].reshape(count, HEAD_DIM)
                score = dot(query, key, 1, 1)
                if masked:
                    allowed = positions(1, mine ^ which) <= positions(0, mine)
                    score = jnp.where(allowed, score, masked_score)
                scores.append(score)
            top = functools.reduce(jnp.maximum, scores)
            best = best_ref[...]
            best_next = jnp.maximum(best, jnp.max(top, axis=1, keepdims=True))
            best_ref[...] = best_next
            shrink = jnp.exp2((best - best_next) * exponent_scale)
            best_wide = jnp.concatenate([best_next, best_next], axis=1)
            total = total_ref[...] * jnp.concatenate([shrink, shrink], axis=1)
            for score, segment in zip(scores, segments):
                weight = jnp.exp2((score - best_wide) * exponent_scale).astype(jnp.bfloat16)
                value = segment[tile(key_tile), PIECE : 2 * PIECE, :].reshape(count, HEAD_DIM)
                total += dot(weight, jnp.concatenate([value, ones], axis=1), 1, 0)
            total_ref[...] = total

        def unmasked(key_tile, nothing):
            attend(key_tile, False)
            return nothing

        lax.fori_loop(0, query_tile, unmasked, 0)
        attend(query_tile, True)
        outcome = total_ref[:, :HEAD_DIM] / total_ref[:, HEAD_DIM:]
        out_ref[tile(query_tile)] = outcome.astype(jnp.bfloat16).reshape(
            QUERY_TILE, PIECE, HEAD_DIM
        )
        return nothing

    lax.fori_loop(0, BLOCKS // QUERY_TILE, per_tile, 0)


def lightning_kernel(query_ref, key_ref, value_ref, decay_ref, prior_ref, out_ref):
    decay = decay_ref[...]
    causal = lower_triangle()
    running_sum = running_sums(decay)
    later = jnp.where(causal, 0.0, 1.0).astype(jnp.float32)
    shape = (TOKENS, TOKENS)
    upper = lax.broadcasted_iota(jnp.int32, shape, 0) <= lax.broadcasted_iota(jnp.int32, shape, 1)
    upper = jnp.where(upper, 1.0, 0.0).astype(jnp.float32)
    running_row = dot(decay, upper, 0, 0, lax.Precision.HIGHEST)
    for head in range(HEADS_HERE):
        sums = running_sum[:, head : head + 1]
        spread = sums - running_row[head : head + 1, :]
        query = query_ref[:, columns(head)]
        value = value_ref[:, columns(head)]
        scores = dot(query, key_ref[:, columns(head)], 1, 1)
        decayed = jnp.where(causal, jnp.exp(jnp.where(causal, spread, 0.0)), 0.0) * scores
        total = dot(decayed.astype(jnp.bfloat16), value, 1, 0)
        query_scaled = (query.astype(jnp.float32) * jnp.exp(sums)).astype(jnp.bfloat16)
        prior = prior_ref[4 * head : 4 * head + 4].reshape(HEAD_DIM, HEAD_DIM)
        total += dot(query_scaled, prior, 1, 0)
        mean = jnp.mean(total * total, axis=1, keepdims=True)
        out_ref[:, columns(head)] = (total * lax.rsqrt(mean + norm_eps)).astype(jnp.bfloat16)


def unpack_kernel(moved_ref, out_ref):
    for device in range(BLOCKS):
        head, quarter = place_of(device)
        out_ref[rows(quarter), columns(head)] = moved_ref[device]


def exchange(value):
    return lax.all_to_all(value, "ctx", split_axis=0, concat_axis=0, tiled=True)


def swap(value, step):
    return lax.ppermute(value, "ctx", [(d, d ^ step) for d in range(BLOCKS)])


def shards(lin_query, lin_key, lin_value, log_decay, soft_query, soft_key, soft_value):
    half = jnp.bfloat16
    shape = jax.ShapeDtypeStruct
    index = lax.axis_index("ctx")
    quarter = (index // X_STEP % 2 * 2 + index % 2).astype(jnp.int32).reshape(1)

    packed_keys = call(
        pack_keys_kernel, shape((BLOCKS, 2 * PIECE, HEAD_DIM), half), (soft_key, soft_value), 1000
    )
    kv0 = exchange(packed_keys)
    packed_queries = call(
        states_kernel,
        shape((BLOCKS, 2 * PIECE + 8, HEAD_DIM), half),
        (lin_key, lin_value, log_decay, soft_query),
        10**8,
    )
    kv2 = swap(kv0, X_STEP)
    kv1 = swap(kv0, 1)
    queries = exchange(packed_queries)
    kv3 = swap(kv2, 1)
    piece = shape((BLOCKS, PIECE, HEAD_DIM), half)
    prior = exchange(call(scan_kernel, piece, (queries,), 10**6))
    count = QUERY_TILE * PIECE
    attended = call(
        attention_kernel,
        piece,
        (quarter, queries, kv0, kv1, kv2, kv3),
        10**10,
        (
            pltpu.VMEM((count, HEAD_DIM), jnp.float32),
            pltpu.VMEM((count, 2 * HEAD_DIM), jnp.float32),
        ),
        smem=1,
    )
    returned = exchange(attended)
    whole_out = shape((TOKENS, HEADS_HERE * HEAD_DIM), half)
    lin_out = call(
        lightning_kernel, whole_out, (lin_query, lin_key, lin_value, log_decay, prior), 2 * 10**8
    )
    soft_out = call(unpack_kernel, whole_out, (returned,), 1000)
    return (lin_out, soft_out)


def solution(mesh):
    spec = P("ctx", "head")
    return jax.shard_map(
        shards, mesh=mesh, in_specs=(spec,) * 7, out_specs=(spec, spec), check_vma=False
    )
```

```python
import functools
import math

import jax
import jax.numpy as jnp
import numpy as np
from jax import lax
from jax.experimental import pallas as pl
from jax.experimental.pallas import tpu as pltpu
from jax.sharding import PartitionSpec as P

HEAD_DIM = 128
TOKENS = 128
HEADS_HERE = 16
BLOCKS = 64
PIECE = 32

norm_eps = 1e-06
masked_score = -1e30
exponent_scale = HEAD_DIM ** (-0.5) * math.log2(math.e)
X_STEP = 16
QUERY_TILE = 16


def place_of(device):
    x, z, core = device // 16, device // 2 % 8, device % 2
    return 2 * z + x // 2, 2 * (x % 2) + core


def columns(head):
    return slice(head * HEAD_DIM, (head + 1) * HEAD_DIM)


def rows(quarter):
    return slice(quarter * PIECE, (quarter + 1) * PIECE)


def whole():
    return pl.BlockSpec(memory_space=pltpu.VMEM)


def dot(left, right, left_dim, right_dim, precision=None):
    return lax.dot_general(
        left,
        right,
        (((left_dim,), (right_dim,)), ((), ())),
        precision=precision,
        preferred_element_type=jnp.float32,
    )


def call(kernel, out_shape, operands, flops, scratch=(), smem=0, limit=16):
    moved = [*operands, *jax.tree.leaves(out_shape)]
    return pl.pallas_call(
        kernel,
        out_shape=out_shape,
        in_specs=[pl.BlockSpec(memory_space=pltpu.SMEM)] * smem
        + [whole() for _ in operands[smem:]],
        out_specs=jax.tree.map(lambda _: whole(), out_shape),
        scratch_shapes=list(scratch),
        compiler_params=pltpu.CompilerParams(vmem_limit_bytes=limit << 20),
        cost_estimate=pl.CostEstimate(
            flops=flops,
            bytes_accessed=sum(math.prod(o.shape) * o.dtype.itemsize for o in moved),
            transcendentals=0,
        ),
    )(*operands)


def pack_kernel(query_ref, key_ref, value_ref, out_ref):
    for device in range(BLOCKS):
        head, quarter = place_of(device)
        for which, source in enumerate((query_ref, key_ref, value_ref)):
            out_ref[device, rows(which), :] = source[rows(quarter), columns(head)]


def lower_triangle():
    shape = (TOKENS, TOKENS)
    return lax.broadcasted_iota(jnp.int32, shape, 0) >= lax.broadcasted_iota(jnp.int32, shape, 1)


def running_sums(decay):
    ones = jnp.where(lower_triangle(), 1.0, 0.0).astype(jnp.float32)
    return dot(ones, decay, 1, 0, lax.Precision.HIGHEST)


def states_kernel(key_ref, value_ref, decay_ref, out_ref):
    running_sum = running_sums(decay_ref[...])
    part = lax.broadcasted_iota(jnp.int32, (8, HEAD_DIM), 0)
    for head in range(HEADS_HERE):
        sums = running_sum[:, head : head + 1]
        ending = running_sum[TOKENS - 1 : TOKENS, head : head + 1]
        key_wide = key_ref[:, columns(head)].astype(jnp.float32)
        key_scaled = (key_wide * jnp.exp(ending - sums)).astype(jnp.bfloat16)
        state = dot(key_scaled, value_ref[:, columns(head)], 0, 0).astype(jnp.bfloat16)
        coarse = ending.astype(jnp.bfloat16).astype(jnp.float32)
        middle = (ending - coarse).astype(jnp.bfloat16).astype(jnp.float32)
        fine = ending - coarse - middle
        parts = jnp.where(part == 0, coarse, jnp.where(part == 1, middle, fine))
        parts = parts.astype(jnp.bfloat16)
        for quarter in range(4):
            out_ref[4 * head + quarter, 0:PIECE, :] = state[rows(quarter), :]
            out_ref[4 * head + quarter, PIECE:, :] = parts


def scan_kernel(moved_ref, out_ref):
    def step(block, carry):
        out_ref[block] = carry.astype(jnp.bfloat16)
        parts = moved_ref[block, PIECE:, :].astype(jnp.float32)
        ending = parts[0:1] + parts[1:2] + parts[2:3]
        state = moved_ref[block, 0:PIECE, :].astype(jnp.float32)
        return jnp.exp(ending) * carry + state

    lax.fori_loop(0, BLOCKS, step, jnp.zeros((PIECE, HEAD_DIM), jnp.float32), unroll=4)


def attention_kernel(
    which, first, last_tile, has_state, finishes, quarter_ref, query_ref, *refs
):
    count = QUERY_TILE * PIECE
    number = len(which)
    segments, refs = refs[:number], refs[number:]
    if has_state:
        (best_in, total_in), refs = refs[:2], refs[3:]
    results, (best_ref, total_ref, score_ref, bias_ref) = refs[:-4], refs[-4:]
    mine = quarter_ref[0]
    ones = jnp.ones((count, HEAD_DIM), jnp.bfloat16)
    lanes = count // HEAD_DIM

    def tile(index):
        return pl.ds(pl.multiple_of(index * QUERY_TILE, QUERY_TILE), QUERY_TILE)

    def tile_rows(index):
        return pl.ds(pl.multiple_of(index * count, count), count)

    def positions(shape, dim, quarter):
        row = lax.broadcasted_iota(jnp.int32, shape, dim)
        return (row // PIECE) * TOKENS + row % PIECE + quarter * PIECE

    def widen(value):
        return jnp.concatenate([value] * lanes, axis=1)

    query_places = widen(positions((count, HEAD_DIM), 0, mine))
    for slot, step in enumerate(which):
        allowed = positions((1, count), 1, mine ^ step) <= query_places
        bias_ref[slot] = jnp.where(allowed, 0.0, masked_score)

    def per_tile(query_tile, carry):
        query = query_ref[tile(query_tile), rows(0), :].reshape(count, HEAD_DIM)
        if has_state:
            best_ref[...] = best_in[tile_rows(query_tile), :]
        else:
            best_ref[...] = jnp.full_like(best_ref, masked_score)

        def find_best(key_tile, masked):
            best = best_ref[...]
            for slot, segment in enumerate(segments):
                key = segment[tile(key_tile), rows(segment.shape[1] // PIECE - 2), :].reshape(count, HEAD_DIM)
                score = dot(query, key, 1, 1)
                if masked:
                    score += bias_ref[slot]
                score_ref[number * (key_tile - first) + slot] = score
                for lane in range(lanes):
                    best = jnp.maximum(best, score[:, columns(lane)])
            best_ref[...] = best

        def unmasked(key_tile, nothing):
            find_best(key_tile, False)
            return nothing

        lax.fori_loop(first, jnp.minimum(query_tile, last_tile), unmasked, 0)

        @pl.when(jnp.logical_and(query_tile >= first, query_tile < last_tile))
        def _():
            find_best(query_tile, True)

        best = jnp.broadcast_to(jnp.max(best_ref[...], axis=1, keepdims=True), best_ref.shape)
        best_ref[...] = best
        if has_state:
            shrink = jnp.exp2((best_in[tile_rows(query_tile), :] - best) * exponent_scale)
            total_ref[...] = total_in[tile_rows(query_tile), :] * jnp.concatenate(
                [shrink, shrink], axis=1
            )
        else:
            total_ref[...] = jnp.zeros_like(total_ref)

        def add_up(key_tile, nothing):
            best_wide = widen(best_ref[...])
            weights, values = [], []
            for slot, segment in enumerate(segments):
                score = score_ref[number * (key_tile - first) + slot]
                weight = jnp.exp2((score - best_wide) * exponent_scale)
                weights.append(weight.astype(jnp.bfloat16))
                value = segment[tile(key_tile), rows(segment.shape[1] // PIECE - 1), :].reshape(count, HEAD_DIM)
                values.append(jnp.concatenate([value, ones], axis=1))
            total_ref[...] += dot(
                jnp.concatenate(weights, axis=1), jnp.concatenate(values, axis=0), 1, 0
            )
            return nothing

        lax.fori_loop(first, jnp.minimum(query_tile + 1, last_tile), add_up, 0)
        if finishes:
            outcome = total_ref[:, :HEAD_DIM] / total_ref[:, HEAD_DIM:]
            results[0][tile(query_tile)] = outcome.astype(jnp.bfloat16).reshape(
                QUERY_TILE, PIECE, HEAD_DIM
            )
        else:
            results[0][tile_rows(query_tile), :] = best_ref[...]
            results[1][tile_rows(query_tile), :] = total_ref[...]
        return carry

    lax.fori_loop(0, BLOCKS // QUERY_TILE, per_tile, 0)


def attend(which, key_tiles, quarter, queries, segments, state, finishes, token=()):
    shape = jax.ShapeDtypeStruct
    count = QUERY_TILE * PIECE
    first, last_tile = key_tiles
    kernel = functools.partial(
        attention_kernel, which, first, last_tile, state is not None, finishes
    )
    if finishes:
        out_shape = shape((BLOCKS, PIECE, HEAD_DIM), jnp.bfloat16)
    else:
        out_shape = (
            shape((BLOCKS * PIECE, HEAD_DIM), jnp.float32),
            shape((BLOCKS * PIECE, 2 * HEAD_DIM), jnp.float32),
        )
    return call(
        kernel,
        out_shape,
        (quarter, queries, *segments, *(state or ()), *token),
        3 * 10**9 * len(which),
        (
            pltpu.VMEM((count, HEAD_DIM), jnp.float32),
            pltpu.VMEM((count, 2 * HEAD_DIM), jnp.float32),
            pltpu.VMEM((len(which) * (last_tile - first), count, count), jnp.float32),
            pltpu.VMEM((len(which), count, count), jnp.float32),
        ),
        smem=1,
        limit=24,
    )


def lightning_kernel(query_ref, key_ref, value_ref, decay_ref, prior_ref, out_ref):
    decay = decay_ref[...]
    causal = lower_triangle()
    running_sum = running_sums(decay)
    later = jnp.where(causal, 0.0, 1.0).astype(jnp.float32)
    shape = (TOKENS, TOKENS)
    upper = lax.broadcasted_iota(jnp.int32, shape, 0) <= lax.broadcasted_iota(jnp.int32, shape, 1)
    upper = jnp.where(upper, 1.0, 0.0).astype(jnp.float32)
    running_row = dot(decay, upper, 0, 0, lax.Precision.HIGHEST)
    for head in range(HEADS_HERE):
        sums = running_sum[:, head : head + 1]
        spread = sums - running_row[head : head + 1, :]
        query = query_ref[:, columns(head)]
        value = value_ref[:, columns(head)]
        scores = dot(query, key_ref[:, columns(head)], 1, 1)
        decayed = jnp.where(causal, jnp.exp(jnp.where(causal, spread, 0.0)), 0.0) * scores
        total = dot(decayed.astype(jnp.bfloat16), value, 1, 0)
        query_scaled = (query.astype(jnp.float32) * jnp.exp(sums)).astype(jnp.bfloat16)
        prior = prior_ref[4 * head : 4 * head + 4].reshape(HEAD_DIM, HEAD_DIM)
        total += dot(query_scaled, prior, 1, 0)
        mean = jnp.mean(total * total, axis=1, keepdims=True)
        out_ref[:, columns(head)] = (total * lax.rsqrt(mean + norm_eps)).astype(jnp.bfloat16)


def unpack_kernel(moved_ref, out_ref):
    for device in range(BLOCKS):
        head, quarter = place_of(device)
        out_ref[rows(quarter), columns(head)] = moved_ref[device]


def exchange(value):
    return lax.all_to_all(value, "ctx", split_axis=0, concat_axis=0, tiled=True)


def swap(value, step):
    return lax.ppermute(value, "ctx", [(d, d ^ step) for d in range(BLOCKS)])


def shards(lin_query, lin_key, lin_value, log_decay, soft_query, soft_key, soft_value):
    half = jnp.bfloat16
    shape = jax.ShapeDtypeStruct
    index = lax.axis_index("ctx")
    quarter = (index // X_STEP % 2 * 2 + index % 2).astype(jnp.int32).reshape(1)

    kv0 = exchange(
        call(
            pack_kernel,
            shape((BLOCKS, 3 * PIECE, HEAD_DIM), half),
            (soft_query, soft_key, soft_value),
            1000,
        )
    )
    states = call(
        states_kernel,
        shape((BLOCKS, PIECE + 8, HEAD_DIM), half),
        (lin_key, lin_value, log_decay),
        10**8,
    )
    kv0, states = lax.optimization_barrier((kv0, states))
    kv2 = swap(kv0[:, PIECE:], X_STEP)
    kv1 = swap(kv0[:, PIECE:], 1)
    moved_states = exchange(states)
    piece = shape((BLOCKS, PIECE, HEAD_DIM), half)
    tiles = (0, BLOCKS // QUERY_TILE)
    state = attend((0, 1), tiles, quarter, kv0, (kv0, kv1), None, False)
    token, kv2, moved_states = lax.optimization_barrier((state[0][0:8, :], kv2, moved_states))
    kv3 = swap(kv2, 1)
    prior = exchange(call(scan_kernel, piece, (moved_states,), 10**6))
    attended = attend((2, 3), tiles, quarter, kv0, (kv2, kv3), state, True, (token,))
    returned = exchange(attended)
    whole_out = shape((TOKENS, HEADS_HERE * HEAD_DIM), half)
    lin_out = call(
        lightning_kernel, whole_out, (lin_query, lin_key, lin_value, log_decay, prior), 2 * 10**8
    )
    soft_out = call(unpack_kernel, whole_out, (returned,), 1000)
    return (lin_out, soft_out)


def solution(mesh):
    spec = P("ctx", "head")
    return jax.shard_map(
        shards, mesh=mesh, in_specs=(spec,) * 7, out_specs=(spec, spec), check_vma=False
    )
```

```python
import functools
import math

import jax
import jax.numpy as jnp
import numpy as np
from jax import lax
from jax.experimental import pallas as pl
from jax.experimental.pallas import tpu as pltpu
from jax.sharding import PartitionSpec as P

HEAD_DIM = 128
TOKENS = 128
HEADS_HERE = 16
BLOCKS = 64
PIECE = 32

norm_eps = 1e-06
masked_score = -1e30
exponent_scale = HEAD_DIM ** (-0.5) * math.log2(math.e)
X_STEP = 16
X_CHIPS, Z_CHIPS = 4, 8
HALF = HEADS_HERE // 2
QUARTER, X, Z, CORE = range(4)
QUERY_TILE = 16


def place_of(device):
    x, z, core = device // 16, device // 2 % 8, device % 2
    return 2 * z + x // 2, 2 * (x % 2) + core


def columns(head):
    return slice(head * HEAD_DIM, (head + 1) * HEAD_DIM)


def rows(quarter):
    return slice(quarter * PIECE, (quarter + 1) * PIECE)


def whole(space=pltpu.VMEM):
    return pl.BlockSpec(memory_space=space)


def dot(left, right, left_dim, right_dim, precision=None):
    return lax.dot_general(
        left,
        right,
        (((left_dim,), (right_dim,)), ((), ())),
        precision=precision,
        preferred_element_type=jnp.float32,
    )


def call(kernel, out_shape, operands, flops, spaces=None, out_space=pltpu.VMEM, scratch=(), limit=16):
    moved = [*operands, *jax.tree.leaves(out_shape)]
    spaces = spaces or [pltpu.VMEM] * len(operands)
    operands = [
        pltpu.with_memory_space_constraint(o, space) if space is pltpu.HBM else o
        for o, space in zip(operands, spaces)
    ]
    if out_space is pltpu.HBM:
        out_shape = jax.tree.map(lambda o: pltpu.HBM(o.shape, o.dtype), out_shape)
    return pl.pallas_call(
        kernel,
        out_shape=out_shape,
        in_specs=[whole(space) for space in spaces],
        out_specs=jax.tree.map(lambda _: whole(out_space), out_shape),
        scratch_shapes=list(scratch),
        compiler_params=pltpu.CompilerParams(vmem_limit_bytes=limit << 20),
        cost_estimate=pl.CostEstimate(
            flops=flops,
            bytes_accessed=sum(math.prod(o.shape) * o.dtype.itemsize for o in moved),
            transcendentals=0,
        ),
    )(*operands)


def pack_kernel(query_ref, key_ref, value_ref, out_ref, held_ref, semaphores):
    sources = (query_ref, key_ref, value_ref)
    copies = [
        pltpu.make_async_copy(source, held_ref.at[which], semaphores.at[which])
        for which, source in enumerate(sources)
    ]
    for copy in copies:
        copy.start()
    for which, copy in enumerate(copies):
        copy.wait()
        for device in range(BLOCKS):
            head, quarter = place_of(device)
            out_ref[device, rows(which), :] = held_ref[which, rows(quarter), columns(head)]


def lower_triangle():
    shape = (TOKENS, TOKENS)
    return lax.broadcasted_iota(jnp.int32, shape, 0) >= lax.broadcasted_iota(jnp.int32, shape, 1)


def running_sums(decay):
    ones = jnp.where(lower_triangle(), 1.0, 0.0).astype(jnp.float32)
    return dot(ones, decay, 1, 0, lax.Precision.HIGHEST)


def split_parts(value):
    coarse = value.astype(jnp.bfloat16).astype(jnp.float32)
    middle = (value - coarse).astype(jnp.bfloat16).astype(jnp.float32)
    parts = (coarse, middle, value - coarse - middle)
    return jnp.concatenate([part.astype(jnp.bfloat16) for part in parts], axis=0)


def join_parts(parts, heads):
    wide = parts.astype(jnp.float32)
    return wide[0:heads] + wide[heads : 2 * heads] + wide[2 * heads : 3 * heads]


def head_rows(head):
    return slice(head * HEAD_DIM, (head + 1) * HEAD_DIM)


def states_kernel(key_ref, value_ref, decay_ref, out_ref):
    decay = decay_ref[...]
    running_sum = running_sums(decay)
    ones = jnp.ones((TOKENS, HEAD_DIM), jnp.float32)
    endings = dot(decay, ones, 0, 0, lax.Precision.HIGHEST)
    out_ref[HEADS_HERE * HEAD_DIM :, :] = split_parts(endings)
    for head in range(HEADS_HERE):
        sums = running_sum[:, head : head + 1]
        ending = running_sum[TOKENS - 1 : TOKENS, head : head + 1]
        key_wide = key_ref[:, columns(head)].astype(jnp.float32)
        key_scaled = (key_wide * jnp.exp(ending - sums)).astype(jnp.bfloat16)
        state = dot(key_scaled, value_ref[:, columns(head)], 0, 0)
        out_ref[head_rows(head), :] = state.astype(jnp.bfloat16)


def chip_kernel(place_ref, mine_ref, other_ref, out_ref, ending_ref):
    first = place_ref[CORE] == 0
    tail = slice(HEADS_HERE * HEAD_DIM, None)
    mine = join_parts(mine_ref[tail, :], HEADS_HERE)
    other = join_parts(other_ref[tail, :], HEADS_HERE)
    both = mine + other
    later = jnp.where(first, other, mine)
    ending_ref[...] = jnp.where(first, both[0:HALF], both[HALF:])
    out_ref[HALF * HEAD_DIM :, :] = split_parts(ending_ref[...])
    ending_ref[...] = jnp.where(first, later[0:HALF], later[HALF:])
    for head in range(HALF):
        place = place_ref[CORE] * (HALF * HEAD_DIM) + head * HEAD_DIM
        here = pl.ds(pl.multiple_of(place, HEAD_DIM), HEAD_DIM)
        mine = mine_ref[here, :].astype(jnp.float32)
        other = other_ref[here, :].astype(jnp.float32)
        fade = jnp.exp(ending_ref[head : head + 1, :])
        state = jnp.where(first, fade * mine + other, fade * other + mine)
        out_ref[head_rows(head), :] = state.astype(jnp.bfloat16)


def plane_kernel(place_ref, gathered_ref, plane_ref, before_ref, faded_ref):
    mine = place_ref[Z]
    endings = [join_parts(gathered_ref[z, HALF * HEAD_DIM :, :], HALF) for z in range(Z_CHIPS)]
    faded = jnp.zeros((HALF, HEAD_DIM), jnp.float32)
    for z in range(Z_CHIPS):
        faded += jnp.where(z < mine, endings[z], 0.0)
    faded_ref[...] = faded
    plane_ref[HALF * HEAD_DIM :, :] = split_parts(functools.reduce(jnp.add, endings))
    for head in range(HALF):
        carry = jnp.zeros((HEAD_DIM, HEAD_DIM), jnp.float32)
        before = carry
        for z in range(Z_CHIPS):
            before = jnp.where(z == mine, carry, before)
            fade = jnp.exp(endings[z][head : head + 1, :])
            carry = fade * carry + gathered_ref[z, head_rows(head), :].astype(jnp.float32)
        before_ref[head_rows(head), :] = before
        plane_ref[head_rows(head), :] = carry.astype(jnp.bfloat16)


def prior_kernel(place_ref, planes_ref, before_ref, faded_ref, out_ref):
    mine = place_ref[X]
    endings = [join_parts(planes_ref[x, HALF * HEAD_DIM :, :], HALF) for x in range(X_CHIPS)]
    for head in range(HALF):
        carry = jnp.zeros((HEAD_DIM, HEAD_DIM), jnp.float32)
        before = carry
        for x in range(X_CHIPS):
            before = jnp.where(x == mine, carry, before)
            fade = jnp.exp(endings[x][head : head + 1, :])
            carry = fade * carry + planes_ref[x, head_rows(head), :].astype(jnp.float32)
        fade = jnp.exp(faded_ref[head : head + 1, :])
        prior = fade * before + before_ref[head_rows(head), :]
        out_ref[head_rows(head), :] = prior.astype(jnp.bfloat16)


def attention_kernel(
    which, first, last_tile, has_state, finishes, place_ref, query_ref, *refs
):
    count = QUERY_TILE * PIECE
    tiles = BLOCKS // QUERY_TILE
    number = len(which)
    segments, refs = refs[:number], refs[number:]
    if has_state:
        state_in, refs = refs[:2], refs[2 + 1 :]
    results, (best_all, total_all, score_ref, bias_ref, semaphores) = refs[:-5], refs[-5:]
    held = (best_all, total_all)
    mine = place_ref[QUARTER]
    ones = jnp.ones((count, HEAD_DIM), jnp.bfloat16)
    lanes = count // HEAD_DIM

    def tile(index):
        return pl.ds(pl.multiple_of(index * QUERY_TILE, QUERY_TILE), QUERY_TILE)

    def tile_rows(index):
        return pl.ds(pl.multiple_of(index * count, count), count)

    def copy_in(which_array, index):
        here = (tile_rows(index), slice(None))
        return pltpu.make_async_copy(
            state_in[which_array].at[here],
            held[which_array].at[here],
            semaphores.at[0, which_array, index],
        )

    def copy_out(which_array, index):
        here = (tile_rows(index), slice(None))
        return pltpu.make_async_copy(
            held[which_array].at[here],
            results[which_array].at[here],
            semaphores.at[1, which_array, index],
        )

    if has_state:
        for index in range(tiles):
            copy_in(0, index).start()
            copy_in(1, index).start()

    def positions(shape, dim, quarter):
        row = lax.broadcasted_iota(jnp.int32, shape, dim)
        return (row // PIECE) * TOKENS + row % PIECE + quarter * PIECE

    def widen(value):
        return jnp.concatenate([value] * lanes, axis=1)

    query_places = widen(positions((count, HEAD_DIM), 0, mine))
    for slot, step in enumerate(which):
        allowed = positions((1, count), 1, mine ^ step) <= query_places
        bias_ref[slot] = jnp.where(allowed, 0.0, masked_score)

    def per_tile(query_tile, carry):
        best_ref = best_all.at[tile_rows(query_tile)]
        total_ref = total_all.at[tile_rows(query_tile)]
        query = query_ref[tile(query_tile), rows(0), :].reshape(count, HEAD_DIM)
        if has_state:
            copy_in(0, query_tile).wait()
            copy_in(1, query_tile).wait()
            best_before = best_ref[...]
        else:
            best_ref[...] = jnp.full((count, HEAD_DIM), masked_score, jnp.float32)

        def find_best(key_tile, masked):
            best = best_ref[...]
            for slot, segment in enumerate(segments):
                key = segment[tile(key_tile - first), rows(segment.shape[1] // PIECE - 2), :]
                score = dot(query, key.reshape(count, HEAD_DIM), 1, 1)
                if masked:
                    score += bias_ref[slot]
                score_ref[number * (key_tile - first) + slot] = score
                for lane in range(lanes):
                    best = jnp.maximum(best, score[:, columns(lane)])
            best_ref[...] = best

        def unmasked(key_tile, nothing):
            find_best(key_tile, False)
            return nothing

        lax.fori_loop(first, jnp.minimum(query_tile, last_tile), unmasked, 0)
        if first == 0 and last_tile == tiles:
            find_best(query_tile, True)
        else:

            @pl.when(jnp.logical_and(query_tile >= first, query_tile < last_tile))
            def _():
                find_best(query_tile, True)

        best = jnp.broadcast_to(
            jnp.max(best_ref[...], axis=1, keepdims=True), (count, HEAD_DIM)
        )
        best_ref[...] = best
        if has_state:
            shrink = jnp.exp2((best_before - best) * exponent_scale)
            total_ref[...] *= jnp.concatenate([shrink, shrink], axis=1)
        else:
            total_ref[...] = jnp.zeros((count, 2 * HEAD_DIM), jnp.float32)

        def add_up(key_tile, nothing):
            best_wide = widen(best_ref[...])
            weights, values = [], []
            for slot, segment in enumerate(segments):
                score = score_ref[number * (key_tile - first) + slot]
                weight = jnp.exp2((score - best_wide) * exponent_scale)
                weights.append(weight.astype(jnp.bfloat16))
                value = segment[tile(key_tile - first), rows(segment.shape[1] // PIECE - 1), :]
                values.append(jnp.concatenate([value.reshape(count, HEAD_DIM), ones], axis=1))
            total_ref[...] += dot(
                jnp.concatenate(weights, axis=1), jnp.concatenate(values, axis=0), 1, 0
            )
            return nothing

        lax.fori_loop(first, jnp.minimum(query_tile + 1, last_tile), add_up, 0)
        if finishes:
            outcome = total_ref[:, :HEAD_DIM] / total_ref[:, HEAD_DIM:]
            results[0][tile(query_tile)] = outcome.astype(jnp.bfloat16).reshape(
                QUERY_TILE, PIECE, HEAD_DIM
            )
        else:
            copy_out(0, query_tile).start()
            copy_out(1, query_tile).start()
        return carry

    lax.fori_loop(0, tiles, per_tile, 0)
    if not finishes:
        for index in range(tiles):
            copy_out(0, index).wait()
            copy_out(1, index).wait()


def attend(which, key_tiles, place, queries, segments, state, finishes, token=()):
    shape = jax.ShapeDtypeStruct
    count = QUERY_TILE * PIECE
    tiles = BLOCKS // QUERY_TILE
    first, last_tile = key_tiles
    kernel = functools.partial(
        attention_kernel, which, first, last_tile, state is not None, finishes
    )
    best_shape = (BLOCKS * PIECE, HEAD_DIM)
    total_shape = (BLOCKS * PIECE, 2 * HEAD_DIM)
    if finishes:
        out_shape = shape((BLOCKS, PIECE, HEAD_DIM), jnp.bfloat16)
    else:
        out_shape = (shape(best_shape, jnp.float32), shape(total_shape, jnp.float32))
    spaces = [pltpu.SMEM, *[pltpu.VMEM] * (1 + len(segments))]
    if state is not None:
        spaces += [pltpu.HBM, pltpu.HBM, pltpu.VMEM]
    return call(
        kernel,
        out_shape,
        (place, queries, *segments, *(state or ()), *token),
        10**9 * len(which) * (last_tile - first),
        spaces,
        pltpu.VMEM if finishes else pltpu.HBM,
        (
            pltpu.VMEM(best_shape, jnp.float32),
            pltpu.VMEM(total_shape, jnp.float32),
            pltpu.VMEM((len(which) * (last_tile - first), count, count), jnp.float32),
            pltpu.VMEM((len(which), count, count), jnp.float32),
            pltpu.SemaphoreType.DMA((2, 2, tiles)),
        ),
        limit=24,
    )


def lightning_kernel(
    place_ref, query_ref, key_ref, value_ref, decay_ref, mine_ref, other_ref, sibling_ref, out_ref
):
    second = place_ref[CORE] == 1
    endings = join_parts(sibling_ref[HEADS_HERE * HEAD_DIM :, :], HEADS_HERE)
    decay = decay_ref[...]
    causal = lower_triangle()
    running_sum = running_sums(decay)
    later = jnp.where(causal, 0.0, 1.0).astype(jnp.float32)
    shape = (TOKENS, TOKENS)
    upper = lax.broadcasted_iota(jnp.int32, shape, 0) <= lax.broadcasted_iota(jnp.int32, shape, 1)
    upper = jnp.where(upper, 1.0, 0.0).astype(jnp.float32)
    running_row = dot(decay, upper, 0, 0, lax.Precision.HIGHEST)
    for head in range(HEADS_HERE):
        sums = running_sum[:, head : head + 1]
        spread = sums - running_row[head : head + 1, :]
        query = query_ref[:, columns(head)]
        value = value_ref[:, columns(head)]
        scores = dot(query, key_ref[:, columns(head)], 1, 1)
        decayed = jnp.where(causal, jnp.exp(jnp.where(causal, spread, 0.0)), 0.0) * scores
        total = dot(decayed.astype(jnp.bfloat16), value, 1, 0)
        query_scaled = (query.astype(jnp.float32) * jnp.exp(sums)).astype(jnp.bfloat16)
        half, place = head // HALF, head_rows(head % HALF)
        mine = mine_ref[place, :].astype(jnp.float32)
        other = other_ref[place, :].astype(jnp.float32)
        prior = jnp.where(place_ref[CORE] == half, mine, other)
        fade = jnp.exp(endings[head : head + 1, :])
        passed = fade * prior + sibling_ref[head_rows(head), :].astype(jnp.float32)
        prior = jnp.where(second, passed, prior)
        total += dot(query_scaled, prior.astype(jnp.bfloat16), 1, 0)
        mean = jnp.mean(total * total, axis=1, keepdims=True)
        out_ref[:, columns(head)] = (total * lax.rsqrt(mean + norm_eps)).astype(jnp.bfloat16)


def unpack_kernel(moved_ref, order_ref, out_ref):
    for device in range(BLOCKS):
        head, quarter = place_of(device)
        out_ref[rows(quarter), columns(head)] = moved_ref[device]


def exchange(value):
    return lax.all_to_all(value, "ctx", split_axis=0, concat_axis=0, tiled=True)


def swap(value, step):
    return lax.ppermute(value, "ctx", [(d, d ^ step) for d in range(BLOCKS)])


def gather(value, groups):
    return lax.all_gather(value, "ctx", axis=0, axis_index_groups=groups)


def shards(lin_query, lin_key, lin_value, log_decay, soft_query, soft_key, soft_value):
    half = jnp.bfloat16
    shape = jax.ShapeDtypeStruct
    index = lax.axis_index("ctx").astype(jnp.int32)
    x, z, core = index // X_STEP, index // 2 % Z_CHIPS, index % 2
    place = jnp.stack([2 * (x % 2) + core, x, z, core])
    everyone = np.arange(BLOCKS).reshape(X_CHIPS, Z_CHIPS, 2)
    along_z = everyone.transpose(0, 2, 1).reshape(-1, Z_CHIPS).tolist()
    along_x = everyone.transpose(1, 2, 0).reshape(-1, X_CHIPS).tolist()

    width = HEADS_HERE * HEAD_DIM
    packed = call(
        pack_kernel,
        shape((BLOCKS, 3 * PIECE, HEAD_DIM), half),
        (soft_query, soft_key, soft_value),
        1000,
        [pltpu.HBM] * 3,
        scratch=(pltpu.VMEM((3, TOKENS, width), half), pltpu.SemaphoreType.DMA((3,))),
    )
    kv0 = exchange(packed)
    states = call(
        states_kernel,
        shape((width + 3 * HEADS_HERE, HEAD_DIM), half),
        (lin_key, lin_value, log_decay),
        10**8,
    )
    sibling = swap(states, 1)
    on_core = [pltpu.SMEM] + [pltpu.VMEM] * 8
    part = shape((HALF * HEAD_DIM + 3 * HALF, HEAD_DIM), half)
    chip = call(
        chip_kernel,
        part,
        (place, states, sibling),
        10**7,
        on_core[:3],
        scratch=(pltpu.VMEM((HALF, HEAD_DIM), jnp.float32),),
    )
    kv0, chip = lax.optimization_barrier((kv0, chip))
    early = BLOCKS // 2
    kv2a = swap(kv0[:early, PIECE:], X_STEP)
    kv2b = swap(kv0[early:, PIECE:], X_STEP)
    kv1 = swap(kv0[:, PIECE:], 1)
    chips = gather(chip, along_z)

    tiles = BLOCKS // QUERY_TILE
    state = attend((0, 1), (0, tiles), place, kv0, (kv0, kv1), None, False)
    token, kv2a = lax.optimization_barrier((state[0][0:8, :], kv2a))
    kv3a = swap(kv2a, 1)
    state = attend((2, 3), (0, tiles // 2), place, kv0, (kv2a, kv3a), state, False, (token,))
    token, kv2b, chips = lax.optimization_barrier((state[0][0:8, :], kv2b, chips))
    kv3b = swap(kv2b, 1)
    wide = shape((HALF * HEAD_DIM, HEAD_DIM), jnp.float32)
    plane, before, faded = call(
        plane_kernel,
        (part, wide, shape((HALF, HEAD_DIM), jnp.float32)),
        (place, chips),
        10**7,
        on_core[:2],
    )
    planes = gather(plane, along_x)
    attended = attend((2, 3), (tiles // 2, tiles), place, kv0, (kv2b, kv3b), state, True, (token,))
    returned = exchange(attended)
    prior = call(
        prior_kernel,
        shape((HALF * HEAD_DIM, HEAD_DIM), half),
        (place, planes, before, faded),
        10**7,
        on_core[:4],
    )
    other_prior = swap(prior, 1)
    whole_out = shape((TOKENS, width), half)
    lin_out = call(
        lightning_kernel,
        whole_out,
        (place, lin_query, lin_key, lin_value, log_decay, prior, other_prior, sibling),
        2 * 10**8,
        on_core[:8],
    )
    token, returned = lax.optimization_barrier((lin_out[0:8, 0:HEAD_DIM], returned))
    soft_out = call(unpack_kernel, whole_out, (returned, token), 1000)
    return (lin_out, soft_out)


def solution(mesh):
    spec = P("ctx", "head")
    return jax.shard_map(
        shards, mesh=mesh, in_specs=(spec,) * 7, out_specs=(spec, spec), check_vma=False
    )
```

```python
import functools
import math

import jax
import jax.numpy as jnp
from jax import lax
from jax.experimental import pallas as pl
from jax.experimental.pallas import tpu as pltpu
from jax.sharding import PartitionSpec as P

HEAD_DIM = 128
TOKENS = 128
HEADS_HERE = 16
BLOCKS = 64
PIECE = 32

norm_eps = 1e-06
masked_score = -1e30
exponent_scale = HEAD_DIM ** (-0.5) * math.log2(math.e)
X_STEP = 16
HALF = HEADS_HERE // 2
SLICE = HALF * HEAD_DIM // BLOCKS
QUARTER, CORE = range(2)
QUERY_TILE = 8


def place_of(device):
    x, z, core = device // 16, device // 2 % 8, device % 2
    return 2 * z + x // 2, 2 * (x % 2) + core


def columns(head):
    return slice(head * HEAD_DIM, (head + 1) * HEAD_DIM)


def rows(quarter):
    return slice(quarter * PIECE, (quarter + 1) * PIECE)


def whole(space=pltpu.VMEM):
    return pl.BlockSpec(memory_space=space)


def dot(left, right, left_dim, right_dim, precision=None):
    return lax.dot_general(
        left,
        right,
        (((left_dim,), (right_dim,)), ((), ())),
        precision=precision,
        preferred_element_type=jnp.float32,
    )


def call(kernel, out_shape, operands, flops, spaces=None, out_spaces=None, scratch=(), limit=16):
    out_shape = tuple(out_shape)
    bytes_moved = sum(math.prod(o.shape) * o.dtype.itemsize for o in (*operands, *out_shape))
    spaces = spaces or [pltpu.VMEM] * len(operands)
    out_spaces = out_spaces or [pltpu.VMEM] * len(out_shape)
    operands = [
        pltpu.with_memory_space_constraint(o, space) if space is pltpu.HBM else o
        for o, space in zip(operands, spaces)
    ]
    out_shape = [
        pltpu.HBM(o.shape, o.dtype) if space is pltpu.HBM else o
        for o, space in zip(out_shape, out_spaces)
    ]
    return pl.pallas_call(
        kernel,
        out_shape=out_shape,
        in_specs=[whole(space) for space in spaces],
        out_specs=[whole(space) for space in out_spaces],
        scratch_shapes=list(scratch),
        compiler_params=pltpu.CompilerParams(vmem_limit_bytes=limit << 20),
        cost_estimate=pl.CostEstimate(
            flops=flops, bytes_accessed=bytes_moved, transcendentals=0
        ),
    )(*operands)


def pack_kernel(query_ref, key_ref, value_ref, out_ref, held_ref, semaphores):
    sources = (query_ref, key_ref, value_ref)
    copies = [
        pltpu.make_async_copy(source, held_ref.at[which], semaphores.at[which])
        for which, source in enumerate(sources)
    ]
    for copy in copies:
        copy.start()
    for which, copy in enumerate(copies):
        copy.wait()
        for device in range(BLOCKS):
            head, quarter = place_of(device)
            out_ref[device, rows(which), :] = held_ref[which, rows(quarter), columns(head)]


def lower_triangle():
    shape = (TOKENS, TOKENS)
    return lax.broadcasted_iota(jnp.int32, shape, 0) >= lax.broadcasted_iota(jnp.int32, shape, 1)


def running_sums(decay):
    ones = jnp.where(lower_triangle(), 1.0, 0.0).astype(jnp.float32)
    return dot(ones, decay, 1, 0, lax.Precision.HIGHEST)


def split_parts(value):
    coarse = value.astype(jnp.bfloat16).astype(jnp.float32)
    middle = (value - coarse).astype(jnp.bfloat16).astype(jnp.float32)
    parts = (coarse, middle, value - coarse - middle)
    return jnp.concatenate([part.astype(jnp.bfloat16) for part in parts], axis=0)


def join_parts(parts, heads):
    wide = parts.astype(jnp.float32)
    return wide[0:heads] + wide[heads : 2 * heads] + wide[2 * heads : 3 * heads]


def head_rows(head):
    return slice(head * HEAD_DIM, (head + 1) * HEAD_DIM)


def states_kernel(key_ref, value_ref, decay_ref, out_ref):
    decay = decay_ref[...]
    running_sum = running_sums(decay)
    ones = jnp.ones((TOKENS, HEAD_DIM), jnp.float32)
    endings = dot(decay, ones, 0, 0, lax.Precision.HIGHEST)
    out_ref[HEADS_HERE * HEAD_DIM :, :] = split_parts(endings)
    for head in range(HEADS_HERE):
        sums = running_sum[:, head : head + 1]
        ending = running_sum[TOKENS - 1 : TOKENS, head : head + 1]
        key_wide = key_ref[:, columns(head)].astype(jnp.float32)
        key_scaled = (key_wide * jnp.exp(ending - sums)).astype(jnp.bfloat16)
        state = dot(key_scaled, value_ref[:, columns(head)], 0, 0)
        out_ref[head_rows(head), :] = state.astype(jnp.bfloat16)


def chip_kernel(place_ref, mine_ref, other_ref, out_ref, ending_ref):
    first = place_ref[CORE] == 0
    tail = slice(HEADS_HERE * HEAD_DIM, None)
    mine = join_parts(mine_ref[tail, :], HEADS_HERE)
    other = join_parts(other_ref[tail, :], HEADS_HERE)
    both = mine + other
    later = jnp.where(first, other, mine)
    ending_ref[...] = jnp.where(first, both[0:HALF], both[HALF:])
    part = lax.broadcasted_iota(jnp.int32, (8, HEAD_DIM), 0)
    for head in range(HALF):
        ending = ending_ref[head : head + 1, :]
        coarse = ending.astype(jnp.bfloat16).astype(jnp.float32)
        middle = (ending - coarse).astype(jnp.bfloat16).astype(jnp.float32)
        fine = ending - coarse - middle
        parts = jnp.where(part == 0, coarse, jnp.where(part == 1, middle, fine))
        for piece in range(HALF):
            out_ref[HALF * head + piece, SLICE:, :] = parts.astype(jnp.bfloat16)
    ending_ref[...] = jnp.where(first, later[0:HALF], later[HALF:])
    for head in range(HALF):
        place = place_ref[CORE] * (HALF * HEAD_DIM) + head * HEAD_DIM
        here = pl.ds(pl.multiple_of(place, HEAD_DIM), HEAD_DIM)
        mine = mine_ref[here, :].astype(jnp.float32)
        other = other_ref[here, :].astype(jnp.float32)
        fade = jnp.exp(ending_ref[head : head + 1, :])
        state = jnp.where(first, fade * mine + other, fade * other + mine)
        pieces = state.astype(jnp.bfloat16).reshape(HALF, SLICE, HEAD_DIM)
        out_ref[HALF * head : HALF * (head + 1), 0:SLICE, :] = pieces


def scan_kernel(moved_ref, out_ref):
    def step(chip, carries):
        following = []
        for core, carry in enumerate(carries):
            source = 2 * chip + core
            out_ref[source] = carry.astype(jnp.bfloat16)
            parts = moved_ref[source, SLICE:, :].astype(jnp.float32)
            ending = parts[0:1] + parts[1:2] + parts[2:3]
            state = moved_ref[source, 0:SLICE, :].astype(jnp.float32)
            following.append(jnp.exp(ending) * carry + state)
        return tuple(following)

    zero = jnp.zeros((SLICE, HEAD_DIM), jnp.float32)
    lax.fori_loop(0, BLOCKS // 2, step, (zero, zero), unroll=4)


def attention_kernel(which, keys, queries, finished, has_state, place_ref, query_ref, *refs):
    count = QUERY_TILE * PIECE
    number = len(which)
    segments, refs = refs[:number], refs[number:]
    if has_state:
        state_in, refs = refs[:2], refs[2 + 1 :]
    if finished.stop and finished.start:
        earlier_ref, refs = refs[0], refs[1:]
    best_all, total_all, score_ref, bias_ref, final_ref, semaphores, final_semaphores = refs[-7:]
    results = refs[:-7]
    held = (best_all, total_all)
    carried = range(finished.stop, queries.stop)
    mine = place_ref[QUARTER]
    ones = jnp.ones((count, HEAD_DIM), jnp.bfloat16)
    lanes = count // HEAD_DIM

    def tile(index):
        return slice(index * QUERY_TILE, (index + 1) * QUERY_TILE)

    def tile_rows(index):
        return pl.ds(index * count, count)

    def state_copies(index, inward):
        copies = []
        for array in range(2):
            inside = held[array].at[tile_rows(index - queries.start), :]
            if inward:
                ends = state_in[array].at[tile_rows(index - queries.start), :], inside
            else:
                ends = inside, results[array - 2].at[tile_rows(index - carried.start), :]
            semaphore = semaphores.at[int(inward), array, index]
            copies.append(pltpu.make_async_copy(*ends, semaphore))
        return copies

    if has_state:
        for index in queries:
            for copy in state_copies(index, True):
                copy.start()
    final_copies = []
    if finished.stop and finished.start:
        place = results[0].at[0 : finished.start * QUERY_TILE]
        final_copies.append(pltpu.make_async_copy(earlier_ref, place, final_semaphores.at[0]))
        final_copies[0].start()

    def positions(shape, dim, quarter):
        row = lax.broadcasted_iota(jnp.int32, shape, dim)
        return (row // PIECE) * TOKENS + row % PIECE + quarter * PIECE

    def widen(value):
        return jnp.concatenate([value] * lanes, axis=1)

    query_places = widen(positions((count, HEAD_DIM), 0, mine))
    for slot, step in enumerate(which):
        allowed = positions((1, count), 1, mine ^ step) <= query_places
        bias_ref[slot] = jnp.where(allowed, 0.0, masked_score)

    for query_tile in queries:
        here = query_tile - queries.start
        best_ref = best_all.at[tile_rows(here), :]
        total_ref = total_all.at[tile_rows(here), :]
        query = query_ref[tile(query_tile), rows(0), :].reshape(count, HEAD_DIM)
        if has_state:
            for copy in state_copies(query_tile, True):
                copy.wait()
            best_before = best_ref[...]
        else:
            best_before = jnp.full((count, HEAD_DIM), masked_score, jnp.float32)
        seen = [key_tile for key_tile in keys if key_tile <= query_tile]

        best = best_before
        for key_tile in seen:
            for slot, segment in enumerate(segments):
                part = tile(key_tile - keys.start)
                key = segment[part, rows(segment.shape[1] // PIECE - 2), :]
                score = dot(query, key.reshape(count, HEAD_DIM), 1, 1)
                if key_tile == query_tile:
                    score += bias_ref[slot]
                score_ref[number * (key_tile - keys.start) + slot] = score
                for lane in range(lanes):
                    best = jnp.maximum(best, score[:, columns(lane)])
        best = jnp.broadcast_to(jnp.max(best, axis=1, keepdims=True), best.shape)
        best_ref[...] = best
        if has_state:
            shrink = jnp.exp2((best_before - best) * exponent_scale)
            total_ref[...] *= jnp.concatenate([shrink, shrink], axis=1)
        else:
            total_ref[...] = jnp.zeros((count, 2 * HEAD_DIM), jnp.float32)

        for key_tile in seen:
            best_wide = widen(best_ref[...])
            weights, values = [], []
            for slot, segment in enumerate(segments):
                score = score_ref[number * (key_tile - keys.start) + slot]
                weight = jnp.exp2((score - best_wide) * exponent_scale)
                weights.append(weight.astype(jnp.bfloat16))
                part = tile(key_tile - keys.start)
                value = segment[part, rows(segment.shape[1] // PIECE - 1), :]
                values.append(jnp.concatenate([value.reshape(count, HEAD_DIM), ones], axis=1))
            total_ref[...] += dot(
                jnp.concatenate(weights, axis=1), jnp.concatenate(values, axis=0), 1, 0
            )
        if query_tile in finished:
            outcome = total_ref[:, :HEAD_DIM] / total_ref[:, HEAD_DIM:]
            slot = tile(query_tile - finished.start)
            final_ref[slot] = outcome.astype(jnp.bfloat16).reshape(QUERY_TILE, PIECE, HEAD_DIM)
            copy = pltpu.make_async_copy(
                final_ref.at[slot],
                results[0].at[tile(query_tile)],
                final_semaphores.at[1 + query_tile],
            )
            copy.start()
            final_copies.append(copy)
        else:
            for copy in state_copies(query_tile, False):
                copy.start()
    for query_tile in carried:
        for copy in state_copies(query_tile, False):
            copy.wait()
    for copy in final_copies:
        copy.wait()


def attend(which, keys, queries, finished, place, packed, segments, state=None, token=(), earlier=()):
    shape = jax.ShapeDtypeStruct
    count = QUERY_TILE * PIECE
    kernel = functools.partial(
        attention_kernel, which, keys, queries, finished, state is not None
    )
    out_shape, out_spaces = [], []
    if finished.stop:
        out_shape.append(shape((finished.stop * QUERY_TILE, PIECE, HEAD_DIM), jnp.bfloat16))
        out_spaces.append(pltpu.HBM)
    left = queries.stop - finished.stop
    if left:
        for width in (HEAD_DIM, 2 * HEAD_DIM):
            out_shape.append(shape((left * count, width), jnp.float32))
            out_spaces.append(pltpu.HBM)
    spaces = [pltpu.SMEM, *[pltpu.VMEM] * (1 + len(segments))]
    if state is not None:
        spaces += [pltpu.HBM, pltpu.HBM, pltpu.VMEM]
    spaces += [pltpu.HBM] * len(earlier)
    return call(
        kernel,
        out_shape,
        (place, packed, *segments, *(state or ()), *token, *earlier),
        2 * 10**8 * len(which) * len(keys),
        spaces,
        out_spaces,
        (
            pltpu.VMEM((len(queries) * count, HEAD_DIM), jnp.float32),
            pltpu.VMEM((len(queries) * count, 2 * HEAD_DIM), jnp.float32),
            pltpu.VMEM((len(which) * len(keys), count, count), jnp.float32),
            pltpu.VMEM((len(which), count, count), jnp.float32),
            pltpu.VMEM((max(len(finished), 1) * QUERY_TILE, PIECE, HEAD_DIM), jnp.bfloat16),
            pltpu.SemaphoreType.DMA((2, 2, BLOCKS // QUERY_TILE)),
            pltpu.SemaphoreType.DMA((1 + BLOCKS // QUERY_TILE,)),
        ),
        limit=24,
    )


def lightning_kernel(
    place_ref, query_ref, key_ref, value_ref, decay_ref, mine_ref, other_ref, sibling_ref, out_ref
):
    second = place_ref[CORE] == 1
    endings = join_parts(sibling_ref[HEADS_HERE * HEAD_DIM :, :], HEADS_HERE)
    decay = decay_ref[...]
    causal = lower_triangle()
    running_sum = running_sums(decay)
    later = jnp.where(causal, 0.0, 1.0).astype(jnp.float32)
    shape = (TOKENS, TOKENS)
    upper = lax.broadcasted_iota(jnp.int32, shape, 0) <= lax.broadcasted_iota(jnp.int32, shape, 1)
    upper = jnp.where(upper, 1.0, 0.0).astype(jnp.float32)
    running_row = dot(decay, upper, 0, 0, lax.Precision.HIGHEST)
    for head in range(HEADS_HERE):
        sums = running_sum[:, head : head + 1]
        spread = sums - running_row[head : head + 1, :]
        query = query_ref[:, columns(head)]
        value = value_ref[:, columns(head)]
        scores = dot(query, key_ref[:, columns(head)], 1, 1)
        decayed = jnp.where(causal, jnp.exp(jnp.where(causal, spread, 0.0)), 0.0) * scores
        total = dot(decayed.astype(jnp.bfloat16), value, 1, 0)
        query_scaled = (query.astype(jnp.float32) * jnp.exp(sums)).astype(jnp.bfloat16)
        half, place = head // HALF, head_rows(head % HALF)
        mine = mine_ref[place, :].astype(jnp.float32)
        other = other_ref[place, :].astype(jnp.float32)
        prior = jnp.where(place_ref[CORE] == half, mine, other)
        fade = jnp.exp(endings[head : head + 1, :])
        passed = fade * prior + sibling_ref[head_rows(head), :].astype(jnp.float32)
        prior = jnp.where(second, passed, prior)
        total += dot(query_scaled, prior.astype(jnp.bfloat16), 1, 0)
        mean = jnp.mean(total * total, axis=1, keepdims=True)
        out_ref[:, columns(head)] = (total * lax.rsqrt(mean + norm_eps)).astype(jnp.bfloat16)


def unpack_kernel(moved_ref, order_ref, out_ref):
    for device in range(BLOCKS):
        head, quarter = place_of(device)
        out_ref[rows(quarter), columns(head)] = moved_ref[device]


def exchange(value):
    return lax.all_to_all(value, "ctx", split_axis=0, concat_axis=0, tiled=True)


def swap(value, step):
    return lax.ppermute(value, "ctx", [(d, d ^ step) for d in range(BLOCKS)])


def shards(lin_query, lin_key, lin_value, log_decay, soft_query, soft_key, soft_value):
    half = jnp.bfloat16
    shape = jax.ShapeDtypeStruct
    index = lax.axis_index("ctx").astype(jnp.int32)
    core = index % 2
    place = jnp.stack([2 * (index // X_STEP % 2) + core, core])
    width = HEADS_HERE * HEAD_DIM
    (packed,) = call(
        pack_kernel,
        [shape((BLOCKS, 3 * PIECE, HEAD_DIM), half)],
        (soft_query, soft_key, soft_value),
        1000,
        [pltpu.HBM] * 3,
        scratch=(pltpu.VMEM((3, TOKENS, width), half), pltpu.SemaphoreType.DMA((3,))),
    )
    kv0 = exchange(packed)
    (states,) = call(
        states_kernel,
        [shape((width + 3 * HEADS_HERE, HEAD_DIM), half)],
        (lin_key, lin_value, log_decay),
        10**8,
    )
    sibling = swap(states, 1)
    on_core = [pltpu.SMEM] + [pltpu.VMEM] * 7
    (chip,) = call(
        chip_kernel,
        [shape((BLOCKS, SLICE + 8, HEAD_DIM), half)],
        (place, states, sibling),
        10**7,
        on_core[:3],
        scratch=(pltpu.VMEM((HALF, HEAD_DIM), jnp.float32),),
    )
    kv0, chip = lax.optimization_barrier((kv0, chip))
    early = BLOCKS // 2
    kv2a = swap(kv0[:early, PIECE:], X_STEP)
    kv1 = swap(kv0[:, PIECE:], 1)
    chips = exchange(chip)

    tiles = BLOCKS // QUERY_TILE
    every, low, high = range(tiles), range(tiles // 2), range(tiles // 2, tiles)
    state = attend((0, 1), every, every, range(0), place, kv0, (kv0, kv1))
    token, kv2a, kv0b = lax.optimization_barrier((state[0][0:8, :], kv2a, kv0[early:, PIECE:]))
    kv3a = swap(kv2a, 1)
    kv2b = swap(kv0b, X_STEP)
    first, *state = attend(
        (2, 3), low, every, low, place, kv0, (kv2a, kv3a), state, (token,)
    )
    token, chips = lax.optimization_barrier((state[0][0:8, :], chips))
    (scanned,) = call(scan_kernel, [shape((BLOCKS, SLICE, HEAD_DIM), half)], (chips,), 10**6)
    token, kv2b = lax.optimization_barrier((token, kv2b))
    kv3b = swap(kv2b, 1)
    prior = exchange(scanned).reshape(HALF * HEAD_DIM, HEAD_DIM)
    (attended,) = attend(
        (2, 3), high, high, high, place, kv0, (kv2b, kv3b), state, (token,), (first,)
    )
    returned = exchange(attended)
    other_prior = swap(prior, 1)
    whole_out = shape((TOKENS, width), half)
    (lin_out,) = call(
        lightning_kernel,
        [whole_out],
        (place, lin_query, lin_key, lin_value, log_decay, prior, other_prior, sibling),
        2 * 10**8,
        on_core[:8],
    )
    token, returned = lax.optimization_barrier((lin_out[0:8, 0:HEAD_DIM], returned))
    (soft_out,) = call(unpack_kernel, [whole_out], (returned, token), 1000)
    return (lin_out, soft_out)


def solution(mesh):
    spec = P("ctx", "head")
    return jax.shard_map(
        shards, mesh=mesh, in_specs=(spec,) * 7, out_specs=(spec, spec), check_vma=False
    )
```

```python
import functools
import math

import jax
import jax.numpy as jnp
from jax import lax
from jax.experimental import pallas as pl
from jax.experimental.pallas import tpu as pltpu
from jax.sharding import PartitionSpec as P

HEAD_DIM = 128
TOKENS = 128
HEADS_HERE = 16
BLOCKS = 64
PIECE = 32

norm_eps = 1e-06
masked_score = -1e30
exponent_scale = HEAD_DIM ** (-0.5) * math.log2(math.e)
X_STEP = 16
HALF = HEADS_HERE // 2
SLICE = HALF * HEAD_DIM // BLOCKS
QUARTER, CORE = range(2)
QUERY_TILE = 8


def place_of(device):
    x, z, core = device // 16, device // 2 % 8, device % 2
    return 2 * z + x // 2, 2 * (x % 2) + core


def columns(head):
    return slice(head * HEAD_DIM, (head + 1) * HEAD_DIM)


def rows(quarter):
    return slice(quarter * PIECE, (quarter + 1) * PIECE)


def whole(space=pltpu.VMEM):
    return pl.BlockSpec(memory_space=space)


def dot(left, right, left_dim, right_dim, precision=None):
    return lax.dot_general(
        left,
        right,
        (((left_dim,), (right_dim,)), ((), ())),
        precision=precision,
        preferred_element_type=jnp.float32,
    )


def call(kernel, out_shape, operands, flops, spaces=None, out_spaces=None, scratch=(), limit=16):
    out_shape = tuple(out_shape)
    bytes_moved = sum(math.prod(o.shape) * o.dtype.itemsize for o in (*operands, *out_shape))
    spaces = spaces or [pltpu.VMEM] * len(operands)
    out_spaces = out_spaces or [pltpu.VMEM] * len(out_shape)
    operands = [
        pltpu.with_memory_space_constraint(o, space) if space is pltpu.HBM else o
        for o, space in zip(operands, spaces)
    ]
    out_shape = [
        pltpu.HBM(o.shape, o.dtype) if space is pltpu.HBM else o
        for o, space in zip(out_shape, out_spaces)
    ]
    return pl.pallas_call(
        kernel,
        out_shape=out_shape,
        in_specs=[whole(space) for space in spaces],
        out_specs=[whole(space) for space in out_spaces],
        scratch_shapes=list(scratch),
        compiler_params=pltpu.CompilerParams(vmem_limit_bytes=limit << 20),
        cost_estimate=pl.CostEstimate(
            flops=flops, bytes_accessed=bytes_moved, transcendentals=0
        ),
    )(*operands)


def pack_kernel(query_ref, key_ref, value_ref, out_ref, held_ref, semaphores):
    sources = (query_ref, key_ref, value_ref)
    copies = [
        pltpu.make_async_copy(source, held_ref.at[which], semaphores.at[which])
        for which, source in enumerate(sources)
    ]
    for copy in copies:
        copy.start()
    for which, copy in enumerate(copies):
        copy.wait()
        for device in range(BLOCKS):
            head, quarter = place_of(device)
            out_ref[device, rows(which), :] = held_ref[which, rows(quarter), columns(head)]


def lower_triangle():
    shape = (TOKENS, TOKENS)
    return lax.broadcasted_iota(jnp.int32, shape, 0) >= lax.broadcasted_iota(jnp.int32, shape, 1)


def running_sums(decay):
    ones = jnp.where(lower_triangle(), 1.0, 0.0).astype(jnp.float32)
    return dot(ones, decay, 1, 0, lax.Precision.HIGHEST)


def split_parts(value):
    coarse = value.astype(jnp.bfloat16).astype(jnp.float32)
    middle = (value - coarse).astype(jnp.bfloat16).astype(jnp.float32)
    parts = (coarse, middle, value - coarse - middle)
    return jnp.concatenate([part.astype(jnp.bfloat16) for part in parts], axis=0)


def join_parts(parts, heads):
    wide = parts.astype(jnp.float32)
    return wide[0:heads] + wide[heads : 2 * heads] + wide[2 * heads : 3 * heads]


def head_rows(head):
    return slice(head * HEAD_DIM, (head + 1) * HEAD_DIM)


def states_kernel(key_ref, value_ref, decay_ref, out_ref):
    decay = decay_ref[...]
    running_sum = running_sums(decay)
    ones = jnp.ones((TOKENS, HEAD_DIM), jnp.float32)
    endings = dot(decay, ones, 0, 0, lax.Precision.HIGHEST)
    out_ref[HEADS_HERE * HEAD_DIM :, :] = split_parts(endings)
    for head in range(HEADS_HERE):
        sums = running_sum[:, head : head + 1]
        ending = running_sum[TOKENS - 1 : TOKENS, head : head + 1]
        key_wide = key_ref[:, columns(head)].astype(jnp.float32)
        key_scaled = (key_wide * jnp.exp(ending - sums)).astype(jnp.bfloat16)
        state = dot(key_scaled, value_ref[:, columns(head)], 0, 0)
        out_ref[head_rows(head), :] = state.astype(jnp.bfloat16)


def chip_kernel(place_ref, mine_ref, other_ref, out_ref, ending_ref):
    first = place_ref[CORE] == 0
    tail = slice(HEADS_HERE * HEAD_DIM, None)
    mine = join_parts(mine_ref[tail, :], HEADS_HERE)
    other = join_parts(other_ref[tail, :], HEADS_HERE)
    both = mine + other
    later = jnp.where(first, other, mine)
    ending_ref[...] = jnp.where(first, both[0:HALF], both[HALF:])
    part = lax.broadcasted_iota(jnp.int32, (8, HEAD_DIM), 0)
    for head in range(HALF):
        ending = ending_ref[head : head + 1, :]
        coarse = ending.astype(jnp.bfloat16).astype(jnp.float32)
        middle = (ending - coarse).astype(jnp.bfloat16).astype(jnp.float32)
        fine = ending - coarse - middle
        parts = jnp.where(part == 0, coarse, jnp.where(part == 1, middle, fine))
        for piece in range(HALF):
            out_ref[HALF * head + piece, SLICE:, :] = parts.astype(jnp.bfloat16)
    ending_ref[...] = jnp.where(first, later[0:HALF], later[HALF:])
    for head in range(HALF):
        place = place_ref[CORE] * (HALF * HEAD_DIM) + head * HEAD_DIM
        here = pl.ds(pl.multiple_of(place, HEAD_DIM), HEAD_DIM)
        mine = mine_ref[here, :].astype(jnp.float32)
        other = other_ref[here, :].astype(jnp.float32)
        fade = jnp.exp(ending_ref[head : head + 1, :])
        state = jnp.where(first, fade * mine + other, fade * other + mine)
        pieces = state.astype(jnp.bfloat16).reshape(HALF, SLICE, HEAD_DIM)
        out_ref[HALF * head : HALF * (head + 1), 0:SLICE, :] = pieces


def scan_kernel(moved_ref, out_ref):
    def step(chip, carries):
        following = []
        for core, carry in enumerate(carries):
            source = 2 * chip + core
            out_ref[source] = carry.astype(jnp.bfloat16)
            parts = moved_ref[source, SLICE:, :].astype(jnp.float32)
            ending = parts[0:1] + parts[1:2] + parts[2:3]
            state = moved_ref[source, 0:SLICE, :].astype(jnp.float32)
            following.append(jnp.exp(ending) * carry + state)
        return tuple(following)

    zero = jnp.zeros((SLICE, HEAD_DIM), jnp.float32)
    lax.fori_loop(0, BLOCKS // 2, step, (zero, zero), unroll=4)


def attention_kernel(which, keys, queries, has_state, finishes, place_ref, query_ref, *refs):
    count = QUERY_TILE * PIECE
    tiles = BLOCKS // QUERY_TILE
    halves = 2 if keys.stop > tiles // 2 else 1
    refs = list(refs)
    segments = [[refs.pop(0) for _ in range(halves)] for step in which if step]
    if has_state:
        best_in, total_in, earlier = (refs.pop(0) for _ in range(3))
    refs, (best_ref, total_ref, score_ref, bias_ref, kv_ref, kv_semaphores) = refs[:-6], refs[-6:]
    kv_copies = []
    for number, source in enumerate(jax.tree.leaves(segments)):
        copy = pltpu.make_async_copy(source, kv_ref.at[number], kv_semaphores.at[number])
        copy.start()
        kv_copies.append(copy)
    segments = [
        [kv_ref.at[place * halves + half] for half in range(halves)]
        for place in range(len(segments))
    ]
    if 0 in which:
        segments = [[query_ref] * halves] + segments
    mine = place_ref[QUARTER]
    ones = jnp.ones((count, HEAD_DIM), jnp.bfloat16)
    lanes = count // HEAD_DIM
    copies = []
    if has_state:
        held_best, held_total, final_ref, semaphores = refs[-4:]
        shift = queries.start * QUERY_TILE
        copies = [
            pltpu.make_async_copy(best_in, held_best, semaphores.at[0]),
            pltpu.make_async_copy(total_in, held_total, semaphores.at[1]),
            pltpu.make_async_copy(earlier, final_ref.at[0:shift], semaphores.at[2]),
        ]
        for copy in copies:
            copy.start()

    def positions(shape, dim, quarter):
        row = lax.broadcasted_iota(jnp.int32, shape, dim)
        return (row // PIECE) * TOKENS + row % PIECE + quarter * PIECE

    def widen(value):
        return jnp.concatenate([value] * lanes, axis=1)

    def part_of(segment, key_tile, from_end):
        array = segment[key_tile // (tiles // 2)]
        place = key_tile if array.shape[0] == BLOCKS else key_tile % (tiles // 2)
        blocks = slice(place * QUERY_TILE, (place + 1) * QUERY_TILE)
        return array[blocks, rows(array.shape[1] // PIECE - from_end), :].reshape(count, HEAD_DIM)

    query_places = widen(positions((count, HEAD_DIM), 0, mine))
    for slot, step in enumerate(which):
        allowed = positions((1, count), 1, mine ^ step) <= query_places
        bias_ref[slot] = jnp.where(allowed, 0.0, masked_score)
    for copy in kv_copies:
        copy.wait()

    for query_tile in queries:
        blocks = slice(query_tile * QUERY_TILE, (query_tile + 1) * QUERY_TILE)
        here = slice((query_tile - queries.start) * count, (query_tile - queries.start + 1) * count)
        query = query_ref[blocks, rows(0), :].reshape(count, HEAD_DIM)
        seen = [key_tile for key_tile in keys if key_tile <= query_tile]
        best_ref[here, :] = jnp.full((count, HEAD_DIM), masked_score, jnp.float32)
        for key_tile in seen:
            best = best_ref[here, :]
            for slot, segment in enumerate(segments):
                score = dot(query, part_of(segment, key_tile, 2), 1, 1)
                if key_tile == query_tile:
                    score += bias_ref[slot]
                score_ref[len(which) * key_tile + slot] = score
                for lane in range(lanes):
                    best = jnp.maximum(best, score[:, columns(lane)])
            best_ref[here, :] = best
        best = jnp.max(best_ref[here, :], axis=1, keepdims=True)
        best_ref[here, :] = jnp.broadcast_to(best, (count, HEAD_DIM))
        total_ref[here, :] = jnp.zeros((count, 2 * HEAD_DIM), jnp.float32)
        for key_tile in seen:
            best_wide = widen(best_ref[here, :])
            weights, values = [], []
            for slot, segment in enumerate(segments):
                score = score_ref[len(which) * key_tile + slot]
                weight = jnp.exp2((score - best_wide) * exponent_scale)
                weights.append(weight.astype(jnp.bfloat16))
                values.append(jnp.concatenate([part_of(segment, key_tile, 1), ones], axis=1))
            total_ref[here, :] += dot(
                jnp.concatenate(weights, axis=1), jnp.concatenate(values, axis=0), 1, 0
            )
        if finishes and not has_state:
            total = total_ref[here, :]
            outcome = (total[:, :HEAD_DIM] / total[:, HEAD_DIM:]).astype(jnp.bfloat16)
            refs[0][blocks] = outcome.reshape(QUERY_TILE, PIECE, HEAD_DIM)

    for copy in copies:
        copy.wait()
    if has_state:
        for query_tile in queries:
            blocks = slice(query_tile * QUERY_TILE, (query_tile + 1) * QUERY_TILE)
            start = (query_tile - queries.start) * count
            here = slice(start, start + count)
            best = jnp.maximum(best_ref[here, :], held_best[here, :])
            fresh = jnp.exp2((best_ref[here, :] - best) * exponent_scale)
            before = jnp.exp2((held_best[here, :] - best) * exponent_scale)
            low, high = slice(0, HEAD_DIM), slice(HEAD_DIM, 2 * HEAD_DIM)
            value = fresh * total_ref[here, low] + before * held_total[here, low]
            mass = fresh * total_ref[here, high] + before * held_total[here, high]
            outcome = (value / mass).astype(jnp.bfloat16)
            final_ref[blocks] = outcome.reshape(QUERY_TILE, PIECE, HEAD_DIM)
        copy = pltpu.make_async_copy(final_ref, refs[0], semaphores.at[3])
        copy.start()
        copy.wait()
    elif finishes:
        refs[1][...] = total_ref[0:8, 0:HEAD_DIM]
    else:
        semaphores = refs[3]
        outward = [
            pltpu.make_async_copy(best_ref, refs[0], semaphores.at[0]),
            pltpu.make_async_copy(total_ref, refs[1], semaphores.at[1]),
        ]
        for copy in outward:
            copy.start()
        refs[2][...] = best_ref[0:8, :]
        for copy in outward:
            copy.wait()


def attend(which, keys, queries, place, packed, segments, state=(), token=(), finishes=True):
    shape = jax.ShapeDtypeStruct
    count = QUERY_TILE * PIECE
    kernel = functools.partial(attention_kernel, which, keys, queries, bool(state), finishes)
    best_shape = (len(queries) * count, HEAD_DIM)
    total_shape = (len(queries) * count, 2 * HEAD_DIM)
    token_shape = shape((8, HEAD_DIM), jnp.float32)
    scratch = []
    if state:
        out_shape = [shape((BLOCKS, PIECE, HEAD_DIM), jnp.bfloat16)]
        out_spaces = [pltpu.HBM]
        scratch = [
            pltpu.VMEM(best_shape, jnp.float32),
            pltpu.VMEM(total_shape, jnp.float32),
            pltpu.VMEM((BLOCKS, PIECE, HEAD_DIM), jnp.bfloat16),
            pltpu.SemaphoreType.DMA((4,)),
        ]
    elif finishes:
        out_shape = [shape((len(queries) * QUERY_TILE, PIECE, HEAD_DIM), jnp.bfloat16), token_shape]
        out_spaces = [pltpu.VMEM, pltpu.VMEM]
    else:
        out_shape = [shape(best_shape, jnp.float32), shape(total_shape, jnp.float32), token_shape]
        out_spaces = [pltpu.HBM, pltpu.HBM, pltpu.VMEM]
        scratch = [pltpu.SemaphoreType.DMA((2,))]
    segments = jax.tree.leaves(segments)
    spaces = [pltpu.SMEM, pltpu.VMEM, *[pltpu.HBM] * (len(segments) + len(state))]
    spaces += [pltpu.VMEM] * len(token)

    def without_token(*refs):
        place = 2 + len(segments) + len(state)
        kernel(*refs[:place], *refs[place + len(token) :])

    return call(
        without_token,
        out_shape,
        (place, packed, *segments, *state, *token),
        10**8 * len(which) * len(keys),
        spaces,
        out_spaces,
        (
            *scratch,
            pltpu.VMEM(best_shape, jnp.float32),
            pltpu.VMEM(total_shape, jnp.float32),
            pltpu.VMEM((len(which) * len(keys), count, count), jnp.float32),
            pltpu.VMEM((len(which), count, count), jnp.float32),
            pltpu.VMEM((len(segments), BLOCKS // 2, 2 * PIECE, HEAD_DIM), jnp.bfloat16),
            pltpu.SemaphoreType.DMA((len(segments),)),
        ),
        limit=24,
    )


def lightning_kernel(
    place_ref, query_ref, key_ref, value_ref, decay_ref, mine_ref, other_ref, sibling_ref, out_ref
):
    second = place_ref[CORE] == 1
    endings = join_parts(sibling_ref[HEADS_HERE * HEAD_DIM :, :], HEADS_HERE)
    decay = decay_ref[...]
    causal = lower_triangle()
    running_sum = running_sums(decay)
    later = jnp.where(causal, 0.0, 1.0).astype(jnp.float32)
    shape = (TOKENS, TOKENS)
    upper = lax.broadcasted_iota(jnp.int32, shape, 0) <= lax.broadcasted_iota(jnp.int32, shape, 1)
    upper = jnp.where(upper, 1.0, 0.0).astype(jnp.float32)
    running_row = dot(decay, upper, 0, 0, lax.Precision.HIGHEST)
    for head in range(HEADS_HERE):
        sums = running_sum[:, head : head + 1]
        spread = sums - running_row[head : head + 1, :]
        query = query_ref[:, columns(head)]
        value = value_ref[:, columns(head)]
        scores = dot(query, key_ref[:, columns(head)], 1, 1)
        decayed = jnp.where(causal, jnp.exp(jnp.where(causal, spread, 0.0)), 0.0) * scores
        total = dot(decayed.astype(jnp.bfloat16), value, 1, 0)
        query_scaled = (query.astype(jnp.float32) * jnp.exp(sums)).astype(jnp.bfloat16)
        half, place = head // HALF, head_rows(head % HALF)
        mine = mine_ref[place, :].astype(jnp.float32)
        other = other_ref[place, :].astype(jnp.float32)
        prior = jnp.where(place_ref[CORE] == half, mine, other)
        fade = jnp.exp(endings[head : head + 1, :])
        passed = fade * prior + sibling_ref[head_rows(head), :].astype(jnp.float32)
        prior = jnp.where(second, passed, prior)
        total += dot(query_scaled, prior.astype(jnp.bfloat16), 1, 0)
        mean = jnp.mean(total * total, axis=1, keepdims=True)
        out_ref[:, columns(head)] = (total * lax.rsqrt(mean + norm_eps)).astype(jnp.bfloat16)


def unpack_kernel(moved_ref, order_ref, out_ref):
    for device in range(BLOCKS):
        head, quarter = place_of(device)
        out_ref[rows(quarter), columns(head)] = moved_ref[device]


def exchange(value):
    return lax.all_to_all(value, "ctx", split_axis=0, concat_axis=0, tiled=True)


def swap(value, step):
    return lax.ppermute(value, "ctx", [(d, d ^ step) for d in range(BLOCKS)])


def shards(lin_query, lin_key, lin_value, log_decay, soft_query, soft_key, soft_value):
    half = jnp.bfloat16
    shape = jax.ShapeDtypeStruct
    index = lax.axis_index("ctx").astype(jnp.int32)
    core = index % 2
    place = jnp.stack([2 * (index // X_STEP % 2) + core, core])
    width = HEADS_HERE * HEAD_DIM
    (packed,) = call(
        pack_kernel,
        [shape((BLOCKS, 3 * PIECE, HEAD_DIM), half)],
        (soft_query, soft_key, soft_value),
        1000,
        [pltpu.HBM] * 3,
        scratch=(pltpu.VMEM((3, TOKENS, width), half), pltpu.SemaphoreType.DMA((3,))),
    )
    kv0 = exchange(packed)
    (states,) = call(
        states_kernel,
        [shape((width + 3 * HEADS_HERE, HEAD_DIM), half)],
        (lin_key, lin_value, log_decay),
        10**8,
    )
    sibling = swap(states, 1)
    on_core = [pltpu.SMEM] + [pltpu.VMEM] * 7
    (chip,) = call(
        chip_kernel,
        [shape((BLOCKS, SLICE + 8, HEAD_DIM), half)],
        (place, states, sibling),
        10**7,
        on_core[:3],
        scratch=(pltpu.VMEM((HALF, HEAD_DIM), jnp.float32),),
    )
    kv0, chip = lax.optimization_barrier((kv0, chip))
    half_blocks = BLOCKS // 2
    kv0a, kv0 = lax.optimization_barrier((kv0[:half_blocks, PIECE:], kv0))
    kv0b = kv0[half_blocks:, PIECE:]
    kv2a = swap(kv0a, X_STEP)
    kv1a, kv1b = swap(kv0a, 1), swap(kv0b, 1)
    chips = exchange(chip)

    tiles = BLOCKS // QUERY_TILE
    early, late = range(tiles // 2), range(tiles // 2, tiles)
    best, total, token = attend(
        (0, 1), range(tiles), late, place, kv0, ((kv1a, kv1b),), finishes=False
    )
    token, kv2a, kv0b = lax.optimization_barrier((token, kv2a, kv0b))
    kv3a = swap(kv2a, 1)
    kv2b = swap(kv0b, X_STEP)
    first, token = attend(
        (0, 1, 2, 3), early, early, place, kv0, ((kv1a,), (kv2a,), (kv3a,)), (), (token,)
    )
    token, chips, kv2b = lax.optimization_barrier((token, chips, kv2b))
    kv3b = swap(kv2b, 1)
    (scanned,) = call(scan_kernel, [shape((BLOCKS, SLICE, HEAD_DIM), half)], (chips,), 10**6)
    prior = exchange(scanned).reshape(HALF * HEAD_DIM, HEAD_DIM)
    (attended,) = attend(
        (2, 3),
        range(tiles),
        late,
        place,
        kv0,
        ((kv2a, kv2b), (kv3a, kv3b)),
        (best, total, first),
        (token,),
    )
    returned = exchange(attended)
    other_prior = swap(prior, 1)
    whole_out = shape((TOKENS, width), half)
    (lin_out,) = call(
        lightning_kernel,
        [whole_out],
        (place, lin_query, lin_key, lin_value, log_decay, prior, other_prior, sibling),
        2 * 10**8,
        on_core[:8],
    )
    token, returned = lax.optimization_barrier((lin_out[0:8, 0:HEAD_DIM], returned))
    (soft_out,) = call(unpack_kernel, [whole_out], (returned, token), 1000)
    return (lin_out, soft_out)


def solution(mesh):
    spec = P("ctx", "head")
    return jax.shard_map(
        shards, mesh=mesh, in_specs=(spec,) * 7, out_specs=(spec, spec), check_vma=False
    )
```

```python
import functools
import math

import jax
import jax.numpy as jnp
from jax import lax
from jax.experimental import pallas as pl
from jax.experimental.pallas import tpu as pltpu
from jax.sharding import PartitionSpec as P

HEAD_DIM = 128
TOKENS = 128
HEADS_HERE = 16
BLOCKS = 64
PIECE = 32

norm_eps = 1e-06
masked_score = -1e30
exponent_scale = HEAD_DIM ** (-0.5) * math.log2(math.e)
X_STEP = 16
HALF = HEADS_HERE // 2
SLICE = HALF * HEAD_DIM // BLOCKS
QUARTER, CORE = range(2)
QUERY_TILE = 8
TILE_ROWS = QUERY_TILE * PIECE
LANES = TILE_ROWS // HEAD_DIM
TILES = BLOCKS // QUERY_TILE
HALF_TILES = TILES // 2
EARLY, LATE = range(HALF_TILES), range(HALF_TILES, TILES)


def place_of(device):
    x, z, core = device // 16, device // 2 % 8, device % 2
    return 2 * z + x // 2, 2 * (x % 2) + core


def columns(head):
    return slice(head * HEAD_DIM, (head + 1) * HEAD_DIM)


def rows(quarter):
    return slice(quarter * PIECE, (quarter + 1) * PIECE)


def whole(space=pltpu.VMEM):
    return pl.BlockSpec(memory_space=space)


def dot(left, right, left_dim, right_dim, precision=None):
    return lax.dot_general(
        left,
        right,
        (((left_dim,), (right_dim,)), ((), ())),
        precision=precision,
        preferred_element_type=jnp.float32,
    )


def call(kernel, out_shape, operands, flops, spaces=None, out_spaces=None, scratch=(), limit=16):
    out_shape = tuple(out_shape)
    bytes_moved = sum(math.prod(o.shape) * o.dtype.itemsize for o in (*operands, *out_shape))
    spaces = spaces or [pltpu.VMEM] * len(operands)
    out_spaces = out_spaces or [pltpu.VMEM] * len(out_shape)
    operands = [
        pltpu.with_memory_space_constraint(o, space) if space is pltpu.HBM else o
        for o, space in zip(operands, spaces)
    ]
    out_shape = [
        pltpu.HBM(o.shape, o.dtype) if space is pltpu.HBM else o
        for o, space in zip(out_shape, out_spaces)
    ]
    return pl.pallas_call(
        kernel,
        out_shape=out_shape,
        in_specs=[whole(space) for space in spaces],
        out_specs=[whole(space) for space in out_spaces],
        scratch_shapes=list(scratch),
        compiler_params=pltpu.CompilerParams(vmem_limit_bytes=limit << 20),
        cost_estimate=pl.CostEstimate(
            flops=flops, bytes_accessed=bytes_moved if flops else 0, transcendentals=0
        ),
    )(*operands)


def pack_kernel(query_ref, key_ref, value_ref, out_ref, held_ref, semaphores):
    sources = (query_ref, key_ref, value_ref)
    copies = [
        pltpu.make_async_copy(source, held_ref.at[which], semaphores.at[which])
        for which, source in enumerate(sources)
    ]
    for copy in copies:
        copy.start()
    for which, copy in enumerate(copies):
        copy.wait()
        for device in range(BLOCKS):
            head, quarter = place_of(device)
            out_ref[device, rows(which), :] = held_ref[which, rows(quarter), columns(head)]


def lower_triangle():
    shape = (TOKENS, TOKENS)
    return lax.broadcasted_iota(jnp.int32, shape, 0) >= lax.broadcasted_iota(jnp.int32, shape, 1)


def running_sums(decay):
    ones = jnp.where(lower_triangle(), 1.0, 0.0).astype(jnp.float32)
    return dot(ones, decay, 1, 0, lax.Precision.HIGHEST)


def split_parts(value):
    coarse = value.astype(jnp.bfloat16).astype(jnp.float32)
    middle = (value - coarse).astype(jnp.bfloat16).astype(jnp.float32)
    parts = (coarse, middle, value - coarse - middle)
    return jnp.concatenate([part.astype(jnp.bfloat16) for part in parts], axis=0)


def join_parts(parts, heads):
    wide = parts.astype(jnp.float32)
    return wide[0:heads] + wide[heads : 2 * heads] + wide[2 * heads : 3 * heads]


def head_rows(head):
    return slice(head * HEAD_DIM, (head + 1) * HEAD_DIM)


def states_kernel(key_ref, value_ref, decay_ref, out_ref):
    decay = decay_ref[...]
    running_sum = running_sums(decay)
    ones = jnp.ones((TOKENS, HEAD_DIM), jnp.float32)
    endings = dot(decay, ones, 0, 0, lax.Precision.HIGHEST)
    out_ref[HEADS_HERE * HEAD_DIM :, :] = split_parts(endings)
    for head in range(HEADS_HERE):
        sums = running_sum[:, head : head + 1]
        ending = running_sum[TOKENS - 1 : TOKENS, head : head + 1]
        key_wide = key_ref[:, columns(head)].astype(jnp.float32)
        key_scaled = (key_wide * jnp.exp(ending - sums)).astype(jnp.bfloat16)
        state = dot(key_scaled, value_ref[:, columns(head)], 0, 0)
        out_ref[head_rows(head), :] = state.astype(jnp.bfloat16)


def chip_kernel(place_ref, mine_ref, other_ref, out_ref, ending_ref):
    first = place_ref[CORE] == 0
    tail = slice(HEADS_HERE * HEAD_DIM, None)
    mine = join_parts(mine_ref[tail, :], HEADS_HERE)
    other = join_parts(other_ref[tail, :], HEADS_HERE)
    both = mine + other
    later = jnp.where(first, other, mine)
    ending_ref[...] = jnp.where(first, both[0:HALF], both[HALF:])
    part = lax.broadcasted_iota(jnp.int32, (8, HEAD_DIM), 0)
    for head in range(HALF):
        ending = ending_ref[head : head + 1, :]
        coarse = ending.astype(jnp.bfloat16).astype(jnp.float32)
        middle = (ending - coarse).astype(jnp.bfloat16).astype(jnp.float32)
        fine = ending - coarse - middle
        parts = jnp.where(part == 0, coarse, jnp.where(part == 1, middle, fine))
        for piece in range(HALF):
            out_ref[HALF * head + piece, SLICE:, :] = parts.astype(jnp.bfloat16)
    ending_ref[...] = jnp.where(first, later[0:HALF], later[HALF:])
    for head in range(HALF):
        place = place_ref[CORE] * (HALF * HEAD_DIM) + head * HEAD_DIM
        here = pl.ds(pl.multiple_of(place, HEAD_DIM), HEAD_DIM)
        mine = mine_ref[here, :].astype(jnp.float32)
        other = other_ref[here, :].astype(jnp.float32)
        fade = jnp.exp(ending_ref[head : head + 1, :])
        state = jnp.where(first, fade * mine + other, fade * other + mine)
        pieces = state.astype(jnp.bfloat16).reshape(HALF, SLICE, HEAD_DIM)
        out_ref[HALF * head : HALF * (head + 1), 0:SLICE, :] = pieces


def scan_kernel(moved_ref, out_ref):
    def step(chip, carries):
        following = []
        for core, carry in enumerate(carries):
            source = 2 * chip + core
            out_ref[source] = carry.astype(jnp.bfloat16)
            parts = moved_ref[source, SLICE:, :].astype(jnp.float32)
            ending = parts[0:1] + parts[1:2] + parts[2:3]
            state = moved_ref[source, 0:SLICE, :].astype(jnp.float32)
            following.append(jnp.exp(ending) * carry + state)
        return tuple(following)

    zero = jnp.zeros((SLICE, HEAD_DIM), jnp.float32)
    lax.fori_loop(0, BLOCKS // 2, step, (zero, zero), unroll=4)


def tile_pairs(queries, keys):
    return [(query, key) for query in queries for key in keys if key <= query]


def tile_blocks(index):
    return slice(index * QUERY_TILE, (index + 1) * QUERY_TILE)


class Attention:
    def __init__(self, queries, keys, slots, query_ref, part, bias_ref, best_ref, total_ref, score_ref):
        self.queries, self.keys, self.slots = queries, keys, slots
        self.query_ref, self.part, self.bias_ref = query_ref, part, bias_ref
        self.best_ref, self.total_ref, self.score_ref = best_ref, total_ref, score_ref
        self.pairs = tile_pairs(queries, keys)
        best_ref[...] = jnp.full(best_ref.shape, masked_score, jnp.float32)

    def here(self, query_tile):
        start = (query_tile - self.queries.start) * TILE_ROWS
        return slice(start, start + TILE_ROWS)

    def place(self, query_tile, key_tile, slot):
        return len(self.slots) * self.pairs.index((query_tile, key_tile)) + self.slots.index(slot)

    def find_best(self, query_tile, slots):
        here = self.here(query_tile)
        query = self.query_ref[tile_blocks(query_tile), rows(0), :].reshape(TILE_ROWS, HEAD_DIM)
        for key_tile in self.keys:
            if key_tile > query_tile or not slots:
                continue
            best = self.best_ref[here, :]
            for slot in slots:
                score = dot(query, self.part(slot, key_tile, 2), 1, 1)
                if key_tile == query_tile:
                    score += self.bias_ref[slot]
                self.score_ref[self.place(query_tile, key_tile, slot)] = score
                for lane in range(LANES):
                    best = jnp.maximum(best, score[:, columns(lane)])
            self.best_ref[here, :] = best

    def add_up(self, query_tile):
        here = self.here(query_tile)
        best = jnp.max(self.best_ref[here, :], axis=1, keepdims=True)
        self.best_ref[here, :] = jnp.broadcast_to(best, (TILE_ROWS, HEAD_DIM))
        self.total_ref[here, :] = jnp.zeros((TILE_ROWS, 2 * HEAD_DIM), jnp.float32)
        ones = jnp.ones((TILE_ROWS, HEAD_DIM), jnp.bfloat16)
        for key_tile in self.keys:
            if key_tile > query_tile:
                continue
            best_wide = jnp.concatenate([self.best_ref[here, :]] * LANES, axis=1)
            weights, values = [], []
            for slot in self.slots:
                score = self.score_ref[self.place(query_tile, key_tile, slot)]
                weight = jnp.exp2((score - best_wide) * exponent_scale)
                weights.append(weight.astype(jnp.bfloat16))
                values.append(jnp.concatenate([self.part(slot, key_tile, 1), ones], axis=1))
            self.total_ref[here, :] += dot(
                jnp.concatenate(weights, axis=1), jnp.concatenate(values, axis=0), 1, 0
            )


def load_part(array, place, from_end):
    wanted = rows(array.shape[1] // PIECE - from_end)
    return array[tile_blocks(place), wanted, :].reshape(TILE_ROWS, HEAD_DIM)


def fill_bias(place_ref, bias_ref, steps):
    mine = place_ref[QUARTER]

    def positions(shape, dim, quarter):
        row = lax.broadcasted_iota(jnp.int32, shape, dim)
        return (row // PIECE) * TOKENS + row % PIECE + quarter * PIECE

    queries = positions((TILE_ROWS, HEAD_DIM), 0, mine)
    queries = jnp.concatenate([queries] * LANES, axis=1)
    for slot, step in enumerate(steps):
        allowed = positions((1, TILE_ROWS), 1, mine ^ step) <= queries
        bias_ref[slot] = jnp.where(allowed, 0.0, masked_score)


def start_copies(sources, targets, semaphores):
    copies = [
        pltpu.make_async_copy(source, target, semaphores.at[number])
        for number, (source, target) in enumerate(zip(sources, targets))
    ]
    for copy in copies:
        copy.start()
    return copies


def ratio(total):
    outcome = (total[:, :HEAD_DIM] / total[:, HEAD_DIM:]).astype(jnp.bfloat16)
    return outcome.reshape(QUERY_TILE, PIECE, HEAD_DIM)


def first_kernel(
    place_ref, packed_ref, early_ref, late_ref, best_out, total_out, token_ref,
    kv_ref, bias_ref, best_ref, total_ref, score_ref, kv_sems, out_sems,
):
    copies = start_copies((early_ref, late_ref), (kv_ref.at[0], kv_ref.at[1]), kv_sems)
    fill_bias(place_ref, bias_ref, (0, 1))

    def part(slot, key_tile, from_end):
        if slot == 0:
            return load_part(packed_ref, key_tile, from_end)
        return load_part(kv_ref.at[key_tile // HALF_TILES], key_tile % HALF_TILES, from_end)

    work = Attention(
        LATE, range(TILES), (0, 1), packed_ref, part, bias_ref, best_ref, total_ref, score_ref
    )
    for query_tile in LATE:
        work.find_best(query_tile, (0,))
    for copy in copies:
        copy.wait()
    outward, sent = [], 0
    for query_tile in LATE:
        work.find_best(query_tile, (1,))
        work.add_up(query_tile)
        if query_tile >= TILES - 2:
            done = work.here(query_tile).stop
            place = pl.ds(sent, done - sent)
            outward += start_copies(
                (best_ref.at[place, :], total_ref.at[place, :]),
                (best_out.at[place, :], total_out.at[place, :]),
                out_sems.at[query_tile - (TILES - 2)],
            )
            sent = done
    token_ref[...] = best_ref[0:8, :]
    for copy in outward:
        copy.wait()


def second_kernel(
    place_ref, packed_ref, sibling_ref, across_ref, diagonal_ref, order_ref,
    best_out, total_out, final_out, token_ref,
    kv_ref, bias_ref, best_ref, total_ref, score_ref, best2_ref, total2_ref, score2_ref, final_ref,
    kv_sems, out_sems, final_sem,
):
    copies = start_copies((across_ref, sibling_ref), (kv_ref.at[1], kv_ref.at[0]), kv_sems)
    fill_bias(place_ref, bias_ref, (0, 1, 2, 3))

    def part(slot, key_tile, from_end):
        if slot == 0:
            return load_part(packed_ref, key_tile, from_end)
        return load_part(diagonal_ref if slot == 3 else kv_ref.at[slot - 1], key_tile, from_end)

    early = Attention(
        EARLY, EARLY, (0, 1, 2, 3), packed_ref, part, bias_ref, best2_ref, total2_ref, score2_ref
    )
    for query_tile in EARLY:
        early.find_best(query_tile, (0,))
    late = Attention(
        LATE, EARLY, (2, 3), packed_ref, part, bias_ref, best_ref, total_ref, score_ref
    )
    for copy in copies:
        copy.wait()
    for query_tile in LATE:
        late.find_best(query_tile, (2, 3))
        late.add_up(query_tile)
    outward = start_copies((best_ref, total_ref), (best_out, total_out), out_sems)
    for query_tile in EARLY:
        early.find_best(query_tile, (1, 2, 3))
        early.add_up(query_tile)
        final_ref[tile_blocks(query_tile)] = ratio(total2_ref[early.here(query_tile), :])
    copy = pltpu.make_async_copy(final_ref, final_out, final_sem)
    copy.start()
    token_ref[...] = best2_ref[0:8, :]
    for other in outward:
        other.wait()
    copy.wait()


def third_kernel(
    place_ref, packed_ref, across_ref, diagonal_ref, best_a, total_a, best_b, total_b, final_in, order_ref,
    out_ref,
    kv_ref, bias_ref, best_ref, total_ref, score_ref, bests_ref, totals_ref, final_ref,
    kv_sems, state_sems, final_sems,
):
    copies = start_copies((across_ref, diagonal_ref), (kv_ref.at[0], kv_ref.at[1]), kv_sems)
    half_blocks = BLOCKS // 2
    state = start_copies(
        (best_a, best_b, total_a, total_b, final_in),
        (bests_ref.at[0], bests_ref.at[1], totals_ref.at[0], totals_ref.at[1], final_ref.at[0:half_blocks]),
        state_sems,
    )
    fill_bias(place_ref, bias_ref, (2, 3))

    def part(slot, key_tile, from_end):
        return load_part(kv_ref.at[slot], key_tile % HALF_TILES, from_end)

    for copy in copies:
        copy.wait()
    work = Attention(
        LATE, LATE, (0, 1), packed_ref, part, bias_ref, best_ref, total_ref, score_ref
    )
    for query_tile in LATE:
        work.find_best(query_tile, (0, 1))
        work.add_up(query_tile)
    for copy in state:
        copy.wait()
    outward = start_copies(
        (final_ref.at[0:half_blocks],), (out_ref.at[0:half_blocks],), final_sems
    )
    for query_tile in LATE:
        here = work.here(query_tile)
        bests = [best_ref[here, :], bests_ref[0, here, :], bests_ref[1, here, :]]
        totals = [total_ref[here, :], totals_ref[0, here, :], totals_ref[1, here, :]]
        best = functools.reduce(jnp.maximum, bests)
        joined = 0.0
        for one, total in zip(bests, totals):
            shrink = jnp.exp2((one - best) * exponent_scale)
            joined += jnp.concatenate([shrink, shrink], axis=1) * total
        blocks = tile_blocks(query_tile)
        final_ref[blocks] = ratio(joined)
        outward += start_copies(
            (final_ref.at[blocks],),
            (out_ref.at[blocks],),
            final_sems.at[1 + query_tile - LATE.start : 2 + query_tile - LATE.start],
        )
    for copy in outward:
        copy.wait()


def work_space(queries, keys, slots):
    rows_here = len(queries) * TILE_ROWS
    return [
        pltpu.VMEM((rows_here, HEAD_DIM), jnp.float32),
        pltpu.VMEM((rows_here, 2 * HEAD_DIM), jnp.float32),
        pltpu.VMEM((slots * len(tile_pairs(queries, keys)), TILE_ROWS, TILE_ROWS), jnp.float32),
    ]


def final_space(blocks):
    return pltpu.VMEM((blocks, PIECE, HEAD_DIM), jnp.bfloat16)


def attention_space(segments, slots):
    return [
        pltpu.VMEM((segments, BLOCKS // 2, 2 * PIECE, HEAD_DIM), jnp.bfloat16),
        pltpu.VMEM((slots, TILE_ROWS, TILE_ROWS), jnp.float32),
    ]


def lightning_kernel(
    place_ref, query_ref, key_ref, value_ref, decay_ref, mine_ref, other_ref, sibling_ref, out_ref
):
    second = place_ref[CORE] == 1
    endings = join_parts(sibling_ref[HEADS_HERE * HEAD_DIM :, :], HEADS_HERE)
    decay = decay_ref[...]
    causal = lower_triangle()
    running_sum = running_sums(decay)
    later = jnp.where(causal, 0.0, 1.0).astype(jnp.float32)
    shape = (TOKENS, TOKENS)
    upper = lax.broadcasted_iota(jnp.int32, shape, 0) <= lax.broadcasted_iota(jnp.int32, shape, 1)
    upper = jnp.where(upper, 1.0, 0.0).astype(jnp.float32)
    running_row = dot(decay, upper, 0, 0, lax.Precision.HIGHEST)
    for head in range(HEADS_HERE):
        sums = running_sum[:, head : head + 1]
        spread = sums - running_row[head : head + 1, :]
        query = query_ref[:, columns(head)]
        value = value_ref[:, columns(head)]
        scores = dot(query, key_ref[:, columns(head)], 1, 1)
        decayed = jnp.where(causal, jnp.exp(jnp.where(causal, spread, 0.0)), 0.0) * scores
        total = dot(decayed.astype(jnp.bfloat16), value, 1, 0)
        query_scaled = (query.astype(jnp.float32) * jnp.exp(sums)).astype(jnp.bfloat16)
        half, place = head // HALF, head_rows(head % HALF)
        mine = mine_ref[place, :].astype(jnp.float32)
        other = other_ref[place, :].astype(jnp.float32)
        prior = jnp.where(place_ref[CORE] == half, mine, other)
        fade = jnp.exp(endings[head : head + 1, :])
        passed = fade * prior + sibling_ref[head_rows(head), :].astype(jnp.float32)
        prior = jnp.where(second, passed, prior)
        total += dot(query_scaled, prior.astype(jnp.bfloat16), 1, 0)
        mean = jnp.mean(total * total, axis=1, keepdims=True)
        out_ref[:, columns(head)] = (total * lax.rsqrt(mean + norm_eps)).astype(jnp.bfloat16)


def unpack_kernel(moved_ref, order_ref, out_ref):
    for device in range(BLOCKS):
        head, quarter = place_of(device)
        out_ref[rows(quarter), columns(head)] = moved_ref[device]


def exchange(value):
    return lax.all_to_all(value, "ctx", split_axis=0, concat_axis=0, tiled=True)


def swap(value, step):
    return lax.ppermute(value, "ctx", [(d, d ^ step) for d in range(BLOCKS)])


def shards(lin_query, lin_key, lin_value, log_decay, soft_query, soft_key, soft_value):
    half = jnp.bfloat16
    shape = jax.ShapeDtypeStruct
    index = lax.axis_index("ctx").astype(jnp.int32)
    core = index % 2
    place = jnp.stack([2 * (index // X_STEP % 2) + core, core])
    width = HEADS_HERE * HEAD_DIM
    (packed,) = call(
        pack_kernel,
        [shape((BLOCKS, 3 * PIECE, HEAD_DIM), half)],
        (soft_query, soft_key, soft_value),
        1000,
        [pltpu.HBM] * 3,
        scratch=(pltpu.VMEM((3, TOKENS, width), half), pltpu.SemaphoreType.DMA((3,))),
    )
    kv0 = exchange(packed)
    (states,) = call(
        states_kernel,
        [shape((width + 3 * HEADS_HERE, HEAD_DIM), half)],
        (lin_key, lin_value, log_decay),
        10**8,
    )
    sibling = swap(states, 1)
    on_core = [pltpu.SMEM] + [pltpu.VMEM] * 7
    (chip,) = call(
        chip_kernel,
        [shape((BLOCKS, SLICE + 8, HEAD_DIM), half)],
        (place, states, sibling),
        10**7,
        on_core[:3],
        scratch=(pltpu.VMEM((HALF, HEAD_DIM), jnp.float32),),
    )
    kv0, chip = lax.optimization_barrier((kv0, chip))
    half_blocks = BLOCKS // 2
    kv0a, kv0 = lax.optimization_barrier((kv0[:half_blocks, PIECE:], kv0))
    kv0b = kv0[half_blocks:, PIECE:]
    kv2a = swap(kv0a, X_STEP)
    kv1a, kv1b = swap(kv0a, 1), swap(kv0b, 1)
    chips = exchange(chip)

    dma = pltpu.SemaphoreType.DMA
    token_shape = shape((8, HEAD_DIM), jnp.float32)
    state_shapes = [
        shape((len(LATE) * TILE_ROWS, HEAD_DIM), jnp.float32),
        shape((len(LATE) * TILE_ROWS, 2 * HEAD_DIM), jnp.float32),
    ]
    in_hbm, in_vmem, in_smem = pltpu.HBM, pltpu.VMEM, pltpu.SMEM
    best_a, total_a, token = call(
        first_kernel,
        [*state_shapes, token_shape],
        (place, kv0, kv1a, kv1b),
        0,
        [in_smem, in_vmem, in_hbm, in_hbm],
        [in_hbm, in_hbm, in_vmem],
        [*attention_space(2, 2), *work_space(LATE, range(TILES), 2), dma((2,)), dma((2, 2))],
        limit=32,
    )
    token, kv2a, kv0b = lax.optimization_barrier((token, kv2a, kv0b))
    kv3a = swap(kv2a, 1)
    kv2b = swap(kv0b, X_STEP)
    best_b, total_b, first, token = call(
        second_kernel,
        [*state_shapes, shape((half_blocks, PIECE, HEAD_DIM), half), token_shape],
        (place, kv0, kv1a, kv2a, kv3a, token),
        0,
        [in_smem, in_vmem, in_hbm, in_hbm, in_vmem, in_vmem],
        [in_hbm, in_hbm, in_hbm, in_vmem],
        [
            *attention_space(2, 4),
            *work_space(LATE, EARLY, 2),
            *work_space(EARLY, EARLY, 4),
            final_space(half_blocks),
            dma((2,)),
            dma((2,)),
            dma,
        ],
        limit=40,
    )
    token, chips, kv2b = lax.optimization_barrier((token, chips, kv2b))
    kv3b = swap(kv2b, 1)
    (scanned,) = call(scan_kernel, [shape((BLOCKS, SLICE, HEAD_DIM), half)], (chips,), 10**6)
    prior = exchange(scanned).reshape(HALF * HEAD_DIM, HEAD_DIM)
    (attended,) = call(
        third_kernel,
        [shape((BLOCKS, PIECE, HEAD_DIM), half)],
        (place, kv0, kv2b, kv3b, best_a, total_a, best_b, total_b, first, token),
        0,
        [in_smem, in_vmem, *[in_hbm] * 7, in_vmem],
        [in_hbm],
        [
            *attention_space(2, 2),
            *work_space(LATE, LATE, 2),
            pltpu.VMEM((2, len(LATE) * TILE_ROWS, HEAD_DIM), jnp.float32),
            pltpu.VMEM((2, len(LATE) * TILE_ROWS, 2 * HEAD_DIM), jnp.float32),
            final_space(BLOCKS),
            dma((2,)),
            dma((5,)),
            dma((1 + len(LATE),)),
        ],
        limit=32,
    )
    returned = exchange(attended)
    other_prior = swap(prior, 1)
    whole_out = shape((TOKENS, width), half)
    (lin_out,) = call(
        lightning_kernel,
        [whole_out],
        (place, lin_query, lin_key, lin_value, log_decay, prior, other_prior, sibling),
        2 * 10**8,
        on_core[:8],
    )
    token, returned = lax.optimization_barrier((lin_out[0:8, 0:HEAD_DIM], returned))
    (soft_out,) = call(unpack_kernel, [whole_out], (returned, token), 1000)
    return (lin_out, soft_out)


def solution(mesh):
    spec = P("ctx", "head")
    return jax.shard_map(
        shards, mesh=mesh, in_specs=(spec,) * 7, out_specs=(spec, spec), check_vma=False
    )
```

```python
import functools
import math

import jax
import jax.numpy as jnp
from jax import lax
from jax.experimental import pallas as pl
from jax.experimental.pallas import tpu as pltpu
from jax.sharding import PartitionSpec as P

HEAD_DIM = 128
TOKENS = 128
HEADS_HERE = 16
BLOCKS = 64
PIECE = 32

norm_eps = 1e-06
masked_score = -1e30
exponent_scale = HEAD_DIM ** (-0.5) * math.log2(math.e)
X_STEP = 16
HALF = HEADS_HERE // 2
SLICE = HALF * HEAD_DIM // BLOCKS
QUARTER, CORE = range(2)
QUERY_TILE = 8
TILE_ROWS = QUERY_TILE * PIECE
LANES = TILE_ROWS // HEAD_DIM
TILES = BLOCKS // QUERY_TILE
HALF_TILES = TILES // 2
EARLY, LATE = range(HALF_TILES), range(HALF_TILES, TILES)


def place_of(device):
    x, z, core = device // 16, device // 2 % 8, device % 2
    return 2 * z + x // 2, 2 * (x % 2) + core


def columns(head):
    return slice(head * HEAD_DIM, (head + 1) * HEAD_DIM)


def rows(quarter):
    return slice(quarter * PIECE, (quarter + 1) * PIECE)


def whole(space=pltpu.VMEM):
    return pl.BlockSpec(memory_space=space)


def dot(left, right, left_dim, right_dim, precision=None):
    return lax.dot_general(
        left,
        right,
        (((left_dim,), (right_dim,)), ((), ())),
        precision=precision,
        preferred_element_type=jnp.float32,
    )


def call(kernel, out_shape, operands, flops, spaces=None, out_spaces=None, scratch=(), limit=16):
    out_shape = tuple(out_shape)
    bytes_moved = sum(math.prod(o.shape) * o.dtype.itemsize for o in (*operands, *out_shape))
    spaces = spaces or [pltpu.VMEM] * len(operands)
    out_spaces = out_spaces or [pltpu.VMEM] * len(out_shape)
    operands = [
        pltpu.with_memory_space_constraint(o, space) if space is pltpu.HBM else o
        for o, space in zip(operands, spaces)
    ]
    out_shape = [
        pltpu.HBM(o.shape, o.dtype) if space is pltpu.HBM else o
        for o, space in zip(out_shape, out_spaces)
    ]
    return pl.pallas_call(
        kernel,
        out_shape=out_shape,
        in_specs=[whole(space) for space in spaces],
        out_specs=[whole(space) for space in out_spaces],
        scratch_shapes=list(scratch),
        compiler_params=pltpu.CompilerParams(vmem_limit_bytes=limit << 20),
        cost_estimate=pl.CostEstimate(
            flops=flops, bytes_accessed=bytes_moved if flops else 0, transcendentals=0
        ),
    )(*operands)


def pack_kernel(query_ref, key_ref, value_ref, out_ref, held_ref, semaphores):
    sources = (query_ref, key_ref, value_ref)
    copies = [
        pltpu.make_async_copy(source, held_ref.at[which], semaphores.at[which])
        for which, source in enumerate(sources)
    ]
    for copy in copies:
        copy.start()
    for which, copy in enumerate(copies):
        copy.wait()
        for device in range(BLOCKS):
            head, quarter = place_of(device)
            out_ref[device, rows(which), :] = held_ref[which, rows(quarter), columns(head)]


def lower_triangle():
    shape = (TOKENS, TOKENS)
    return lax.broadcasted_iota(jnp.int32, shape, 0) >= lax.broadcasted_iota(jnp.int32, shape, 1)


def running_sums(decay):
    ones = jnp.where(lower_triangle(), 1.0, 0.0).astype(jnp.float32)
    return dot(ones, decay, 1, 0, lax.Precision.HIGHEST)


def split_parts(value):
    coarse = value.astype(jnp.bfloat16).astype(jnp.float32)
    middle = (value - coarse).astype(jnp.bfloat16).astype(jnp.float32)
    parts = (coarse, middle, value - coarse - middle)
    return jnp.concatenate([part.astype(jnp.bfloat16) for part in parts], axis=0)


def join_parts(parts, heads):
    wide = parts.astype(jnp.float32)
    return wide[0:heads] + wide[heads : 2 * heads] + wide[2 * heads : 3 * heads]


def head_rows(head):
    return slice(head * HEAD_DIM, (head + 1) * HEAD_DIM)


def states_kernel(key_ref, value_ref, decay_ref, out_ref):
    decay = decay_ref[...]
    running_sum = running_sums(decay)
    ones = jnp.ones((TOKENS, HEAD_DIM), jnp.float32)
    endings = dot(decay, ones, 0, 0, lax.Precision.HIGHEST)
    out_ref[HEADS_HERE * HEAD_DIM :, :] = split_parts(endings)
    for head in range(HEADS_HERE):
        sums = running_sum[:, head : head + 1]
        ending = running_sum[TOKENS - 1 : TOKENS, head : head + 1]
        key_wide = key_ref[:, columns(head)].astype(jnp.float32)
        key_scaled = (key_wide * jnp.exp(ending - sums)).astype(jnp.bfloat16)
        state = dot(key_scaled, value_ref[:, columns(head)], 0, 0)
        out_ref[head_rows(head), :] = state.astype(jnp.bfloat16)


def chip_kernel(place_ref, mine_ref, other_ref, out_ref, ending_ref):
    first = place_ref[CORE] == 0
    tail = slice(HEADS_HERE * HEAD_DIM, None)
    mine = join_parts(mine_ref[tail, :], HEADS_HERE)
    other = join_parts(other_ref[tail, :], HEADS_HERE)
    both = mine + other
    later = jnp.where(first, other, mine)
    ending_ref[...] = jnp.where(first, both[0:HALF], both[HALF:])
    part = lax.broadcasted_iota(jnp.int32, (8, HEAD_DIM), 0)
    for head in range(HALF):
        ending = ending_ref[head : head + 1, :]
        coarse = ending.astype(jnp.bfloat16).astype(jnp.float32)
        middle = (ending - coarse).astype(jnp.bfloat16).astype(jnp.float32)
        fine = ending - coarse - middle
        parts = jnp.where(part == 0, coarse, jnp.where(part == 1, middle, fine))
        for piece in range(HALF):
            out_ref[HALF * head + piece, SLICE:, :] = parts.astype(jnp.bfloat16)
    ending_ref[...] = jnp.where(first, later[0:HALF], later[HALF:])
    for head in range(HALF):
        place = place_ref[CORE] * (HALF * HEAD_DIM) + head * HEAD_DIM
        here = pl.ds(pl.multiple_of(place, HEAD_DIM), HEAD_DIM)
        mine = mine_ref[here, :].astype(jnp.float32)
        other = other_ref[here, :].astype(jnp.float32)
        fade = jnp.exp(ending_ref[head : head + 1, :])
        state = jnp.where(first, fade * mine + other, fade * other + mine)
        pieces = state.astype(jnp.bfloat16).reshape(HALF, SLICE, HEAD_DIM)
        out_ref[HALF * head : HALF * (head + 1), 0:SLICE, :] = pieces


def scan_kernel(moved_ref, out_ref):
    def step(chip, carries):
        following = []
        for core, carry in enumerate(carries):
            source = 2 * chip + core
            out_ref[source] = carry.astype(jnp.bfloat16)
            parts = moved_ref[source, SLICE:, :].astype(jnp.float32)
            ending = parts[0:1] + parts[1:2] + parts[2:3]
            state = moved_ref[source, 0:SLICE, :].astype(jnp.float32)
            following.append(jnp.exp(ending) * carry + state)
        return tuple(following)

    zero = jnp.zeros((SLICE, HEAD_DIM), jnp.float32)
    lax.fori_loop(0, BLOCKS // 2, step, (zero, zero), unroll=4)


def tile_pairs(queries, keys):
    return [(query, key) for query in queries for key in keys if key <= query]


def tile_blocks(index):
    return slice(index * QUERY_TILE, (index + 1) * QUERY_TILE)


class Attention:
    def __init__(self, queries, keys, slots, query_ref, part, bias_ref, best_ref, total_ref, score_ref):
        self.queries, self.keys, self.slots = queries, keys, slots
        self.query_ref, self.part, self.bias_ref = query_ref, part, bias_ref
        self.best_ref, self.total_ref, self.score_ref = best_ref, total_ref, score_ref
        self.pairs = tile_pairs(queries, keys)
        best_ref[...] = jnp.full(best_ref.shape, masked_score, jnp.float32)

    def here(self, query_tile):
        start = (query_tile - self.queries.start) * TILE_ROWS
        return slice(start, start + TILE_ROWS)

    def place(self, query_tile, key_tile, slot):
        return len(self.slots) * self.pairs.index((query_tile, key_tile)) + self.slots.index(slot)

    def find_best(self, query_tile, slots):
        here = self.here(query_tile)
        query = self.query_ref[tile_blocks(query_tile), rows(0), :].reshape(TILE_ROWS, HEAD_DIM)
        for key_tile in self.keys:
            if key_tile > query_tile or not slots:
                continue
            best = self.best_ref[here, :]
            for slot in slots:
                score = dot(query, self.part(slot, key_tile, 2), 1, 1)
                if key_tile == query_tile:
                    score += self.bias_ref[slot]
                self.score_ref[self.place(query_tile, key_tile, slot)] = score
                for lane in range(LANES):
                    best = jnp.maximum(best, score[:, columns(lane)])
            self.best_ref[here, :] = best

    def add_up(self, query_tile):
        here = self.here(query_tile)
        best = jnp.max(self.best_ref[here, :], axis=1, keepdims=True)
        self.best_ref[here, :] = jnp.broadcast_to(best, (TILE_ROWS, HEAD_DIM))
        self.total_ref[here, :] = jnp.zeros((TILE_ROWS, 2 * HEAD_DIM), jnp.float32)
        ones = jnp.ones((TILE_ROWS, HEAD_DIM), jnp.bfloat16)
        for key_tile in self.keys:
            if key_tile > query_tile:
                continue
            best_wide = jnp.concatenate([self.best_ref[here, :]] * LANES, axis=1)
            weights, values = [], []
            for slot in self.slots:
                score = self.score_ref[self.place(query_tile, key_tile, slot)]
                weight = jnp.exp2((score - best_wide) * exponent_scale)
                weights.append(weight.astype(jnp.bfloat16))
                values.append(jnp.concatenate([self.part(slot, key_tile, 1), ones], axis=1))
            self.total_ref[here, :] += dot(
                jnp.concatenate(weights, axis=1), jnp.concatenate(values, axis=0), 1, 0
            )


def load_part(array, place, from_end):
    wanted = rows(array.shape[1] // PIECE - from_end)
    return array[tile_blocks(place), wanted, :].reshape(TILE_ROWS, HEAD_DIM)


def fill_bias(place_ref, bias_ref, steps):
    mine = place_ref[QUARTER]

    def positions(shape, dim, quarter):
        row = lax.broadcasted_iota(jnp.int32, shape, dim)
        return (row // PIECE) * TOKENS + row % PIECE + quarter * PIECE

    queries = positions((TILE_ROWS, HEAD_DIM), 0, mine)
    queries = jnp.concatenate([queries] * LANES, axis=1)
    for slot, step in enumerate(steps):
        allowed = positions((1, TILE_ROWS), 1, mine ^ step) <= queries
        bias_ref[slot] = jnp.where(allowed, 0.0, masked_score)


def start_copies(sources, targets, semaphores):
    copies = [
        pltpu.make_async_copy(source, target, semaphores.at[number])
        for number, (source, target) in enumerate(zip(sources, targets))
    ]
    for copy in copies:
        copy.start()
    return copies


def ratio(total):
    outcome = (total[:, :HEAD_DIM] / total[:, HEAD_DIM:]).astype(jnp.bfloat16)
    return outcome.reshape(QUERY_TILE, PIECE, HEAD_DIM)


def first_kernel(
    place_ref, packed_ref, early_ref, late_ref, best_out, total_out, token_ref,
    bias_ref, best_ref, total_ref, score_ref, out_sems,
):
    fill_bias(place_ref, bias_ref, (0, 1))

    def part(slot, key_tile, from_end):
        if slot == 0:
            return load_part(packed_ref, key_tile, from_end)
        return load_part((early_ref, late_ref)[key_tile // HALF_TILES], key_tile % HALF_TILES, from_end)

    work = Attention(
        LATE, range(TILES), (0, 1), packed_ref, part, bias_ref, best_ref, total_ref, score_ref
    )
    outward, sent = [], 0
    for query_tile in LATE:
        work.find_best(query_tile, (0, 1))
        work.add_up(query_tile)
        if query_tile >= TILES - 2:
            done = work.here(query_tile).stop
            place = pl.ds(sent, done - sent)
            outward += start_copies(
                (best_ref.at[place, :], total_ref.at[place, :]),
                (best_out.at[place, :], total_out.at[place, :]),
                out_sems.at[query_tile - (TILES - 2)],
            )
            sent = done
    token_ref[...] = best_ref[0:8, :]
    for copy in outward:
        copy.wait()


def second_kernel(
    place_ref, packed_ref, sibling_ref, across_ref, diagonal_ref, order_ref,
    best_out, total_out, final_out, token_ref,
    kv_ref, bias_ref, best_ref, total_ref, score_ref, best2_ref, total2_ref, score2_ref, final_ref,
    kv_sems, out_sems, final_sem,
):
    copies = start_copies((across_ref,), (kv_ref,), kv_sems)
    fill_bias(place_ref, bias_ref, (0, 1, 2, 3))

    def part(slot, key_tile, from_end):
        if slot == 0:
            return load_part(packed_ref, key_tile, from_end)
        return load_part((sibling_ref, kv_ref, diagonal_ref)[slot - 1], key_tile, from_end)

    early = Attention(
        EARLY, EARLY, (0, 1, 2, 3), packed_ref, part, bias_ref, best2_ref, total2_ref, score2_ref
    )
    for query_tile in EARLY:
        early.find_best(query_tile, (0, 1))
    late = Attention(
        LATE, EARLY, (2, 3), packed_ref, part, bias_ref, best_ref, total_ref, score_ref
    )
    for copy in copies:
        copy.wait()
    for query_tile in LATE:
        late.find_best(query_tile, (2, 3))
        late.add_up(query_tile)
    outward = start_copies((best_ref, total_ref), (best_out, total_out), out_sems)
    for query_tile in EARLY:
        early.find_best(query_tile, (2, 3))
        early.add_up(query_tile)
        final_ref[tile_blocks(query_tile)] = ratio(total2_ref[early.here(query_tile), :])
    copy = pltpu.make_async_copy(final_ref, final_out, final_sem)
    copy.start()
    token_ref[...] = best2_ref[0:8, :]
    for other in outward:
        other.wait()
    copy.wait()


def third_kernel(
    place_ref, packed_ref, across_ref, diagonal_ref, best_a, total_a, best_b, total_b, final_in, order_ref,
    out_ref,
    kv_ref, bias_ref, best_ref, total_ref, score_ref, bests_ref, totals_ref, final_ref,
    kv_sems, state_sems, final_sems,
):
    copies = start_copies((across_ref,), (kv_ref,), kv_sems)
    half_blocks = BLOCKS // 2
    state = start_copies(
        (best_a, best_b, total_a, total_b, final_in),
        (bests_ref.at[0], bests_ref.at[1], totals_ref.at[0], totals_ref.at[1], final_ref.at[0:half_blocks]),
        state_sems,
    )
    fill_bias(place_ref, bias_ref, (2, 3))

    def part(slot, key_tile, from_end):
        return load_part((kv_ref, diagonal_ref)[slot], key_tile % HALF_TILES, from_end)

    for copy in copies:
        copy.wait()
    work = Attention(
        LATE, LATE, (0, 1), packed_ref, part, bias_ref, best_ref, total_ref, score_ref
    )
    for query_tile in LATE:
        work.find_best(query_tile, (0, 1))
        work.add_up(query_tile)
    for copy in state:
        copy.wait()
    outward = start_copies(
        (final_ref.at[0:half_blocks],), (out_ref.at[0:half_blocks],), final_sems
    )
    for query_tile in LATE:
        here = work.here(query_tile)
        bests = [best_ref[here, :], bests_ref[0, here, :], bests_ref[1, here, :]]
        totals = [total_ref[here, :], totals_ref[0, here, :], totals_ref[1, here, :]]
        best = functools.reduce(jnp.maximum, bests)
        joined = 0.0
        for one, total in zip(bests, totals):
            shrink = jnp.exp2((one - best) * exponent_scale)
            joined += jnp.concatenate([shrink, shrink], axis=1) * total
        blocks = tile_blocks(query_tile)
        final_ref[blocks] = ratio(joined)
        outward += start_copies(
            (final_ref.at[blocks],),
            (out_ref.at[blocks],),
            final_sems.at[1 + query_tile - LATE.start : 2 + query_tile - LATE.start],
        )
    for copy in outward:
        copy.wait()


def work_space(queries, keys, slots):
    rows_here = len(queries) * TILE_ROWS
    return [
        pltpu.VMEM((rows_here, HEAD_DIM), jnp.float32),
        pltpu.VMEM((rows_here, 2 * HEAD_DIM), jnp.float32),
        pltpu.VMEM((slots * len(tile_pairs(queries, keys)), TILE_ROWS, TILE_ROWS), jnp.float32),
    ]


def final_space(blocks):
    return pltpu.VMEM((blocks, PIECE, HEAD_DIM), jnp.bfloat16)


def half_space():
    return pltpu.VMEM((BLOCKS // 2, 2 * PIECE, HEAD_DIM), jnp.bfloat16)


def bias_space(slots):
    return pltpu.VMEM((slots, TILE_ROWS, TILE_ROWS), jnp.float32)


def lightning_kernel(
    place_ref, query_ref, key_ref, value_ref, decay_ref, mine_ref, other_ref, sibling_ref, out_ref
):
    second = place_ref[CORE] == 1
    endings = join_parts(sibling_ref[HEADS_HERE * HEAD_DIM :, :], HEADS_HERE)
    decay = decay_ref[...]
    causal = lower_triangle()
    running_sum = running_sums(decay)
    later = jnp.where(causal, 0.0, 1.0).astype(jnp.float32)
    shape = (TOKENS, TOKENS)
    upper = lax.broadcasted_iota(jnp.int32, shape, 0) <= lax.broadcasted_iota(jnp.int32, shape, 1)
    upper = jnp.where(upper, 1.0, 0.0).astype(jnp.float32)
    running_row = dot(decay, upper, 0, 0, lax.Precision.HIGHEST)
    for head in range(HEADS_HERE):
        sums = running_sum[:, head : head + 1]
        spread = sums - running_row[head : head + 1, :]
        query = query_ref[:, columns(head)]
        value = value_ref[:, columns(head)]
        scores = dot(query, key_ref[:, columns(head)], 1, 1)
        decayed = jnp.where(causal, jnp.exp(jnp.where(causal, spread, 0.0)), 0.0) * scores
        total = dot(decayed.astype(jnp.bfloat16), value, 1, 0)
        query_scaled = (query.astype(jnp.float32) * jnp.exp(sums)).astype(jnp.bfloat16)
        half, place = head // HALF, head_rows(head % HALF)
        mine = mine_ref[place, :].astype(jnp.float32)
        other = other_ref[place, :].astype(jnp.float32)
        prior = jnp.where(place_ref[CORE] == half, mine, other)
        fade = jnp.exp(endings[head : head + 1, :])
        passed = fade * prior + sibling_ref[head_rows(head), :].astype(jnp.float32)
        prior = jnp.where(second, passed, prior)
        total += dot(query_scaled, prior.astype(jnp.bfloat16), 1, 0)
        mean = jnp.mean(total * total, axis=1, keepdims=True)
        out_ref[:, columns(head)] = (total * lax.rsqrt(mean + norm_eps)).astype(jnp.bfloat16)


def unpack_kernel(moved_ref, order_ref, out_ref):
    for device in range(BLOCKS):
        head, quarter = place_of(device)
        out_ref[rows(quarter), columns(head)] = moved_ref[device]


def exchange(value):
    return lax.all_to_all(value, "ctx", split_axis=0, concat_axis=0, tiled=True)


def swap(value, step):
    return lax.ppermute(value, "ctx", [(d, d ^ step) for d in range(BLOCKS)])


def shards(lin_query, lin_key, lin_value, log_decay, soft_query, soft_key, soft_value):
    half = jnp.bfloat16
    shape = jax.ShapeDtypeStruct
    index = lax.axis_index("ctx").astype(jnp.int32)
    core = index % 2
    place = jnp.stack([2 * (index // X_STEP % 2) + core, core])
    width = HEADS_HERE * HEAD_DIM
    (packed,) = call(
        pack_kernel,
        [shape((BLOCKS, 3 * PIECE, HEAD_DIM), half)],
        (soft_query, soft_key, soft_value),
        1000,
        [pltpu.HBM] * 3,
        scratch=(pltpu.VMEM((3, TOKENS, width), half), pltpu.SemaphoreType.DMA((3,))),
    )
    kv0 = exchange(packed)
    (states,) = call(
        states_kernel,
        [shape((width + 3 * HEADS_HERE, HEAD_DIM), half)],
        (lin_key, lin_value, log_decay),
        10**8,
    )
    sibling = swap(states, 1)
    on_core = [pltpu.SMEM] + [pltpu.VMEM] * 7
    (chip,) = call(
        chip_kernel,
        [shape((BLOCKS, SLICE + 8, HEAD_DIM), half)],
        (place, states, sibling),
        10**7,
        on_core[:3],
        scratch=(pltpu.VMEM((HALF, HEAD_DIM), jnp.float32),),
    )
    kv0, chip = lax.optimization_barrier((kv0, chip))
    half_blocks = BLOCKS // 2
    kv0a, kv0 = lax.optimization_barrier((kv0[:half_blocks, PIECE:], kv0))
    kv0b = kv0[half_blocks:, PIECE:]
    kv2a = swap(kv0a, X_STEP)
    kv1a, kv1b = swap(kv0a, 1), swap(kv0b, 1)
    chips = exchange(chip)

    dma = pltpu.SemaphoreType.DMA
    token_shape = shape((8, HEAD_DIM), jnp.float32)
    state_shapes = [
        shape((len(LATE) * TILE_ROWS, HEAD_DIM), jnp.float32),
        shape((len(LATE) * TILE_ROWS, 2 * HEAD_DIM), jnp.float32),
    ]
    in_hbm, in_vmem, in_smem = pltpu.HBM, pltpu.VMEM, pltpu.SMEM
    best_a, total_a, token = call(
        first_kernel,
        [*state_shapes, token_shape],
        (place, kv0, kv1a, kv1b),
        0,
        [in_smem, in_vmem, in_vmem, in_vmem],
        [in_hbm, in_hbm, in_vmem],
        [bias_space(2), *work_space(LATE, range(TILES), 2), dma((2, 2))],
        limit=32,
    )
    token, kv2a, kv0b = lax.optimization_barrier((token, kv2a, kv0b))
    kv3a = swap(kv2a, 1)
    kv2b = swap(kv0b, X_STEP)
    best_b, total_b, first, token = call(
        second_kernel,
        [*state_shapes, shape((half_blocks, PIECE, HEAD_DIM), half), token_shape],
        (place, kv0, kv1a, kv2a, kv3a, token),
        0,
        [in_smem, in_vmem, in_vmem, in_hbm, in_vmem, in_vmem],
        [in_hbm, in_hbm, in_hbm, in_vmem],
        [
            half_space(),
            bias_space(4),
            *work_space(LATE, EARLY, 2),
            *work_space(EARLY, EARLY, 4),
            final_space(half_blocks),
            dma((1,)),
            dma((2,)),
            dma,
        ],
        limit=40,
    )
    (scanned,) = call(scan_kernel, [shape((BLOCKS, SLICE, HEAD_DIM), half)], (chips,), 10**6)
    prior = exchange(scanned)
    prior, kv2b, token = lax.optimization_barrier((prior, kv2b, token))
    prior = prior.reshape(HALF * HEAD_DIM, HEAD_DIM)
    kv3b = swap(kv2b, 1)
    (attended,) = call(
        third_kernel,
        [shape((BLOCKS, PIECE, HEAD_DIM), half)],
        (place, kv0, kv2b, kv3b, best_a, total_a, best_b, total_b, first, token),
        0,
        [in_smem, in_vmem, in_hbm, in_vmem, *[in_hbm] * 5, in_vmem],
        [in_hbm],
        [
            half_space(),
            bias_space(2),
            *work_space(LATE, LATE, 2),
            pltpu.VMEM((2, len(LATE) * TILE_ROWS, HEAD_DIM), jnp.float32),
            pltpu.VMEM((2, len(LATE) * TILE_ROWS, 2 * HEAD_DIM), jnp.float32),
            final_space(BLOCKS),
            dma((1,)),
            dma((5,)),
            dma((1 + len(LATE),)),
        ],
        limit=32,
    )
    returned = exchange(attended)
    other_prior = swap(prior, 1)
    whole_out = shape((TOKENS, width), half)
    (lin_out,) = call(
        lightning_kernel,
        [whole_out],
        (place, lin_query, lin_key, lin_value, log_decay, prior, other_prior, sibling),
        2 * 10**8,
        on_core[:8],
    )
    token, returned = lax.optimization_barrier((lin_out[0:8, 0:HEAD_DIM], returned))
    (soft_out,) = call(unpack_kernel, [whole_out], (returned, token), 1000)
    return (lin_out, soft_out)


def solution(mesh):
    spec = P("ctx", "head")
    return jax.shard_map(
        shards, mesh=mesh, in_specs=(spec,) * 7, out_specs=(spec, spec), check_vma=False
    )
```

```python
import functools
import math

import jax
import jax.numpy as jnp
from jax import lax
from jax.experimental import pallas as pl
from jax.experimental.pallas import tpu as pltpu
from jax.sharding import PartitionSpec as P

HEAD_DIM = 128
TOKENS = 128
HEADS_HERE = 16
BLOCKS = 64
PIECE = 32

norm_eps = 1e-06
masked_score = -1e30
exponent_scale = HEAD_DIM ** (-0.5) * math.log2(math.e)
X_STEP = 16
HALF = HEADS_HERE // 2
SLICE = HALF * HEAD_DIM // BLOCKS
QUARTER, CORE = range(2)
QUERY_TILE = 8
TILE_ROWS = QUERY_TILE * PIECE
LANES = TILE_ROWS // HEAD_DIM
TILES = BLOCKS // QUERY_TILE
HALF_TILES = TILES // 2
EARLY, LATE = range(HALF_TILES), range(HALF_TILES, TILES)


def place_of(device):
    x, z, core = device // 16, device // 2 % 8, device % 2
    return 2 * z + x // 2, 2 * (x % 2) + core


def columns(head):
    return slice(head * HEAD_DIM, (head + 1) * HEAD_DIM)


def rows(quarter):
    return slice(quarter * PIECE, (quarter + 1) * PIECE)


def whole(space=pltpu.VMEM):
    return pl.BlockSpec(memory_space=space)


def dot(left, right, left_dim, right_dim, precision=None):
    return lax.dot_general(
        left,
        right,
        (((left_dim,), (right_dim,)), ((), ())),
        precision=precision,
        preferred_element_type=jnp.float32,
    )


def call(kernel, out_shape, operands, flops, spaces=None, out_spaces=None, scratch=(), limit=16):
    out_shape = tuple(out_shape)
    bytes_moved = sum(math.prod(o.shape) * o.dtype.itemsize for o in (*operands, *out_shape))
    spaces = spaces or [pltpu.VMEM] * len(operands)
    out_spaces = out_spaces or [pltpu.VMEM] * len(out_shape)
    operands = [
        pltpu.with_memory_space_constraint(o, space) if space is pltpu.HBM else o
        for o, space in zip(operands, spaces)
    ]
    out_shape = [
        pltpu.HBM(o.shape, o.dtype) if space is pltpu.HBM else o
        for o, space in zip(out_shape, out_spaces)
    ]
    return pl.pallas_call(
        kernel,
        out_shape=out_shape,
        in_specs=[whole(space) for space in spaces],
        out_specs=[whole(space) for space in out_spaces],
        scratch_shapes=list(scratch),
        compiler_params=pltpu.CompilerParams(vmem_limit_bytes=limit << 20),
        cost_estimate=pl.CostEstimate(
            flops=flops, bytes_accessed=bytes_moved if flops else 0, transcendentals=0
        ),
    )(*operands)


def pack_kernel(query_ref, key_ref, value_ref, out_ref, held_ref, semaphores):
    sources = (query_ref, key_ref, value_ref)
    copies = [
        pltpu.make_async_copy(source, held_ref.at[which], semaphores.at[which])
        for which, source in enumerate(sources)
    ]
    for copy in copies:
        copy.start()
    for which, copy in enumerate(copies):
        copy.wait()
        for device in range(BLOCKS):
            head, quarter = place_of(device)
            out_ref[device, rows(which), :] = held_ref[which, rows(quarter), columns(head)]


def lower_triangle():
    shape = (TOKENS, TOKENS)
    return lax.broadcasted_iota(jnp.int32, shape, 0) >= lax.broadcasted_iota(jnp.int32, shape, 1)


def running_sums(decay):
    ones = jnp.where(lower_triangle(), 1.0, 0.0).astype(jnp.float32)
    return dot(ones, decay, 1, 0, lax.Precision.HIGHEST)


def split_parts(value):
    coarse = value.astype(jnp.bfloat16).astype(jnp.float32)
    middle = (value - coarse).astype(jnp.bfloat16).astype(jnp.float32)
    parts = (coarse, middle, value - coarse - middle)
    return jnp.concatenate([part.astype(jnp.bfloat16) for part in parts], axis=0)


def join_parts(parts, heads):
    wide = parts.astype(jnp.float32)
    return wide[0:heads] + wide[heads : 2 * heads] + wide[2 * heads : 3 * heads]


def head_rows(head):
    return slice(head * HEAD_DIM, (head + 1) * HEAD_DIM)


def states_kernel(key_ref, value_ref, decay_ref, out_ref):
    decay = decay_ref[...]
    running_sum = running_sums(decay)
    ones = jnp.ones((TOKENS, HEAD_DIM), jnp.float32)
    endings = dot(decay, ones, 0, 0, lax.Precision.HIGHEST)
    out_ref[HEADS_HERE * HEAD_DIM :, :] = split_parts(endings)
    for head in range(HEADS_HERE):
        sums = running_sum[:, head : head + 1]
        ending = running_sum[TOKENS - 1 : TOKENS, head : head + 1]
        key_wide = key_ref[:, columns(head)].astype(jnp.float32)
        key_scaled = (key_wide * jnp.exp(ending - sums)).astype(jnp.bfloat16)
        state = dot(key_scaled, value_ref[:, columns(head)], 0, 0)
        out_ref[head_rows(head), :] = state.astype(jnp.bfloat16)


def chip_kernel(place_ref, mine_ref, other_ref, out_ref, ending_ref):
    first = place_ref[CORE] == 0
    tail = slice(HEADS_HERE * HEAD_DIM, None)
    mine = join_parts(mine_ref[tail, :], HEADS_HERE)
    other = join_parts(other_ref[tail, :], HEADS_HERE)
    both = mine + other
    later = jnp.where(first, other, mine)
    ending_ref[...] = jnp.where(first, both[0:HALF], both[HALF:])
    part = lax.broadcasted_iota(jnp.int32, (8, HEAD_DIM), 0)
    for head in range(HALF):
        ending = ending_ref[head : head + 1, :]
        coarse = ending.astype(jnp.bfloat16).astype(jnp.float32)
        middle = (ending - coarse).astype(jnp.bfloat16).astype(jnp.float32)
        fine = ending - coarse - middle
        parts = jnp.where(part == 0, coarse, jnp.where(part == 1, middle, fine))
        for piece in range(HALF):
            out_ref[HALF * head + piece, SLICE:, :] = parts.astype(jnp.bfloat16)
    ending_ref[...] = jnp.where(first, later[0:HALF], later[HALF:])
    for head in range(HALF):
        place = place_ref[CORE] * (HALF * HEAD_DIM) + head * HEAD_DIM
        here = pl.ds(pl.multiple_of(place, HEAD_DIM), HEAD_DIM)
        mine = mine_ref[here, :].astype(jnp.float32)
        other = other_ref[here, :].astype(jnp.float32)
        fade = jnp.exp(ending_ref[head : head + 1, :])
        state = jnp.where(first, fade * mine + other, fade * other + mine)
        pieces = state.astype(jnp.bfloat16).reshape(HALF, SLICE, HEAD_DIM)
        out_ref[HALF * head : HALF * (head + 1), 0:SLICE, :] = pieces


def scan_kernel(moved_ref, out_ref):
    def step(chip, carries):
        following = []
        for core, carry in enumerate(carries):
            source = 2 * chip + core
            out_ref[source] = carry.astype(jnp.bfloat16)
            parts = moved_ref[source, SLICE:, :].astype(jnp.float32)
            ending = parts[0:1] + parts[1:2] + parts[2:3]
            state = moved_ref[source, 0:SLICE, :].astype(jnp.float32)
            following.append(jnp.exp(ending) * carry + state)
        return tuple(following)

    zero = jnp.zeros((SLICE, HEAD_DIM), jnp.float32)
    lax.fori_loop(0, BLOCKS // 2, step, (zero, zero), unroll=4)


def tile_pairs(queries, keys):
    return [(query, key) for query in queries for key in keys if key <= query]


def tile_blocks(index):
    return slice(index * QUERY_TILE, (index + 1) * QUERY_TILE)


class Attention:
    def __init__(self, queries, keys, slots, query_ref, part, bias_ref, best_ref, total_ref, score_ref):
        self.queries, self.keys, self.slots = queries, keys, slots
        self.query_ref, self.part, self.bias_ref = query_ref, part, bias_ref
        self.best_ref, self.total_ref, self.score_ref = best_ref, total_ref, score_ref
        self.pairs = tile_pairs(queries, keys)
        best_ref[...] = jnp.full(best_ref.shape, masked_score, jnp.float32)

    def here(self, query_tile):
        start = (query_tile - self.queries.start) * TILE_ROWS
        return slice(start, start + TILE_ROWS)

    def place(self, query_tile, key_tile, slot):
        return len(self.slots) * self.pairs.index((query_tile, key_tile)) + self.slots.index(slot)

    def find_best(self, query_tile, slots):
        here = self.here(query_tile)
        query = self.query_ref[tile_blocks(query_tile), rows(0), :].reshape(TILE_ROWS, HEAD_DIM)
        for key_tile in self.keys:
            if key_tile > query_tile or not slots:
                continue
            best = self.best_ref[here, :]
            for slot in slots:
                score = dot(query, self.part(slot, key_tile, 2), 1, 1)
                if key_tile == query_tile:
                    score += self.bias_ref[slot]
                self.score_ref[self.place(query_tile, key_tile, slot)] = score
                for lane in range(LANES):
                    best = jnp.maximum(best, score[:, columns(lane)])
            self.best_ref[here, :] = best

    def add_up(self, query_tile):
        here = self.here(query_tile)
        best = jnp.max(self.best_ref[here, :], axis=1, keepdims=True)
        self.best_ref[here, :] = jnp.broadcast_to(best, (TILE_ROWS, HEAD_DIM))
        self.total_ref[here, :] = jnp.zeros((TILE_ROWS, 2 * HEAD_DIM), jnp.float32)
        ones = jnp.ones((TILE_ROWS, HEAD_DIM), jnp.bfloat16)
        for key_tile in self.keys:
            if key_tile > query_tile:
                continue
            best_wide = jnp.concatenate([self.best_ref[here, :]] * LANES, axis=1)
            weights, values = [], []
            for slot in self.slots:
                score = self.score_ref[self.place(query_tile, key_tile, slot)]
                weight = jnp.exp2((score - best_wide) * exponent_scale)
                weights.append(weight.astype(jnp.bfloat16))
                values.append(jnp.concatenate([self.part(slot, key_tile, 1), ones], axis=1))
            self.total_ref[here, :] += dot(
                jnp.concatenate(weights, axis=1), jnp.concatenate(values, axis=0), 1, 0
            )


def load_part(array, place, from_end):
    wanted = rows(array.shape[1] // PIECE - from_end)
    return array[tile_blocks(place), wanted, :].reshape(TILE_ROWS, HEAD_DIM)


def fill_bias(place_ref, bias_ref, steps):
    mine = place_ref[QUARTER]

    def positions(shape, dim, quarter):
        row = lax.broadcasted_iota(jnp.int32, shape, dim)
        return (row // PIECE) * TOKENS + row % PIECE + quarter * PIECE

    queries = positions((TILE_ROWS, HEAD_DIM), 0, mine)
    queries = jnp.concatenate([queries] * LANES, axis=1)
    for slot, step in enumerate(steps):
        allowed = positions((1, TILE_ROWS), 1, mine ^ step) <= queries
        bias_ref[slot] = jnp.where(allowed, 0.0, masked_score)


def start_copies(sources, targets, semaphores):
    copies = [
        pltpu.make_async_copy(source, target, semaphores.at[number])
        for number, (source, target) in enumerate(zip(sources, targets))
    ]
    for copy in copies:
        copy.start()
    return copies


def ratio(total):
    outcome = (total[:, :HEAD_DIM] / total[:, HEAD_DIM:]).astype(jnp.bfloat16)
    return outcome.reshape(QUERY_TILE, PIECE, HEAD_DIM)


def first_kernel(
    place_ref, packed_ref, early_ref, late_ref, best_out, total_out, token_ref,
    kv_ref, bias_ref, best_ref, total_ref, score_ref, kv_sems, out_sems,
):
    copies = start_copies((early_ref, late_ref), (kv_ref.at[0], kv_ref.at[1]), kv_sems)
    fill_bias(place_ref, bias_ref, (0, 1))

    def part(slot, key_tile, from_end):
        if slot == 0:
            return load_part(packed_ref, key_tile, from_end)
        return load_part(kv_ref.at[key_tile // HALF_TILES], key_tile % HALF_TILES, from_end)

    work = Attention(
        LATE, range(TILES), (0, 1), packed_ref, part, bias_ref, best_ref, total_ref, score_ref
    )
    for query_tile in LATE:
        work.find_best(query_tile, (0,))
    for copy in copies:
        copy.wait()
    outward, sent = [], 0
    for query_tile in LATE:
        work.find_best(query_tile, (1,))
        work.add_up(query_tile)
        if query_tile >= TILES - 2:
            done = work.here(query_tile).stop
            place = pl.ds(sent, done - sent)
            outward += start_copies(
                (best_ref.at[place, :], total_ref.at[place, :]),
                (best_out.at[place, :], total_out.at[place, :]),
                out_sems.at[query_tile - (TILES - 2)],
            )
            sent = done
    token_ref[...] = best_ref[0:8, :]
    for copy in outward:
        copy.wait()


def second_kernel(
    place_ref, packed_ref, sibling_ref, across_ref, diagonal_ref, order_ref,
    best_out, total_out, final_out, token_ref,
    kv_ref, bias_ref, best_ref, total_ref, score_ref, best2_ref, total2_ref, score2_ref, final_ref,
    kv_sems, out_sems, final_sem,
):
    copies = start_copies((across_ref, sibling_ref), (kv_ref.at[1], kv_ref.at[0]), kv_sems)
    fill_bias(place_ref, bias_ref, (0, 1, 2, 3))

    def part(slot, key_tile, from_end):
        if slot == 0:
            return load_part(packed_ref, key_tile, from_end)
        return load_part(diagonal_ref if slot == 3 else kv_ref.at[slot - 1], key_tile, from_end)

    early = Attention(
        EARLY, EARLY, (0, 1, 2, 3), packed_ref, part, bias_ref, best2_ref, total2_ref, score2_ref
    )
    for query_tile in EARLY:
        early.find_best(query_tile, (0,))
    late = Attention(
        LATE, EARLY, (2, 3), packed_ref, part, bias_ref, best_ref, total_ref, score_ref
    )
    for copy in copies:
        copy.wait()
    for query_tile in LATE:
        late.find_best(query_tile, (2, 3))
        late.add_up(query_tile)
    outward = start_copies((best_ref, total_ref), (best_out, total_out), out_sems)
    for query_tile in EARLY:
        early.find_best(query_tile, (1, 2, 3))
        early.add_up(query_tile)
        final_ref[tile_blocks(query_tile)] = ratio(total2_ref[early.here(query_tile), :])
    copy = pltpu.make_async_copy(final_ref, final_out, final_sem)
    copy.start()
    token_ref[...] = best2_ref[0:8, :]
    for other in outward:
        other.wait()
    copy.wait()


def third_kernel(
    place_ref, packed_ref, across1_ref, across2_ref, diagonal1_ref, diagonal2_ref, best_a, total_a, best_b, total_b,
    final_in, order_ref, out_ref,
    kv_ref, bias_ref, best_ref, total_ref, score_ref, bests_ref, totals_ref, final_ref,
    kv_sems, state_sems, final_sems,
):
    half_blocks = BLOCKS // 2
    middle = half_blocks // 2
    copies = start_copies(
        (across1_ref, across2_ref), (kv_ref.at[0:middle], kv_ref.at[middle:half_blocks]), kv_sems
    )
    state = start_copies(
        (best_a, best_b, total_a, total_b, final_in),
        (bests_ref.at[0], bests_ref.at[1], totals_ref.at[0], totals_ref.at[1], final_ref.at[0:half_blocks]),
        state_sems,
    )
    fill_bias(place_ref, bias_ref, (2, 3))

    def part(slot, key_tile, from_end):
        place = key_tile % HALF_TILES
        if slot == 0:
            return load_part(kv_ref, place, from_end)
        diagonal = (diagonal1_ref, diagonal2_ref)[place // (HALF_TILES // 2)]
        return load_part(diagonal, place % (HALF_TILES // 2), from_end)

    for copy in copies:
        copy.wait()
    work = Attention(
        LATE, LATE, (0, 1), packed_ref, part, bias_ref, best_ref, total_ref, score_ref
    )
    for query_tile in LATE:
        work.find_best(query_tile, (0, 1))
        work.add_up(query_tile)
    for copy in state:
        copy.wait()
    outward = start_copies(
        (final_ref.at[0:half_blocks],), (out_ref.at[0:half_blocks],), final_sems
    )
    for query_tile in LATE:
        here = work.here(query_tile)
        bests = [best_ref[here, :], bests_ref[0, here, :], bests_ref[1, here, :]]
        totals = [total_ref[here, :], totals_ref[0, here, :], totals_ref[1, here, :]]
        best = functools.reduce(jnp.maximum, bests)
        joined = 0.0
        for one, total in zip(bests, totals):
            shrink = jnp.exp2((one - best) * exponent_scale)
            joined += jnp.concatenate([shrink, shrink], axis=1) * total
        blocks = tile_blocks(query_tile)
        final_ref[blocks] = ratio(joined)
        outward += start_copies(
            (final_ref.at[blocks],),
            (out_ref.at[blocks],),
            final_sems.at[1 + query_tile - LATE.start : 2 + query_tile - LATE.start],
        )
    for copy in outward:
        copy.wait()


def work_space(queries, keys, slots):
    rows_here = len(queries) * TILE_ROWS
    return [
        pltpu.VMEM((rows_here, HEAD_DIM), jnp.float32),
        pltpu.VMEM((rows_here, 2 * HEAD_DIM), jnp.float32),
        pltpu.VMEM((slots * len(tile_pairs(queries, keys)), TILE_ROWS, TILE_ROWS), jnp.float32),
    ]


def final_space(blocks):
    return pltpu.VMEM((blocks, PIECE, HEAD_DIM), jnp.bfloat16)


def attention_space(segments, slots):
    return [
        pltpu.VMEM((segments, BLOCKS // 2, 2 * PIECE, HEAD_DIM), jnp.bfloat16),
        pltpu.VMEM((slots, TILE_ROWS, TILE_ROWS), jnp.float32),
    ]


def lightning_kernel(
    place_ref, query_ref, key_ref, value_ref, decay_ref, mine_ref, other_ref, sibling_ref, out_ref
):
    second = place_ref[CORE] == 1
    endings = join_parts(sibling_ref[HEADS_HERE * HEAD_DIM :, :], HEADS_HERE)
    decay = decay_ref[...]
    causal = lower_triangle()
    running_sum = running_sums(decay)
    later = jnp.where(causal, 0.0, 1.0).astype(jnp.float32)
    shape = (TOKENS, TOKENS)
    upper = lax.broadcasted_iota(jnp.int32, shape, 0) <= lax.broadcasted_iota(jnp.int32, shape, 1)
    upper = jnp.where(upper, 1.0, 0.0).astype(jnp.float32)
    running_row = dot(decay, upper, 0, 0, lax.Precision.HIGHEST)
    for head in range(HEADS_HERE):
        sums = running_sum[:, head : head + 1]
        spread = sums - running_row[head : head + 1, :]
        query = query_ref[:, columns(head)]
        value = value_ref[:, columns(head)]
        scores = dot(query, key_ref[:, columns(head)], 1, 1)
        decayed = jnp.where(causal, jnp.exp(jnp.where(causal, spread, 0.0)), 0.0) * scores
        total = dot(decayed.astype(jnp.bfloat16), value, 1, 0)
        query_scaled = (query.astype(jnp.float32) * jnp.exp(sums)).astype(jnp.bfloat16)
        half, place = head // HALF, head_rows(head % HALF)
        mine = mine_ref[place, :].astype(jnp.float32)
        other = other_ref[place, :].astype(jnp.float32)
        prior = jnp.where(place_ref[CORE] == half, mine, other)
        fade = jnp.exp(endings[head : head + 1, :])
        passed = fade * prior + sibling_ref[head_rows(head), :].astype(jnp.float32)
        prior = jnp.where(second, passed, prior)
        total += dot(query_scaled, prior.astype(jnp.bfloat16), 1, 0)
        mean = jnp.mean(total * total, axis=1, keepdims=True)
        out_ref[:, columns(head)] = (total * lax.rsqrt(mean + norm_eps)).astype(jnp.bfloat16)


def unpack_kernel(moved_ref, order_ref, out_ref):
    for device in range(BLOCKS):
        head, quarter = place_of(device)
        out_ref[rows(quarter), columns(head)] = moved_ref[device]


def exchange(value):
    return lax.all_to_all(value, "ctx", split_axis=0, concat_axis=0, tiled=True)


def swap(value, step):
    return lax.ppermute(value, "ctx", [(d, d ^ step) for d in range(BLOCKS)])


def shards(lin_query, lin_key, lin_value, log_decay, soft_query, soft_key, soft_value):
    half = jnp.bfloat16
    shape = jax.ShapeDtypeStruct
    index = lax.axis_index("ctx").astype(jnp.int32)
    core = index % 2
    place = jnp.stack([2 * (index // X_STEP % 2) + core, core])
    width = HEADS_HERE * HEAD_DIM
    (packed,) = call(
        pack_kernel,
        [shape((BLOCKS, 3 * PIECE, HEAD_DIM), half)],
        (soft_query, soft_key, soft_value),
        1000,
        [pltpu.HBM] * 3,
        scratch=(pltpu.VMEM((3, TOKENS, width), half), pltpu.SemaphoreType.DMA((3,))),
    )
    kv0 = exchange(packed)
    (states,) = call(
        states_kernel,
        [shape((width + 3 * HEADS_HERE, HEAD_DIM), half)],
        (lin_key, lin_value, log_decay),
        10**8,
    )
    sibling = swap(states, 1)
    on_core = [pltpu.SMEM] + [pltpu.VMEM] * 7
    (chip,) = call(
        chip_kernel,
        [shape((BLOCKS, SLICE + 8, HEAD_DIM), half)],
        (place, states, sibling),
        10**7,
        on_core[:3],
        scratch=(pltpu.VMEM((HALF, HEAD_DIM), jnp.float32),),
    )
    kv0, chip = lax.optimization_barrier((kv0, chip))
    half_blocks = BLOCKS // 2
    kv0a, kv0 = lax.optimization_barrier((kv0[:half_blocks, PIECE:], kv0))
    middle = half_blocks + half_blocks // 2
    kv0b = kv0[half_blocks:, PIECE:]
    kv0c, kv0d = kv0[half_blocks:middle, PIECE:], kv0[middle:, PIECE:]
    kv2a = swap(kv0a, X_STEP)
    kv1a, kv1b = swap(kv0a, 1), swap(kv0b, 1)
    chips = exchange(chip)

    dma = pltpu.SemaphoreType.DMA
    token_shape = shape((8, HEAD_DIM), jnp.float32)
    state_shapes = [
        shape((len(LATE) * TILE_ROWS, HEAD_DIM), jnp.float32),
        shape((len(LATE) * TILE_ROWS, 2 * HEAD_DIM), jnp.float32),
    ]
    in_hbm, in_vmem, in_smem = pltpu.HBM, pltpu.VMEM, pltpu.SMEM
    best_a, total_a, token = call(
        first_kernel,
        [*state_shapes, token_shape],
        (place, kv0, kv1a, kv1b),
        0,
        [in_smem, in_vmem, in_hbm, in_hbm],
        [in_hbm, in_hbm, in_vmem],
        [*attention_space(2, 2), *work_space(LATE, range(TILES), 2), dma((2,)), dma((2, 2))],
        limit=32,
    )
    token, kv2a, kv0c, kv0d = lax.optimization_barrier((token, kv2a, kv0c, kv0d))
    kv3a = swap(kv2a, 1)
    kv2b = swap(kv0c, X_STEP), swap(kv0d, X_STEP)
    best_b, total_b, first, token = call(
        second_kernel,
        [*state_shapes, shape((half_blocks, PIECE, HEAD_DIM), half), token_shape],
        (place, kv0, kv1a, kv2a, kv3a, token),
        0,
        [in_smem, in_vmem, in_hbm, in_hbm, in_vmem, in_vmem],
        [in_hbm, in_hbm, in_hbm, in_vmem],
        [
            *attention_space(2, 4),
            *work_space(LATE, EARLY, 2),
            *work_space(EARLY, EARLY, 4),
            final_space(half_blocks),
            dma((2,)),
            dma((2,)),
            dma,
        ],
        limit=40,
    )
    token, chips = lax.optimization_barrier((token, chips))
    token, *kv2b = lax.optimization_barrier((token, *kv2b))
    kv3b = [swap(part, 1) for part in kv2b]
    (scanned,) = call(scan_kernel, [shape((BLOCKS, SLICE, HEAD_DIM), half)], (chips,), 10**6)
    prior = exchange(scanned).reshape(HALF * HEAD_DIM, HEAD_DIM)
    (attended,) = call(
        third_kernel,
        [shape((BLOCKS, PIECE, HEAD_DIM), half)],
        (place, kv0, *kv2b, *kv3b, best_a, total_a, best_b, total_b, first, token),
        0,
        [in_smem, in_vmem, in_hbm, in_hbm, in_vmem, in_vmem, *[in_hbm] * 5, in_vmem],
        [in_hbm],
        [
            pltpu.VMEM((half_blocks, 2 * PIECE, HEAD_DIM), half),
            pltpu.VMEM((2, TILE_ROWS, TILE_ROWS), jnp.float32),
            *work_space(LATE, LATE, 2),
            pltpu.VMEM((2, len(LATE) * TILE_ROWS, HEAD_DIM), jnp.float32),
            pltpu.VMEM((2, len(LATE) * TILE_ROWS, 2 * HEAD_DIM), jnp.float32),
            final_space(BLOCKS),
            dma((2,)),
            dma((5,)),
            dma((1 + len(LATE),)),
        ],
        limit=32,
    )
    returned = exchange(attended)
    other_prior = swap(prior, 1)
    whole_out = shape((TOKENS, width), half)
    (lin_out,) = call(
        lightning_kernel,
        [whole_out],
        (place, lin_query, lin_key, lin_value, log_decay, prior, other_prior, sibling),
        2 * 10**8,
        on_core[:8],
    )
    token, returned = lax.optimization_barrier((lin_out[0:8, 0:HEAD_DIM], returned))
    (soft_out,) = call(unpack_kernel, [whole_out], (returned, token), 1000)
    return (lin_out, soft_out)


def solution(mesh):
    spec = P("ctx", "head")
    return jax.shard_map(
        shards, mesh=mesh, in_specs=(spec,) * 7, out_specs=(spec, spec), check_vma=False
    )
```

```python
import functools
import math

import jax
import jax.numpy as jnp
from jax import lax
from jax.experimental import pallas as pl
from jax.experimental.pallas import tpu as pltpu
from jax.sharding import PartitionSpec as P

HEAD_DIM = 128
TOKENS = 128
HEADS_HERE = 16
BLOCKS = 64
PIECE = 32

norm_eps = 1e-06
masked_score = -1e30
exponent_scale = HEAD_DIM ** (-0.5) * math.log2(math.e)
X_STEP = 16
HALF = HEADS_HERE // 2
SLICE = HALF * HEAD_DIM // BLOCKS
QUARTER, CORE = range(2)
QUERY_TILE = 8
TILE_ROWS = QUERY_TILE * PIECE
LANES = TILE_ROWS // HEAD_DIM
TILES = BLOCKS // QUERY_TILE
HALF_TILES = TILES // 2
EARLY, LATE = range(HALF_TILES), range(HALF_TILES, TILES)


def place_of(device):
    x, z, core = device // 16, device // 2 % 8, device % 2
    return 2 * z + x // 2, 2 * (x % 2) + core


def columns(head):
    return slice(head * HEAD_DIM, (head + 1) * HEAD_DIM)


def rows(quarter):
    return slice(quarter * PIECE, (quarter + 1) * PIECE)


def whole(space=pltpu.VMEM):
    return pl.BlockSpec(memory_space=space)


def dot(left, right, left_dim, right_dim, precision=None):
    return lax.dot_general(
        left,
        right,
        (((left_dim,), (right_dim,)), ((), ())),
        precision=precision,
        preferred_element_type=jnp.float32,
    )


def call(kernel, out_shape, operands, flops, spaces=None, out_spaces=None, scratch=(), limit=16):
    out_shape = tuple(out_shape)
    bytes_moved = sum(math.prod(o.shape) * o.dtype.itemsize for o in (*operands, *out_shape))
    spaces = spaces or [pltpu.VMEM] * len(operands)
    out_spaces = out_spaces or [pltpu.VMEM] * len(out_shape)
    operands = [
        pltpu.with_memory_space_constraint(o, space) if space is pltpu.HBM else o
        for o, space in zip(operands, spaces)
    ]
    out_shape = [
        pltpu.HBM(o.shape, o.dtype) if space is pltpu.HBM else o
        for o, space in zip(out_shape, out_spaces)
    ]
    return pl.pallas_call(
        kernel,
        out_shape=out_shape,
        in_specs=[whole(space) for space in spaces],
        out_specs=[whole(space) for space in out_spaces],
        scratch_shapes=list(scratch),
        compiler_params=pltpu.CompilerParams(vmem_limit_bytes=limit << 20),
        cost_estimate=pl.CostEstimate(
            flops=flops, bytes_accessed=bytes_moved if flops else 0, transcendentals=0
        ),
    )(*operands)


def pack_kernel(query_ref, key_ref, value_ref, out_ref, held_ref, semaphores):
    sources = (query_ref, key_ref, value_ref)
    copies = [
        pltpu.make_async_copy(source, held_ref.at[which], semaphores.at[which])
        for which, source in enumerate(sources)
    ]
    for copy in copies:
        copy.start()
    for which, copy in enumerate(copies):
        copy.wait()
        for device in range(BLOCKS):
            head, quarter = place_of(device)
            out_ref[device, rows(which), :] = held_ref[which, rows(quarter), columns(head)]


def lower_triangle():
    shape = (TOKENS, TOKENS)
    return lax.broadcasted_iota(jnp.int32, shape, 0) >= lax.broadcasted_iota(jnp.int32, shape, 1)


def running_sums(decay):
    ones = jnp.where(lower_triangle(), 1.0, 0.0).astype(jnp.float32)
    return dot(ones, decay, 1, 0, lax.Precision.HIGHEST)


def split_parts(value):
    coarse = value.astype(jnp.bfloat16).astype(jnp.float32)
    middle = (value - coarse).astype(jnp.bfloat16).astype(jnp.float32)
    parts = (coarse, middle, value - coarse - middle)
    return jnp.concatenate([part.astype(jnp.bfloat16) for part in parts], axis=0)


def join_parts(parts, heads):
    wide = parts.astype(jnp.float32)
    return wide[0:heads] + wide[heads : 2 * heads] + wide[2 * heads : 3 * heads]


def head_rows(head):
    return slice(head * HEAD_DIM, (head + 1) * HEAD_DIM)


def states_kernel(key_ref, value_ref, decay_ref, out_ref):
    decay = decay_ref[...]
    running_sum = running_sums(decay)
    ones = jnp.ones((TOKENS, HEAD_DIM), jnp.float32)
    endings = dot(decay, ones, 0, 0, lax.Precision.HIGHEST)
    out_ref[HEADS_HERE * HEAD_DIM :, :] = split_parts(endings)
    for head in range(HEADS_HERE):
        sums = running_sum[:, head : head + 1]
        ending = running_sum[TOKENS - 1 : TOKENS, head : head + 1]
        key_wide = key_ref[:, columns(head)].astype(jnp.float32)
        key_scaled = (key_wide * jnp.exp(ending - sums)).astype(jnp.bfloat16)
        state = dot(key_scaled, value_ref[:, columns(head)], 0, 0)
        out_ref[head_rows(head), :] = state.astype(jnp.bfloat16)


def chip_kernel(place_ref, mine_ref, other_ref, out_ref, ending_ref):
    first = place_ref[CORE] == 0
    tail = slice(HEADS_HERE * HEAD_DIM, None)
    mine = join_parts(mine_ref[tail, :], HEADS_HERE)
    other = join_parts(other_ref[tail, :], HEADS_HERE)
    both = mine + other
    later = jnp.where(first, other, mine)
    ending_ref[...] = jnp.where(first, both[0:HALF], both[HALF:])
    part = lax.broadcasted_iota(jnp.int32, (8, HEAD_DIM), 0)
    for head in range(HALF):
        ending = ending_ref[head : head + 1, :]
        coarse = ending.astype(jnp.bfloat16).astype(jnp.float32)
        middle = (ending - coarse).astype(jnp.bfloat16).astype(jnp.float32)
        fine = ending - coarse - middle
        parts = jnp.where(part == 0, coarse, jnp.where(part == 1, middle, fine))
        for piece in range(HALF):
            out_ref[HALF * head + piece, SLICE:, :] = parts.astype(jnp.bfloat16)
    ending_ref[...] = jnp.where(first, later[0:HALF], later[HALF:])
    for head in range(HALF):
        place = place_ref[CORE] * (HALF * HEAD_DIM) + head * HEAD_DIM
        here = pl.ds(pl.multiple_of(place, HEAD_DIM), HEAD_DIM)
        mine = mine_ref[here, :].astype(jnp.float32)
        other = other_ref[here, :].astype(jnp.float32)
        fade = jnp.exp(ending_ref[head : head + 1, :])
        state = jnp.where(first, fade * mine + other, fade * other + mine)
        pieces = state.astype(jnp.bfloat16).reshape(HALF, SLICE, HEAD_DIM)
        out_ref[HALF * head : HALF * (head + 1), 0:SLICE, :] = pieces


def scan_kernel(moved_ref, out_ref):
    def step(chip, carries):
        following = []
        for core, carry in enumerate(carries):
            source = 2 * chip + core
            out_ref[source] = carry.astype(jnp.bfloat16)
            parts = moved_ref[source, SLICE:, :].astype(jnp.float32)
            ending = parts[0:1] + parts[1:2] + parts[2:3]
            state = moved_ref[source, 0:SLICE, :].astype(jnp.float32)
            following.append(jnp.exp(ending) * carry + state)
        return tuple(following)

    zero = jnp.zeros((SLICE, HEAD_DIM), jnp.float32)
    lax.fori_loop(0, BLOCKS // 2, step, (zero, zero), unroll=4)


def tile_pairs(queries, keys):
    return [(query, key) for query in queries for key in keys if key <= query]


def tile_blocks(index):
    return slice(index * QUERY_TILE, (index + 1) * QUERY_TILE)


class Attention:
    def __init__(self, queries, keys, slots, query_ref, part, bias_ref, best_ref, total_ref, score_ref):
        self.queries, self.keys, self.slots = queries, keys, slots
        self.query_ref, self.part, self.bias_ref = query_ref, part, bias_ref
        self.best_ref, self.total_ref, self.score_ref = best_ref, total_ref, score_ref
        self.pairs = tile_pairs(queries, keys)
        best_ref[...] = jnp.full(best_ref.shape, masked_score, jnp.float32)

    def here(self, query_tile):
        start = (query_tile - self.queries.start) * TILE_ROWS
        return slice(start, start + TILE_ROWS)

    def place(self, query_tile, key_tile, slot):
        return len(self.slots) * self.pairs.index((query_tile, key_tile)) + self.slots.index(slot)

    def find_best(self, query_tile, slots):
        here = self.here(query_tile)
        query = self.query_ref[tile_blocks(query_tile), rows(0), :].reshape(TILE_ROWS, HEAD_DIM)
        for key_tile in self.keys:
            if key_tile > query_tile or not slots:
                continue
            best = self.best_ref[here, :]
            for slot in slots:
                score = dot(query, self.part(slot, key_tile, 2), 1, 1)
                if key_tile == query_tile:
                    score += self.bias_ref[slot]
                self.score_ref[self.place(query_tile, key_tile, slot)] = score
                for lane in range(LANES):
                    best = jnp.maximum(best, score[:, columns(lane)])
            self.best_ref[here, :] = best

    def add_up(self, query_tile):
        here = self.here(query_tile)
        best = jnp.max(self.best_ref[here, :], axis=1, keepdims=True)
        self.best_ref[here, :] = jnp.broadcast_to(best, (TILE_ROWS, HEAD_DIM))
        self.total_ref[here, :] = jnp.zeros((TILE_ROWS, 2 * HEAD_DIM), jnp.float32)
        ones = jnp.ones((TILE_ROWS, HEAD_DIM), jnp.bfloat16)
        for key_tile in self.keys:
            if key_tile > query_tile:
                continue
            best_wide = jnp.concatenate([self.best_ref[here, :]] * LANES, axis=1)
            weights, values = [], []
            for slot in self.slots:
                score = self.score_ref[self.place(query_tile, key_tile, slot)]
                weight = jnp.exp2((score - best_wide) * exponent_scale)
                weights.append(weight.astype(jnp.bfloat16))
                values.append(jnp.concatenate([self.part(slot, key_tile, 1), ones], axis=1))
            self.total_ref[here, :] += dot(
                jnp.concatenate(weights, axis=1), jnp.concatenate(values, axis=0), 1, 0
            )


def load_part(array, place, from_end):
    wanted = rows(array.shape[1] // PIECE - from_end)
    return array[tile_blocks(place), wanted, :].reshape(TILE_ROWS, HEAD_DIM)


def fill_bias(place_ref, bias_ref, steps):
    mine = place_ref[QUARTER]

    def positions(shape, dim, quarter):
        row = lax.broadcasted_iota(jnp.int32, shape, dim)
        return (row // PIECE) * TOKENS + row % PIECE + quarter * PIECE

    queries = positions((TILE_ROWS, HEAD_DIM), 0, mine)
    queries = jnp.concatenate([queries] * LANES, axis=1)
    for slot, step in enumerate(steps):
        allowed = positions((1, TILE_ROWS), 1, mine ^ step) <= queries
        bias_ref[slot] = jnp.where(allowed, 0.0, masked_score)


def start_copies(sources, targets, semaphores):
    copies = [
        pltpu.make_async_copy(source, target, semaphores.at[number])
        for number, (source, target) in enumerate(zip(sources, targets))
    ]
    for copy in copies:
        copy.start()
    return copies


def ratio(total):
    outcome = (total[:, :HEAD_DIM] / total[:, HEAD_DIM:]).astype(jnp.bfloat16)
    return outcome.reshape(QUERY_TILE, PIECE, HEAD_DIM)


def first_kernel(
    place_ref, packed_ref, early_ref, late_ref, best_out, total_out, token_ref,
    kv_ref, bias_ref, best_ref, total_ref, score_ref, kv_sems, out_sems,
):
    copies = start_copies((early_ref, late_ref), (kv_ref.at[0], kv_ref.at[1]), kv_sems)
    fill_bias(place_ref, bias_ref, (0, 1))

    def part(slot, key_tile, from_end):
        if slot == 0:
            return load_part(packed_ref, key_tile, from_end)
        return load_part(kv_ref.at[key_tile // HALF_TILES], key_tile % HALF_TILES, from_end)

    work = Attention(
        LATE, range(TILES), (0, 1), packed_ref, part, bias_ref, best_ref, total_ref, score_ref
    )
    for query_tile in LATE:
        work.find_best(query_tile, (0,))
    for copy in copies:
        copy.wait()
    outward, sent = [], 0
    for query_tile in LATE:
        work.find_best(query_tile, (1,))
        work.add_up(query_tile)
        if query_tile >= TILES - 2:
            done = work.here(query_tile).stop
            place = pl.ds(sent, done - sent)
            outward += start_copies(
                (best_ref.at[place, :], total_ref.at[place, :]),
                (best_out.at[place, :], total_out.at[place, :]),
                out_sems.at[query_tile - (TILES - 2)],
            )
            sent = done
    token_ref[...] = best_ref[0:8, :]
    for copy in outward:
        copy.wait()


def second_kernel(
    place_ref, packed_ref, across_ref, diagonal_ref, order_ref, best_out, total_out, token_ref,
    kv_ref, best_ref, total_ref, score_ref, kv_sems, out_sems,
):
    copies = start_copies((across_ref,), (kv_ref,), kv_sems)

    def part(slot, key_tile, from_end):
        return load_part((kv_ref, diagonal_ref)[slot], key_tile, from_end)

    work = Attention(
        LATE, EARLY, (0, 1), packed_ref, part, None, best_ref, total_ref, score_ref
    )
    for query_tile in LATE:
        work.find_best(query_tile, (1,))
    for copy in copies:
        copy.wait()
    outward, sent = [], 0
    for query_tile in LATE:
        work.find_best(query_tile, (0,))
        work.add_up(query_tile)
        if query_tile >= TILES - 2:
            done = work.here(query_tile).stop
            place = pl.ds(sent, done - sent)
            outward += start_copies(
                (best_ref.at[place, :], total_ref.at[place, :]),
                (best_out.at[place, :], total_out.at[place, :]),
                out_sems.at[query_tile - (TILES - 2)],
            )
            sent = done
    token_ref[...] = best_ref[0:8, :]
    for copy in outward:
        copy.wait()


def early_kernel(
    place_ref, packed_ref, sibling_ref, across_ref, diagonal_ref, order_ref, final_out,
    kv_ref, bias_ref, best_ref, total_ref, score_ref, final_ref, kv_sems, final_sem,
):
    copies = start_copies((across_ref, sibling_ref), (kv_ref.at[1], kv_ref.at[0]), kv_sems)
    fill_bias(place_ref, bias_ref, (0, 1, 2, 3))

    def part(slot, key_tile, from_end):
        if slot == 0:
            return load_part(packed_ref, key_tile, from_end)
        return load_part(diagonal_ref if slot == 3 else kv_ref.at[slot - 1], key_tile, from_end)

    work = Attention(
        EARLY, EARLY, (0, 1, 2, 3), packed_ref, part, bias_ref, best_ref, total_ref, score_ref
    )
    for query_tile in EARLY:
        work.find_best(query_tile, (0,))
    for copy in copies:
        copy.wait()
    for query_tile in EARLY:
        work.find_best(query_tile, (1, 2, 3))
        work.add_up(query_tile)
        final_ref[tile_blocks(query_tile)] = ratio(total_ref[work.here(query_tile), :])
    copy = pltpu.make_async_copy(final_ref, final_out, final_sem)
    copy.start()
    copy.wait()


def third_kernel(
    place_ref, packed_ref, across1_ref, across2_ref, diagonal1_ref, diagonal2_ref, best_a, total_a, best_b, total_b,
    final_in, order_ref, out_ref,
    kv_ref, bias_ref, best_ref, total_ref, score_ref, bests_ref, totals_ref, final_ref,
    kv_sems, state_sems, final_sems,
):
    half_blocks = BLOCKS // 2
    middle = half_blocks // 2
    copies = start_copies(
        (across1_ref, across2_ref), (kv_ref.at[0:middle], kv_ref.at[middle:half_blocks]), kv_sems
    )
    state = start_copies(
        (best_a, best_b, total_a, total_b, final_in),
        (bests_ref.at[0], bests_ref.at[1], totals_ref.at[0], totals_ref.at[1], final_ref.at[0:half_blocks]),
        state_sems,
    )
    fill_bias(place_ref, bias_ref, (2, 3))

    def part(slot, key_tile, from_end):
        place = key_tile % HALF_TILES
        if slot == 0:
            return load_part(kv_ref, place, from_end)
        diagonal = (diagonal1_ref, diagonal2_ref)[place // (HALF_TILES // 2)]
        return load_part(diagonal, place % (HALF_TILES // 2), from_end)

    for copy in copies:
        copy.wait()
    work = Attention(
        LATE, LATE, (0, 1), packed_ref, part, bias_ref, best_ref, total_ref, score_ref
    )
    for query_tile in LATE:
        work.find_best(query_tile, (0, 1))
        work.add_up(query_tile)
    for copy in state:
        copy.wait()
    outward = start_copies(
        (final_ref.at[0:half_blocks],), (out_ref.at[0:half_blocks],), final_sems
    )
    for query_tile in LATE:
        here = work.here(query_tile)
        bests = [best_ref[here, :], bests_ref[0, here, :], bests_ref[1, here, :]]
        totals = [total_ref[here, :], totals_ref[0, here, :], totals_ref[1, here, :]]
        best = functools.reduce(jnp.maximum, bests)
        joined = 0.0
        for one, total in zip(bests, totals):
            shrink = jnp.exp2((one - best) * exponent_scale)
            joined += jnp.concatenate([shrink, shrink], axis=1) * total
        blocks = tile_blocks(query_tile)
        final_ref[blocks] = ratio(joined)
        outward += start_copies(
            (final_ref.at[blocks],),
            (out_ref.at[blocks],),
            final_sems.at[1 + query_tile - LATE.start : 2 + query_tile - LATE.start],
        )
    for copy in outward:
        copy.wait()


def work_space(queries, keys, slots):
    rows_here = len(queries) * TILE_ROWS
    return [
        pltpu.VMEM((rows_here, HEAD_DIM), jnp.float32),
        pltpu.VMEM((rows_here, 2 * HEAD_DIM), jnp.float32),
        pltpu.VMEM((slots * len(tile_pairs(queries, keys)), TILE_ROWS, TILE_ROWS), jnp.float32),
    ]


def final_space(blocks):
    return pltpu.VMEM((blocks, PIECE, HEAD_DIM), jnp.bfloat16)


def attention_space(segments, slots):
    return [
        pltpu.VMEM((segments, BLOCKS // 2, 2 * PIECE, HEAD_DIM), jnp.bfloat16),
        pltpu.VMEM((slots, TILE_ROWS, TILE_ROWS), jnp.float32),
    ]


def lightning_kernel(
    place_ref, query_ref, key_ref, value_ref, decay_ref, mine_ref, other_ref, sibling_ref, out_ref
):
    second = place_ref[CORE] == 1
    endings = join_parts(sibling_ref[HEADS_HERE * HEAD_DIM :, :], HEADS_HERE)
    decay = decay_ref[...]
    causal = lower_triangle()
    running_sum = running_sums(decay)
    later = jnp.where(causal, 0.0, 1.0).astype(jnp.float32)
    shape = (TOKENS, TOKENS)
    upper = lax.broadcasted_iota(jnp.int32, shape, 0) <= lax.broadcasted_iota(jnp.int32, shape, 1)
    upper = jnp.where(upper, 1.0, 0.0).astype(jnp.float32)
    running_row = dot(decay, upper, 0, 0, lax.Precision.HIGHEST)
    for head in range(HEADS_HERE):
        sums = running_sum[:, head : head + 1]
        spread = sums - running_row[head : head + 1, :]
        query = query_ref[:, columns(head)]
        value = value_ref[:, columns(head)]
        scores = dot(query, key_ref[:, columns(head)], 1, 1)
        decayed = jnp.where(causal, jnp.exp(jnp.where(causal, spread, 0.0)), 0.0) * scores
        total = dot(decayed.astype(jnp.bfloat16), value, 1, 0)
        query_scaled = (query.astype(jnp.float32) * jnp.exp(sums)).astype(jnp.bfloat16)
        half, place = head // HALF, head_rows(head % HALF)
        mine = mine_ref[place, :].astype(jnp.float32)
        other = other_ref[place, :].astype(jnp.float32)
        prior = jnp.where(place_ref[CORE] == half, mine, other)
        fade = jnp.exp(endings[head : head + 1, :])
        passed = fade * prior + sibling_ref[head_rows(head), :].astype(jnp.float32)
        prior = jnp.where(second, passed, prior)
        total += dot(query_scaled, prior.astype(jnp.bfloat16), 1, 0)
        mean = jnp.mean(total * total, axis=1, keepdims=True)
        out_ref[:, columns(head)] = (total * lax.rsqrt(mean + norm_eps)).astype(jnp.bfloat16)


def unpack_kernel(moved_ref, order_ref, out_ref):
    for device in range(BLOCKS):
        head, quarter = place_of(device)
        out_ref[rows(quarter), columns(head)] = moved_ref[device]


def exchange(value):
    return lax.all_to_all(value, "ctx", split_axis=0, concat_axis=0, tiled=True)


def swap(value, step):
    return lax.ppermute(value, "ctx", [(d, d ^ step) for d in range(BLOCKS)])


def shards(lin_query, lin_key, lin_value, log_decay, soft_query, soft_key, soft_value):
    half = jnp.bfloat16
    shape = jax.ShapeDtypeStruct
    index = lax.axis_index("ctx").astype(jnp.int32)
    core = index % 2
    place = jnp.stack([2 * (index // X_STEP % 2) + core, core])
    width = HEADS_HERE * HEAD_DIM
    (packed,) = call(
        pack_kernel,
        [shape((BLOCKS, 3 * PIECE, HEAD_DIM), half)],
        (soft_query, soft_key, soft_value),
        1000,
        [pltpu.HBM] * 3,
        scratch=(pltpu.VMEM((3, TOKENS, width), half), pltpu.SemaphoreType.DMA((3,))),
    )
    kv0 = exchange(packed)
    (states,) = call(
        states_kernel,
        [shape((width + 3 * HEADS_HERE, HEAD_DIM), half)],
        (lin_key, lin_value, log_decay),
        10**8,
    )
    sibling = swap(states, 1)
    on_core = [pltpu.SMEM] + [pltpu.VMEM] * 7
    (chip,) = call(
        chip_kernel,
        [shape((BLOCKS, SLICE + 8, HEAD_DIM), half)],
        (place, states, sibling),
        10**7,
        on_core[:3],
        scratch=(pltpu.VMEM((HALF, HEAD_DIM), jnp.float32),),
    )
    kv0, chip = lax.optimization_barrier((kv0, chip))
    half_blocks = BLOCKS // 2
    kv0a, kv0 = lax.optimization_barrier((kv0[:half_blocks, PIECE:], kv0))
    middle = half_blocks + half_blocks // 2
    kv0b = kv0[half_blocks:, PIECE:]
    kv0c, kv0d = kv0[half_blocks:middle, PIECE:], kv0[middle:, PIECE:]
    kv2a = swap(kv0a, X_STEP)
    kv1a, kv1b = swap(kv0a, 1), swap(kv0b, 1)
    chips = exchange(chip)

    dma = pltpu.SemaphoreType.DMA
    token_shape = shape((8, HEAD_DIM), jnp.float32)
    state_shapes = [
        shape((len(LATE) * TILE_ROWS, HEAD_DIM), jnp.float32),
        shape((len(LATE) * TILE_ROWS, 2 * HEAD_DIM), jnp.float32),
    ]
    in_hbm, in_vmem, in_smem = pltpu.HBM, pltpu.VMEM, pltpu.SMEM
    best_a, total_a, token = call(
        first_kernel,
        [*state_shapes, token_shape],
        (place, kv0, kv1a, kv1b),
        0,
        [in_smem, in_vmem, in_hbm, in_hbm],
        [in_hbm, in_hbm, in_vmem],
        [*attention_space(2, 2), *work_space(LATE, range(TILES), 2), dma((2,)), dma((2, 2))],
        limit=32,
    )
    token, kv2a, kv0c, kv0d = lax.optimization_barrier((token, kv2a, kv0c, kv0d))
    kv3a = swap(kv2a, 1)
    kv2b = swap(kv0c, X_STEP), swap(kv0d, X_STEP)
    best_b, total_b, token = call(
        second_kernel,
        [*state_shapes, token_shape],
        (place, kv0, kv2a, kv3a, token),
        0,
        [in_smem, in_vmem, in_hbm, in_vmem, in_vmem],
        [in_hbm, in_hbm, in_vmem],
        [
            pltpu.VMEM((half_blocks, 2 * PIECE, HEAD_DIM), half),
            *work_space(LATE, EARLY, 2),
            dma((1,)),
            dma((2, 2)),
        ],
        limit=32,
    )
    (first,) = call(
        early_kernel,
        [shape((half_blocks, PIECE, HEAD_DIM), half)],
        (place, kv0, kv1a, kv2a, kv3a, token),
        0,
        [in_smem, in_vmem, in_hbm, in_hbm, in_vmem, in_vmem],
        [in_hbm],
        [
            *attention_space(2, 4),
            *work_space(EARLY, EARLY, 4),
            final_space(half_blocks),
            dma((2,)),
            dma,
        ],
        limit=32,
    )
    token, chips = lax.optimization_barrier((token, chips))
    token, *kv2b = lax.optimization_barrier((token, *kv2b))
    kv3b = [swap(part, 1) for part in kv2b]
    (scanned,) = call(scan_kernel, [shape((BLOCKS, SLICE, HEAD_DIM), half)], (chips,), 10**6)
    prior = exchange(scanned).reshape(HALF * HEAD_DIM, HEAD_DIM)
    (attended,) = call(
        third_kernel,
        [shape((BLOCKS, PIECE, HEAD_DIM), half)],
        (place, kv0, *kv2b, *kv3b, best_a, total_a, best_b, total_b, first, token),
        0,
        [in_smem, in_vmem, in_hbm, in_hbm, in_vmem, in_vmem, *[in_hbm] * 5, in_vmem],
        [in_hbm],
        [
            pltpu.VMEM((half_blocks, 2 * PIECE, HEAD_DIM), half),
            pltpu.VMEM((2, TILE_ROWS, TILE_ROWS), jnp.float32),
            *work_space(LATE, LATE, 2),
            pltpu.VMEM((2, len(LATE) * TILE_ROWS, HEAD_DIM), jnp.float32),
            pltpu.VMEM((2, len(LATE) * TILE_ROWS, 2 * HEAD_DIM), jnp.float32),
            final_space(BLOCKS),
            dma((2,)),
            dma((5,)),
            dma((1 + len(LATE),)),
        ],
        limit=32,
    )
    returned = exchange(attended)
    other_prior = swap(prior, 1)
    whole_out = shape((TOKENS, width), half)
    (lin_out,) = call(
        lightning_kernel,
        [whole_out],
        (place, lin_query, lin_key, lin_value, log_decay, prior, other_prior, sibling),
        2 * 10**8,
        on_core[:8],
    )
    token, returned = lax.optimization_barrier((lin_out[0:8, 0:HEAD_DIM], returned))
    (soft_out,) = call(unpack_kernel, [whole_out], (returned, token), 1000)
    return (lin_out, soft_out)


def solution(mesh):
    spec = P("ctx", "head")
    return jax.shard_map(
        shards, mesh=mesh, in_specs=(spec,) * 7, out_specs=(spec, spec), check_vma=False
    )
```

```python
import functools
import math

import jax
import jax.numpy as jnp
from jax import lax
from jax.experimental import pallas as pl
from jax.experimental.pallas import tpu as pltpu
from jax.sharding import PartitionSpec as P

HEAD_DIM = 128
TOKENS = 128
HEADS_HERE = 16
BLOCKS = 64
PIECE = 32

norm_eps = 1e-06
masked_score = -1e30
exponent_scale = HEAD_DIM ** (-0.5) * math.log2(math.e)
X_STEP = 16
HALF = HEADS_HERE // 2
SLICE = HALF * HEAD_DIM // BLOCKS
QUARTER, CORE = range(2)
QUERY_TILE = 8
TILE_ROWS = QUERY_TILE * PIECE
LANES = TILE_ROWS // HEAD_DIM
TILES = BLOCKS // QUERY_TILE
HALF_TILES = TILES // 2
EARLY, LATE = range(HALF_TILES), range(HALF_TILES, TILES)


def place_of(device):
    x, z, core = device // 16, device // 2 % 8, device % 2
    return 2 * z + x // 2, 2 * (x % 2) + core


def columns(head):
    return slice(head * HEAD_DIM, (head + 1) * HEAD_DIM)


def rows(quarter):
    return slice(quarter * PIECE, (quarter + 1) * PIECE)


def whole(space=pltpu.VMEM):
    return pl.BlockSpec(memory_space=space)


def dot(left, right, left_dim, right_dim, precision=None):
    return lax.dot_general(
        left,
        right,
        (((left_dim,), (right_dim,)), ((), ())),
        precision=precision,
        preferred_element_type=jnp.float32,
    )


def call(kernel, out_shape, operands, flops, spaces=None, out_spaces=None, scratch=(), limit=16):
    out_shape = tuple(out_shape)
    bytes_moved = sum(math.prod(o.shape) * o.dtype.itemsize for o in (*operands, *out_shape))
    spaces = spaces or [pltpu.VMEM] * len(operands)
    out_spaces = out_spaces or [pltpu.VMEM] * len(out_shape)
    operands = [
        pltpu.with_memory_space_constraint(o, space) if space is pltpu.HBM else o
        for o, space in zip(operands, spaces)
    ]
    out_shape = [
        pltpu.HBM(o.shape, o.dtype) if space is pltpu.HBM else o
        for o, space in zip(out_shape, out_spaces)
    ]
    return pl.pallas_call(
        kernel,
        out_shape=out_shape,
        in_specs=[whole(space) for space in spaces],
        out_specs=[whole(space) for space in out_spaces],
        scratch_shapes=list(scratch),
        compiler_params=pltpu.CompilerParams(vmem_limit_bytes=limit << 20),
        cost_estimate=pl.CostEstimate(
            flops=flops, bytes_accessed=bytes_moved if flops else 0, transcendentals=0
        ),
    )(*operands)


def pack_kernel(query_ref, key_ref, value_ref, out_ref, held_ref, packed_ref, semaphores):
    sources = (query_ref, key_ref, value_ref)
    copies = [
        pltpu.make_async_copy(source, held_ref.at[which], semaphores.at[0, which])
        for which, source in enumerate(sources)
    ]
    for copy in copies:
        copy.start()
    outward = []
    for which, copy in enumerate(copies):
        copy.wait()
        for device in range(BLOCKS):
            head, quarter = place_of(device)
            packed_ref[which, device] = held_ref[which, rows(quarter), columns(head)]
        outward.append(
            pltpu.make_async_copy(
                packed_ref.at[which], out_ref.at[:, rows(which), :], semaphores.at[1, which]
            )
        )
        outward[-1].start()
    for copy in outward:
        copy.wait()


def slice_kernel(packed_ref, *refs):
    outs, semaphores = refs[:-1], refs[-1]
    half, middle = BLOCKS // 2, BLOCKS // 2 + BLOCKS // 4
    ranges = ((0, half), (half, BLOCKS), (half, middle), (middle, BLOCKS))
    copies = start_copies(
        [packed_ref.at[first:last, PIECE : 3 * PIECE, :] for first, last in ranges],
        outs,
        semaphores,
    )
    for copy in copies:
        copy.wait()


def lower_triangle():
    shape = (TOKENS, TOKENS)
    return lax.broadcasted_iota(jnp.int32, shape, 0) >= lax.broadcasted_iota(jnp.int32, shape, 1)


def running_sums(decay):
    ones = jnp.where(lower_triangle(), 1.0, 0.0).astype(jnp.float32)
    return dot(ones, decay, 1, 0, lax.Precision.HIGHEST)


def split_parts(value):
    coarse = value.astype(jnp.bfloat16).astype(jnp.float32)
    middle = (value - coarse).astype(jnp.bfloat16).astype(jnp.float32)
    parts = (coarse, middle, value - coarse - middle)
    return jnp.concatenate([part.astype(jnp.bfloat16) for part in parts], axis=0)


def join_parts(parts, heads):
    wide = parts.astype(jnp.float32)
    return wide[0:heads] + wide[heads : 2 * heads] + wide[2 * heads : 3 * heads]


def head_rows(head):
    return slice(head * HEAD_DIM, (head + 1) * HEAD_DIM)


def states_kernel(key_ref, value_ref, decay_ref, out_ref):
    decay = decay_ref[...]
    running_sum = running_sums(decay)
    ones = jnp.ones((TOKENS, HEAD_DIM), jnp.float32)
    endings = dot(decay, ones, 0, 0, lax.Precision.HIGHEST)
    out_ref[HEADS_HERE * HEAD_DIM :, :] = split_parts(endings)
    for head in range(HEADS_HERE):
        sums = running_sum[:, head : head + 1]
        ending = running_sum[TOKENS - 1 : TOKENS, head : head + 1]
        key_wide = key_ref[:, columns(head)].astype(jnp.float32)
        key_scaled = (key_wide * jnp.exp(ending - sums)).astype(jnp.bfloat16)
        state = dot(key_scaled, value_ref[:, columns(head)], 0, 0)
        out_ref[head_rows(head), :] = state.astype(jnp.bfloat16)


def chip_kernel(place_ref, mine_ref, other_ref, out_ref, ending_ref):
    first = place_ref[CORE] == 0
    tail = slice(HEADS_HERE * HEAD_DIM, None)
    mine = join_parts(mine_ref[tail, :], HEADS_HERE)
    other = join_parts(other_ref[tail, :], HEADS_HERE)
    both = mine + other
    later = jnp.where(first, other, mine)
    ending_ref[...] = jnp.where(first, both[0:HALF], both[HALF:])
    part = lax.broadcasted_iota(jnp.int32, (8, HEAD_DIM), 0)
    for head in range(HALF):
        ending = ending_ref[head : head + 1, :]
        coarse = ending.astype(jnp.bfloat16).astype(jnp.float32)
        middle = (ending - coarse).astype(jnp.bfloat16).astype(jnp.float32)
        fine = ending - coarse - middle
        parts = jnp.where(part == 0, coarse, jnp.where(part == 1, middle, fine))
        for piece in range(HALF):
            out_ref[HALF * head + piece, SLICE:, :] = parts.astype(jnp.bfloat16)
    ending_ref[...] = jnp.where(first, later[0:HALF], later[HALF:])
    for head in range(HALF):
        place = place_ref[CORE] * (HALF * HEAD_DIM) + head * HEAD_DIM
        here = pl.ds(pl.multiple_of(place, HEAD_DIM), HEAD_DIM)
        mine = mine_ref[here, :].astype(jnp.float32)
        other = other_ref[here, :].astype(jnp.float32)
        fade = jnp.exp(ending_ref[head : head + 1, :])
        state = jnp.where(first, fade * mine + other, fade * other + mine)
        pieces = state.astype(jnp.bfloat16).reshape(HALF, SLICE, HEAD_DIM)
        out_ref[HALF * head : HALF * (head + 1), 0:SLICE, :] = pieces


def scan_kernel(moved_ref, out_ref):
    def step(chip, carries):
        following = []
        for core, carry in enumerate(carries):
            source = 2 * chip + core
            out_ref[source] = carry.astype(jnp.bfloat16)
            parts = moved_ref[source, SLICE:, :].astype(jnp.float32)
            ending = parts[0:1] + parts[1:2] + parts[2:3]
            state = moved_ref[source, 0:SLICE, :].astype(jnp.float32)
            following.append(jnp.exp(ending) * carry + state)
        return tuple(following)

    zero = jnp.zeros((SLICE, HEAD_DIM), jnp.float32)
    lax.fori_loop(0, BLOCKS // 2, step, (zero, zero), unroll=4)


def tile_pairs(queries, keys):
    return [(query, key) for query in queries for key in keys if key <= query]


def tile_blocks(index):
    return slice(index * QUERY_TILE, (index + 1) * QUERY_TILE)


class Attention:
    def __init__(self, queries, keys, slots, query_ref, part, bias_ref, best_ref, total_ref, score_ref):
        self.queries, self.keys, self.slots = queries, keys, slots
        self.query_ref, self.part, self.bias_ref = query_ref, part, bias_ref
        self.best_ref, self.total_ref, self.score_ref = best_ref, total_ref, score_ref
        self.pairs = tile_pairs(queries, keys)
        best_ref[...] = jnp.full(best_ref.shape, masked_score, jnp.float32)

    def here(self, query_tile):
        start = (query_tile - self.queries.start) * TILE_ROWS
        return slice(start, start + TILE_ROWS)

    def place(self, query_tile, key_tile, slot):
        return len(self.slots) * self.pairs.index((query_tile, key_tile)) + self.slots.index(slot)

    def find_best(self, query_tile, slots):
        here = self.here(query_tile)
        query = self.query_ref[tile_blocks(query_tile), rows(0), :].reshape(TILE_ROWS, HEAD_DIM)
        for key_tile in self.keys:
            if key_tile > query_tile or not slots:
                continue
            best = self.best_ref[here, :]
            for slot in slots:
                score = dot(query, self.part(slot, key_tile, 2), 1, 1)
                if key_tile == query_tile:
                    score += self.bias_ref[slot]
                self.score_ref[self.place(query_tile, key_tile, slot)] = score
                for lane in range(LANES):
                    best = jnp.maximum(best, score[:, columns(lane)])
            self.best_ref[here, :] = best

    def add_up(self, query_tile):
        here = self.here(query_tile)
        best = jnp.max(self.best_ref[here, :], axis=1, keepdims=True)
        self.best_ref[here, :] = jnp.broadcast_to(best, (TILE_ROWS, HEAD_DIM))
        self.total_ref[here, :] = jnp.zeros((TILE_ROWS, 2 * HEAD_DIM), jnp.float32)
        ones = jnp.ones((TILE_ROWS, HEAD_DIM), jnp.bfloat16)
        for key_tile in self.keys:
            if key_tile > query_tile:
                continue
            best_wide = jnp.concatenate([self.best_ref[here, :]] * LANES, axis=1)
            weights, values = [], []
            for slot in self.slots:
                score = self.score_ref[self.place(query_tile, key_tile, slot)]
                weight = jnp.exp2((score - best_wide) * exponent_scale)
                weights.append(weight.astype(jnp.bfloat16))
                values.append(jnp.concatenate([self.part(slot, key_tile, 1), ones], axis=1))
            self.total_ref[here, :] += dot(
                jnp.concatenate(weights, axis=1), jnp.concatenate(values, axis=0), 1, 0
            )


def load_part(array, place, from_end):
    wanted = rows(array.shape[1] // PIECE - from_end)
    return array[tile_blocks(place), wanted, :].reshape(TILE_ROWS, HEAD_DIM)


def fill_bias(place_ref, bias_ref, steps):
    mine = place_ref[QUARTER]

    def positions(shape, dim, quarter):
        row = lax.broadcasted_iota(jnp.int32, shape, dim)
        return (row // PIECE) * TOKENS + row % PIECE + quarter * PIECE

    queries = positions((TILE_ROWS, HEAD_DIM), 0, mine)
    queries = jnp.concatenate([queries] * LANES, axis=1)
    for slot, step in enumerate(steps):
        allowed = positions((1, TILE_ROWS), 1, mine ^ step) <= queries
        bias_ref[slot] = jnp.where(allowed, 0.0, masked_score)


def start_copies(sources, targets, semaphores):
    copies = [
        pltpu.make_async_copy(source, target, semaphores.at[number])
        for number, (source, target) in enumerate(zip(sources, targets))
    ]
    for copy in copies:
        copy.start()
    return copies


def ratio(total):
    outcome = (total[:, :HEAD_DIM] / total[:, HEAD_DIM:]).astype(jnp.bfloat16)
    return outcome.reshape(QUERY_TILE, PIECE, HEAD_DIM)


def first_kernel(
    place_ref, packed_ref, early_ref, late_ref, best_out, total_out, token_ref,
    kv_ref, bias_ref, best_ref, total_ref, score_ref, kv_sems, out_sems,
):
    copies = start_copies((early_ref, late_ref), (kv_ref.at[0], kv_ref.at[1]), kv_sems)
    fill_bias(place_ref, bias_ref, (0, 1))

    def part(slot, key_tile, from_end):
        if slot == 0:
            return load_part(packed_ref, key_tile, from_end)
        return load_part(kv_ref.at[key_tile // HALF_TILES], key_tile % HALF_TILES, from_end)

    work = Attention(
        LATE, range(TILES), (0, 1), packed_ref, part, bias_ref, best_ref, total_ref, score_ref
    )
    for query_tile in LATE:
        work.find_best(query_tile, (0,))
    for copy in copies:
        copy.wait()
    outward, sent = [], 0
    for query_tile in LATE:
        work.find_best(query_tile, (1,))
        work.add_up(query_tile)
        if query_tile >= TILES - 2:
            done = work.here(query_tile).stop
            place = pl.ds(sent, done - sent)
            outward += start_copies(
                (best_ref.at[place, :], total_ref.at[place, :]),
                (best_out.at[place, :], total_out.at[place, :]),
                out_sems.at[query_tile - (TILES - 2)],
            )
            sent = done
    token_ref[...] = best_ref[0:8, :]
    for copy in outward:
        copy.wait()


def second_kernel(
    place_ref, packed_ref, sibling_ref, across_ref, diagonal_ref, order_ref,
    best_out, total_out, final_out, token_ref,
    kv_ref, bias_ref, best_ref, total_ref, score_ref, best2_ref, total2_ref, score2_ref, final_ref,
    kv_sems, out_sems, final_sem,
):
    copies = start_copies((across_ref, sibling_ref), (kv_ref.at[1], kv_ref.at[0]), kv_sems)
    fill_bias(place_ref, bias_ref, (0, 1, 2, 3))

    def part(slot, key_tile, from_end):
        if slot == 0:
            return load_part(packed_ref, key_tile, from_end)
        return load_part(diagonal_ref if slot == 3 else kv_ref.at[slot - 1], key_tile, from_end)

    early = Attention(
        EARLY, EARLY, (0, 1, 2, 3), packed_ref, part, bias_ref, best2_ref, total2_ref, score2_ref
    )
    for query_tile in EARLY:
        early.find_best(query_tile, (0,))
    late = Attention(
        LATE, EARLY, (2, 3), packed_ref, part, bias_ref, best_ref, total_ref, score_ref
    )
    for copy in copies:
        copy.wait()
    for query_tile in LATE:
        late.find_best(query_tile, (2, 3))
        late.add_up(query_tile)
    outward = start_copies((best_ref, total_ref), (best_out, total_out), out_sems)
    for query_tile in EARLY:
        early.find_best(query_tile, (1, 2, 3))
        early.add_up(query_tile)
        final_ref[tile_blocks(query_tile)] = ratio(total2_ref[early.here(query_tile), :])
    copy = pltpu.make_async_copy(final_ref, final_out, final_sem)
    copy.start()
    token_ref[...] = best2_ref[0:8, :]
    for other in outward:
        other.wait()
    copy.wait()


def third_kernel(
    place_ref, packed_ref, across1_ref, across2_ref, diagonal1_ref, diagonal2_ref, best_a, total_a, best_b, total_b,
    final_in, order_ref, out_ref,
    kv_ref, bias_ref, best_ref, total_ref, score_ref, bests_ref, totals_ref, final_ref,
    kv_sems, state_sems, final_sems,
):
    half_blocks = BLOCKS // 2
    middle = half_blocks // 2
    copies = start_copies(
        (across1_ref, across2_ref), (kv_ref.at[0:middle], kv_ref.at[middle:half_blocks]), kv_sems
    )
    state = start_copies(
        (best_a, best_b, total_a, total_b, final_in),
        (bests_ref.at[0], bests_ref.at[1], totals_ref.at[0], totals_ref.at[1], final_ref.at[0:half_blocks]),
        state_sems,
    )
    fill_bias(place_ref, bias_ref, (2, 3))

    def part(slot, key_tile, from_end):
        place = key_tile % HALF_TILES
        if slot == 0:
            return load_part(kv_ref, place, from_end)
        diagonal = (diagonal1_ref, diagonal2_ref)[place // (HALF_TILES // 2)]
        return load_part(diagonal, place % (HALF_TILES // 2), from_end)

    for copy in copies:
        copy.wait()
    work = Attention(
        LATE, LATE, (0, 1), packed_ref, part, bias_ref, best_ref, total_ref, score_ref
    )
    for query_tile in LATE:
        work.find_best(query_tile, (0, 1))
        work.add_up(query_tile)
    for copy in state:
        copy.wait()
    outward = start_copies(
        (final_ref.at[0:half_blocks],), (out_ref.at[0:half_blocks],), final_sems
    )
    for query_tile in LATE:
        here = work.here(query_tile)
        bests = [best_ref[here, :], bests_ref[0, here, :], bests_ref[1, here, :]]
        totals = [total_ref[here, :], totals_ref[0, here, :], totals_ref[1, here, :]]
        best = functools.reduce(jnp.maximum, bests)
        joined = 0.0
        for one, total in zip(bests, totals):
            shrink = jnp.exp2((one - best) * exponent_scale)
            joined += jnp.concatenate([shrink, shrink], axis=1) * total
        blocks = tile_blocks(query_tile)
        final_ref[blocks] = ratio(joined)
        outward += start_copies(
            (final_ref.at[blocks],),
            (out_ref.at[blocks],),
            final_sems.at[1 + query_tile - LATE.start : 2 + query_tile - LATE.start],
        )
    for copy in outward:
        copy.wait()


def work_space(queries, keys, slots):
    rows_here = len(queries) * TILE_ROWS
    return [
        pltpu.VMEM((rows_here, HEAD_DIM), jnp.float32),
        pltpu.VMEM((rows_here, 2 * HEAD_DIM), jnp.float32),
        pltpu.VMEM((slots * len(tile_pairs(queries, keys)), TILE_ROWS, TILE_ROWS), jnp.float32),
    ]


def final_space(blocks):
    return pltpu.VMEM((blocks, PIECE, HEAD_DIM), jnp.bfloat16)


def attention_space(segments, slots):
    return [
        pltpu.VMEM((segments, BLOCKS // 2, 2 * PIECE, HEAD_DIM), jnp.bfloat16),
        pltpu.VMEM((slots, TILE_ROWS, TILE_ROWS), jnp.float32),
    ]


def lightning_kernel(
    place_ref, query_ref, key_ref, value_ref, decay_ref, mine_ref, other_ref, sibling_ref, out_ref
):
    second = place_ref[CORE] == 1
    endings = join_parts(sibling_ref[HEADS_HERE * HEAD_DIM :, :], HEADS_HERE)
    decay = decay_ref[...]
    causal = lower_triangle()
    running_sum = running_sums(decay)
    later = jnp.where(causal, 0.0, 1.0).astype(jnp.float32)
    shape = (TOKENS, TOKENS)
    upper = lax.broadcasted_iota(jnp.int32, shape, 0) <= lax.broadcasted_iota(jnp.int32, shape, 1)
    upper = jnp.where(upper, 1.0, 0.0).astype(jnp.float32)
    running_row = dot(decay, upper, 0, 0, lax.Precision.HIGHEST)
    for head in range(HEADS_HERE):
        sums = running_sum[:, head : head + 1]
        spread = sums - running_row[head : head + 1, :]
        query = query_ref[:, columns(head)]
        value = value_ref[:, columns(head)]
        scores = dot(query, key_ref[:, columns(head)], 1, 1)
        decayed = jnp.where(causal, jnp.exp(jnp.where(causal, spread, 0.0)), 0.0) * scores
        total = dot(decayed.astype(jnp.bfloat16), value, 1, 0)
        query_scaled = (query.astype(jnp.float32) * jnp.exp(sums)).astype(jnp.bfloat16)
        half, place = head // HALF, head_rows(head % HALF)
        mine = mine_ref[place, :].astype(jnp.float32)
        other = other_ref[place, :].astype(jnp.float32)
        prior = jnp.where(place_ref[CORE] == half, mine, other)
        fade = jnp.exp(endings[head : head + 1, :])
        passed = fade * prior + sibling_ref[head_rows(head), :].astype(jnp.float32)
        prior = jnp.where(second, passed, prior)
        total += dot(query_scaled, prior.astype(jnp.bfloat16), 1, 0)
        mean = jnp.mean(total * total, axis=1, keepdims=True)
        out_ref[:, columns(head)] = (total * lax.rsqrt(mean + norm_eps)).astype(jnp.bfloat16)


def unpack_kernel(moved_ref, order_ref, out_ref):
    for device in range(BLOCKS):
        head, quarter = place_of(device)
        out_ref[rows(quarter), columns(head)] = moved_ref[device]


def exchange(value):
    return lax.all_to_all(value, "ctx", split_axis=0, concat_axis=0, tiled=True)


def swap(value, step):
    return lax.ppermute(value, "ctx", [(d, d ^ step) for d in range(BLOCKS)])


def shards(lin_query, lin_key, lin_value, log_decay, soft_query, soft_key, soft_value):
    half = jnp.bfloat16
    shape = jax.ShapeDtypeStruct
    index = lax.axis_index("ctx").astype(jnp.int32)
    core = index % 2
    place = jnp.stack([2 * (index // X_STEP % 2) + core, core])
    width = HEADS_HERE * HEAD_DIM
    (packed,) = call(
        pack_kernel,
        [shape((BLOCKS, 3 * PIECE, HEAD_DIM), half)],
        (soft_query, soft_key, soft_value),
        1000,
        [pltpu.HBM] * 3,
        [pltpu.HBM],
        (
            pltpu.VMEM((3, TOKENS, width), half),
            pltpu.VMEM((3, BLOCKS, PIECE, HEAD_DIM), half),
            pltpu.SemaphoreType.DMA((2, 3)),
        ),
    )
    kv0 = exchange(packed)
    (states,) = call(
        states_kernel,
        [shape((width + 3 * HEADS_HERE, HEAD_DIM), half)],
        (lin_key, lin_value, log_decay),
        10**8,
    )
    sibling = swap(states, 1)
    on_core = [pltpu.SMEM] + [pltpu.VMEM] * 7
    (chip,) = call(
        chip_kernel,
        [shape((BLOCKS, SLICE + 8, HEAD_DIM), half)],
        (place, states, sibling),
        10**7,
        on_core[:3],
        scratch=(pltpu.VMEM((HALF, HEAD_DIM), jnp.float32),),
    )
    kv0, chip = lax.optimization_barrier((kv0, chip))
    half_blocks = BLOCKS // 2
    kv0a, kv0b, kv0c, kv0d = call(
        slice_kernel,
        [
            shape((blocks, 2 * PIECE, HEAD_DIM), half)
            for blocks in (half_blocks, half_blocks, half_blocks // 2, half_blocks // 2)
        ],
        (kv0,),
        0,
        [pltpu.VMEM],
        [pltpu.HBM] * 4,
        [pltpu.SemaphoreType.DMA((4,))],
    )
    kv2a = swap(kv0a, X_STEP)
    kv1a, kv1b = swap(kv0a, 1), swap(kv0b, 1)
    chips = exchange(chip)

    dma = pltpu.SemaphoreType.DMA
    token_shape = shape((8, HEAD_DIM), jnp.float32)
    state_shapes = [
        shape((len(LATE) * TILE_ROWS, HEAD_DIM), jnp.float32),
        shape((len(LATE) * TILE_ROWS, 2 * HEAD_DIM), jnp.float32),
    ]
    in_hbm, in_vmem, in_smem = pltpu.HBM, pltpu.VMEM, pltpu.SMEM
    best_a, total_a, token = call(
        first_kernel,
        [*state_shapes, token_shape],
        (place, kv0, kv1a, kv1b),
        0,
        [in_smem, in_vmem, in_hbm, in_hbm],
        [in_hbm, in_hbm, in_vmem],
        [*attention_space(2, 2), *work_space(LATE, range(TILES), 2), dma((2,)), dma((2, 2))],
        limit=32,
    )
    token, kv2a, kv0c, kv0d = lax.optimization_barrier((token, kv2a, kv0c, kv0d))
    kv3a = swap(kv2a, 1)
    kv2b = swap(kv0c, X_STEP), swap(kv0d, X_STEP)
    best_b, total_b, first, token = call(
        second_kernel,
        [*state_shapes, shape((half_blocks, PIECE, HEAD_DIM), half), token_shape],
        (place, kv0, kv1a, kv2a, kv3a, token),
        0,
        [in_smem, in_vmem, in_hbm, in_hbm, in_vmem, in_vmem],
        [in_hbm, in_hbm, in_hbm, in_vmem],
        [
            *attention_space(2, 4),
            *work_space(LATE, EARLY, 2),
            *work_space(EARLY, EARLY, 4),
            final_space(half_blocks),
            dma((2,)),
            dma((2,)),
            dma,
        ],
        limit=40,
    )
    token, chips = lax.optimization_barrier((token, chips))
    token, *kv2b = lax.optimization_barrier((token, *kv2b))
    kv3b = [swap(part, 1) for part in kv2b]
    (scanned,) = call(scan_kernel, [shape((BLOCKS, SLICE, HEAD_DIM), half)], (chips,), 10**6)
    prior = exchange(scanned).reshape(HALF * HEAD_DIM, HEAD_DIM)
    (attended,) = call(
        third_kernel,
        [shape((BLOCKS, PIECE, HEAD_DIM), half)],
        (place, kv0, *kv2b, *kv3b, best_a, total_a, best_b, total_b, first, token),
        0,
        [in_smem, in_vmem, in_hbm, in_hbm, in_vmem, in_vmem, *[in_hbm] * 5, in_vmem],
        [in_hbm],
        [
            pltpu.VMEM((half_blocks, 2 * PIECE, HEAD_DIM), half),
            pltpu.VMEM((2, TILE_ROWS, TILE_ROWS), jnp.float32),
            *work_space(LATE, LATE, 2),
            pltpu.VMEM((2, len(LATE) * TILE_ROWS, HEAD_DIM), jnp.float32),
            pltpu.VMEM((2, len(LATE) * TILE_ROWS, 2 * HEAD_DIM), jnp.float32),
            final_space(BLOCKS),
            dma((2,)),
            dma((5,)),
            dma((1 + len(LATE),)),
        ],
        limit=32,
    )
    returned = exchange(attended)
    other_prior = swap(prior, 1)
    whole_out = shape((TOKENS, width), half)
    (lin_out,) = call(
        lightning_kernel,
        [whole_out],
        (place, lin_query, lin_key, lin_value, log_decay, prior, other_prior, sibling),
        2 * 10**8,
        on_core[:8],
    )
    token, returned = lax.optimization_barrier((lin_out[0:8, 0:HEAD_DIM], returned))
    (soft_out,) = call(unpack_kernel, [whole_out], (returned, token), 1000)
    return (lin_out, soft_out)


def solution(mesh):
    spec = P("ctx", "head")
    return jax.shard_map(
        shards, mesh=mesh, in_specs=(spec,) * 7, out_specs=(spec, spec), check_vma=False
    )
```

```python
import functools
import math

import jax
import jax.numpy as jnp
from jax import lax
from jax.experimental import pallas as pl
from jax.experimental.pallas import tpu as pltpu
from jax.sharding import PartitionSpec as P

HEAD_DIM = 128
TOKENS = 128
HEADS_HERE = 16
BLOCKS = 64
PIECE = 32

norm_eps = 1e-06
masked_score = -1e30
exponent_scale = HEAD_DIM ** (-0.5) * math.log2(math.e)
X_STEP = 16
HALF = HEADS_HERE // 2
SLICE = HALF * HEAD_DIM // BLOCKS
QUARTER, CORE = range(2)
QUERY_TILE = 8
TILE_ROWS = QUERY_TILE * PIECE
LANES = TILE_ROWS // HEAD_DIM
TILES = BLOCKS // QUERY_TILE
HALF_TILES = TILES // 2
EARLY, LATE = range(HALF_TILES), range(HALF_TILES, TILES)


def place_of(device):
    x, z, core = device // 16, device // 2 % 8, device % 2
    return 2 * z + x // 2, 2 * (x % 2) + core


def columns(head):
    return slice(head * HEAD_DIM, (head + 1) * HEAD_DIM)


def rows(quarter):
    return slice(quarter * PIECE, (quarter + 1) * PIECE)


def whole(space=pltpu.VMEM):
    return pl.BlockSpec(memory_space=space)


def dot(left, right, left_dim, right_dim, precision=None):
    return lax.dot_general(
        left,
        right,
        (((left_dim,), (right_dim,)), ((), ())),
        precision=precision,
        preferred_element_type=jnp.float32,
    )


def call(kernel, out_shape, operands, flops, spaces=None, out_spaces=None, scratch=(), limit=16):
    out_shape = tuple(out_shape)
    bytes_moved = sum(math.prod(o.shape) * o.dtype.itemsize for o in (*operands, *out_shape))
    spaces = spaces or [pltpu.VMEM] * len(operands)
    out_spaces = out_spaces or [pltpu.VMEM] * len(out_shape)
    operands = [
        pltpu.with_memory_space_constraint(o, space) if space is pltpu.HBM else o
        for o, space in zip(operands, spaces)
    ]
    out_shape = [
        pltpu.HBM(o.shape, o.dtype) if space is pltpu.HBM else o
        for o, space in zip(out_shape, out_spaces)
    ]
    return pl.pallas_call(
        kernel,
        out_shape=out_shape,
        in_specs=[whole(space) for space in spaces],
        out_specs=[whole(space) for space in out_spaces],
        scratch_shapes=list(scratch),
        compiler_params=pltpu.CompilerParams(vmem_limit_bytes=limit << 20),
        cost_estimate=pl.CostEstimate(
            flops=flops, bytes_accessed=bytes_moved if flops else 0, transcendentals=0
        ),
    )(*operands)


def pack_kernel(query_ref, key_ref, value_ref, out_ref, held_ref, packed_ref, semaphores):
    sources = (query_ref, key_ref, value_ref)
    copies = [
        pltpu.make_async_copy(source, held_ref.at[which], semaphores.at[0, which])
        for which, source in enumerate(sources)
    ]
    for copy in copies:
        copy.start()
    outward = []
    for which, copy in enumerate(copies):
        copy.wait()
        for device in range(BLOCKS):
            head, quarter = place_of(device)
            packed_ref[which, device] = held_ref[which, rows(quarter), columns(head)]
        outward.append(
            pltpu.make_async_copy(
                packed_ref.at[which], out_ref.at[:, rows(which), :], semaphores.at[1, which]
            )
        )
        outward[-1].start()
    for copy in outward:
        copy.wait()


def slice_kernel(packed_ref, *refs):
    outs, semaphores = refs[:-1], refs[-1]
    half, middle = BLOCKS // 2, BLOCKS // 2 + BLOCKS // 4
    ranges = ((0, half), (half, BLOCKS), (half, middle), (middle, BLOCKS))
    copies = start_copies(
        [packed_ref.at[first:last, PIECE : 3 * PIECE, :] for first, last in ranges],
        outs,
        semaphores,
    )
    for copy in copies:
        copy.wait()


def lower_triangle():
    shape = (TOKENS, TOKENS)
    return lax.broadcasted_iota(jnp.int32, shape, 0) >= lax.broadcasted_iota(jnp.int32, shape, 1)


def running_sums(decay):
    ones = jnp.where(lower_triangle(), 1.0, 0.0).astype(jnp.float32)
    return dot(ones, decay, 1, 0, lax.Precision.HIGHEST)


def split_parts(value):
    coarse = value.astype(jnp.bfloat16).astype(jnp.float32)
    middle = (value - coarse).astype(jnp.bfloat16).astype(jnp.float32)
    parts = (coarse, middle, value - coarse - middle)
    return jnp.concatenate([part.astype(jnp.bfloat16) for part in parts], axis=0)


def join_parts(parts, heads):
    wide = parts.astype(jnp.float32)
    return wide[0:heads] + wide[heads : 2 * heads] + wide[2 * heads : 3 * heads]


def head_rows(head):
    return slice(head * HEAD_DIM, (head + 1) * HEAD_DIM)


def states_kernel(key_ref, value_ref, decay_ref, out_ref):
    decay = decay_ref[...]
    running_sum = running_sums(decay)
    ones = jnp.ones((TOKENS, HEAD_DIM), jnp.float32)
    endings = dot(decay, ones, 0, 0, lax.Precision.HIGHEST)
    out_ref[HEADS_HERE * HEAD_DIM :, :] = split_parts(endings)
    for head in range(HEADS_HERE):
        sums = running_sum[:, head : head + 1]
        ending = running_sum[TOKENS - 1 : TOKENS, head : head + 1]
        key_wide = key_ref[:, columns(head)].astype(jnp.float32)
        key_scaled = (key_wide * jnp.exp(ending - sums)).astype(jnp.bfloat16)
        state = dot(key_scaled, value_ref[:, columns(head)], 0, 0)
        out_ref[head_rows(head), :] = state.astype(jnp.bfloat16)


def chip_kernel(place_ref, mine_ref, other_ref, out_ref, ending_ref):
    first = place_ref[CORE] == 0
    tail = slice(HEADS_HERE * HEAD_DIM, None)
    mine = join_parts(mine_ref[tail, :], HEADS_HERE)
    other = join_parts(other_ref[tail, :], HEADS_HERE)
    both = mine + other
    later = jnp.where(first, other, mine)
    ending_ref[...] = jnp.where(first, both[0:HALF], both[HALF:])
    part = lax.broadcasted_iota(jnp.int32, (8, HEAD_DIM), 0)
    for head in range(HALF):
        ending = ending_ref[head : head + 1, :]
        coarse = ending.astype(jnp.bfloat16).astype(jnp.float32)
        middle = (ending - coarse).astype(jnp.bfloat16).astype(jnp.float32)
        fine = ending - coarse - middle
        parts = jnp.where(part == 0, coarse, jnp.where(part == 1, middle, fine))
        for piece in range(HALF):
            out_ref[HALF * head + piece, SLICE:, :] = parts.astype(jnp.bfloat16)
    ending_ref[...] = jnp.where(first, later[0:HALF], later[HALF:])
    for head in range(HALF):
        place = place_ref[CORE] * (HALF * HEAD_DIM) + head * HEAD_DIM
        here = pl.ds(pl.multiple_of(place, HEAD_DIM), HEAD_DIM)
        mine = mine_ref[here, :].astype(jnp.float32)
        other = other_ref[here, :].astype(jnp.float32)
        fade = jnp.exp(ending_ref[head : head + 1, :])
        state = jnp.where(first, fade * mine + other, fade * other + mine)
        pieces = state.astype(jnp.bfloat16).reshape(HALF, SLICE, HEAD_DIM)
        out_ref[HALF * head : HALF * (head + 1), 0:SLICE, :] = pieces


def scan_kernel(moved_ref, out_ref):
    def step(chip, carries):
        following = []
        for core, carry in enumerate(carries):
            source = 2 * chip + core
            out_ref[source] = carry.astype(jnp.bfloat16)
            parts = moved_ref[source, SLICE:, :].astype(jnp.float32)
            ending = parts[0:1] + parts[1:2] + parts[2:3]
            state = moved_ref[source, 0:SLICE, :].astype(jnp.float32)
            following.append(jnp.exp(ending) * carry + state)
        return tuple(following)

    zero = jnp.zeros((SLICE, HEAD_DIM), jnp.float32)
    lax.fori_loop(0, BLOCKS // 2, step, (zero, zero), unroll=16)


def tile_pairs(queries, keys):
    return [(query, key) for query in queries for key in keys if key <= query]


def tile_blocks(index):
    return slice(index * QUERY_TILE, (index + 1) * QUERY_TILE)


class Attention:
    def __init__(self, queries, keys, slots, query_ref, part, bias_ref, best_ref, total_ref, score_ref):
        self.queries, self.keys, self.slots = queries, keys, slots
        self.query_ref, self.part, self.bias_ref = query_ref, part, bias_ref
        self.best_ref, self.total_ref, self.score_ref = best_ref, total_ref, score_ref
        self.pairs = tile_pairs(queries, keys)
        best_ref[...] = jnp.full(best_ref.shape, masked_score, jnp.float32)

    def here(self, query_tile):
        start = (query_tile - self.queries.start) * TILE_ROWS
        return slice(start, start + TILE_ROWS)

    def place(self, query_tile, key_tile, slot):
        return len(self.slots) * self.pairs.index((query_tile, key_tile)) + self.slots.index(slot)

    def find_best(self, query_tile, slots):
        here = self.here(query_tile)
        query = self.query_ref[tile_blocks(query_tile), rows(0), :].reshape(TILE_ROWS, HEAD_DIM)
        for key_tile in self.keys:
            if key_tile > query_tile or not slots:
                continue
            best = self.best_ref[here, :]
            for slot in slots:
                score = dot(query, self.part(slot, key_tile, 2), 1, 1)
                if key_tile == query_tile:
                    score += self.bias_ref[slot]
                self.score_ref[self.place(query_tile, key_tile, slot)] = score
                for lane in range(LANES):
                    best = jnp.maximum(best, score[:, columns(lane)])
            self.best_ref[here, :] = best

    def add_up(self, query_tile):
        here = self.here(query_tile)
        best = jnp.max(self.best_ref[here, :], axis=1, keepdims=True)
        self.best_ref[here, :] = jnp.broadcast_to(best, (TILE_ROWS, HEAD_DIM))
        self.total_ref[here, :] = jnp.zeros((TILE_ROWS, 2 * HEAD_DIM), jnp.float32)
        ones = jnp.ones((TILE_ROWS, HEAD_DIM), jnp.bfloat16)
        for key_tile in self.keys:
            if key_tile > query_tile:
                continue
            best_wide = jnp.concatenate([self.best_ref[here, :]] * LANES, axis=1)
            weights, values = [], []
            for slot in self.slots:
                score = self.score_ref[self.place(query_tile, key_tile, slot)]
                weight = jnp.exp2((score - best_wide) * exponent_scale)
                weights.append(weight.astype(jnp.bfloat16))
                values.append(jnp.concatenate([self.part(slot, key_tile, 1), ones], axis=1))
            self.total_ref[here, :] += dot(
                jnp.concatenate(weights, axis=1), jnp.concatenate(values, axis=0), 1, 0
            )


def load_part(array, place, from_end):
    wanted = rows(array.shape[1] // PIECE - from_end)
    return array[tile_blocks(place), wanted, :].reshape(TILE_ROWS, HEAD_DIM)


def fill_bias(place_ref, bias_ref, steps):
    mine = place_ref[QUARTER]

    def positions(shape, dim, quarter):
        row = lax.broadcasted_iota(jnp.int32, shape, dim)
        return (row // PIECE) * TOKENS + row % PIECE + quarter * PIECE

    queries = positions((TILE_ROWS, HEAD_DIM), 0, mine)
    queries = jnp.concatenate([queries] * LANES, axis=1)
    for slot, step in enumerate(steps):
        allowed = positions((1, TILE_ROWS), 1, mine ^ step) <= queries
        bias_ref[slot] = jnp.where(allowed, 0.0, masked_score)


def start_copies(sources, targets, semaphores):
    copies = [
        pltpu.make_async_copy(source, target, semaphores.at[number])
        for number, (source, target) in enumerate(zip(sources, targets))
    ]
    for copy in copies:
        copy.start()
    return copies


def ratio(total):
    outcome = (total[:, :HEAD_DIM] / total[:, HEAD_DIM:]).astype(jnp.bfloat16)
    return outcome.reshape(QUERY_TILE, PIECE, HEAD_DIM)


def first_kernel(
    place_ref, packed_ref, early_ref, late_ref, best_out, total_out, token_ref,
    kv_ref, bias_ref, best_ref, total_ref, score_ref, kv_sems, out_sems,
):
    copies = start_copies((early_ref, late_ref), (kv_ref.at[0], kv_ref.at[1]), kv_sems)
    fill_bias(place_ref, bias_ref, (0, 1))

    def part(slot, key_tile, from_end):
        if slot == 0:
            return load_part(packed_ref, key_tile, from_end)
        return load_part(kv_ref.at[key_tile // HALF_TILES], key_tile % HALF_TILES, from_end)

    work = Attention(
        LATE, range(TILES), (0, 1), packed_ref, part, bias_ref, best_ref, total_ref, score_ref
    )
    for query_tile in LATE:
        work.find_best(query_tile, (0,))
    for copy in copies:
        copy.wait()
    outward, sent = [], 0
    for query_tile in LATE:
        work.find_best(query_tile, (1,))
        work.add_up(query_tile)
        if query_tile >= TILES - 2:
            done = work.here(query_tile).stop
            place = pl.ds(sent, done - sent)
            outward += start_copies(
                (best_ref.at[place, :], total_ref.at[place, :]),
                (best_out.at[place, :], total_out.at[place, :]),
                out_sems.at[query_tile - (TILES - 2)],
            )
            sent = done
    token_ref[...] = best_ref[0:8, :]
    for copy in outward:
        copy.wait()


def second_kernel(
    place_ref, packed_ref, sibling_ref, across_ref, diagonal_ref, order_ref,
    best_out, total_out, final_out, token_ref,
    kv_ref, bias_ref, best_ref, total_ref, score_ref, best2_ref, total2_ref, score2_ref, final_ref,
    kv_sems, out_sems, final_sem,
):
    copies = start_copies((across_ref, sibling_ref), (kv_ref.at[1], kv_ref.at[0]), kv_sems)
    fill_bias(place_ref, bias_ref, (0, 1, 2, 3))

    def part(slot, key_tile, from_end):
        if slot == 0:
            return load_part(packed_ref, key_tile, from_end)
        return load_part(diagonal_ref if slot == 3 else kv_ref.at[slot - 1], key_tile, from_end)

    early = Attention(
        EARLY, EARLY, (0, 1, 2, 3), packed_ref, part, bias_ref, best2_ref, total2_ref, score2_ref
    )
    for query_tile in EARLY:
        early.find_best(query_tile, (0,))
    late = Attention(
        LATE, EARLY, (2, 3), packed_ref, part, bias_ref, best_ref, total_ref, score_ref
    )
    for copy in copies:
        copy.wait()
    for query_tile in LATE:
        late.find_best(query_tile, (2, 3))
        late.add_up(query_tile)
    outward = start_copies((best_ref, total_ref), (best_out, total_out), out_sems)
    for query_tile in EARLY:
        early.find_best(query_tile, (1, 2, 3))
        early.add_up(query_tile)
        blocks = tile_blocks(query_tile)
        final_ref[blocks] = ratio(total2_ref[early.here(query_tile), :])
        outward += start_copies(
            (final_ref.at[blocks],), (final_out.at[blocks],), final_sem.at[query_tile : query_tile + 1]
        )
    token_ref[...] = best2_ref[0:8, :]
    for copy in outward:
        copy.wait()


def third_kernel(
    place_ref, packed_ref, across1_ref, across2_ref, diagonal1_ref, diagonal2_ref, best_a, total_a, best_b, total_b,
    final_in, order_ref, out_ref,
    kv_ref, bias_ref, best_ref, total_ref, score_ref, bests_ref, totals_ref, final_ref,
    kv_sems, state_sems, final_sems,
):
    half_blocks = BLOCKS // 2
    middle = half_blocks // 2
    copies = start_copies(
        (across1_ref, across2_ref), (kv_ref.at[0:middle], kv_ref.at[middle:half_blocks]), kv_sems
    )
    state = start_copies(
        (best_a, best_b, total_a, total_b, final_in),
        (bests_ref.at[0], bests_ref.at[1], totals_ref.at[0], totals_ref.at[1], final_ref.at[0:half_blocks]),
        state_sems,
    )
    fill_bias(place_ref, bias_ref, (2, 3))

    def part(slot, key_tile, from_end):
        place = key_tile % HALF_TILES
        if slot == 0:
            return load_part(kv_ref, place, from_end)
        diagonal = (diagonal1_ref, diagonal2_ref)[place // (HALF_TILES // 2)]
        return load_part(diagonal, place % (HALF_TILES // 2), from_end)

    for copy in copies:
        copy.wait()
    work = Attention(
        LATE, LATE, (0, 1), packed_ref, part, bias_ref, best_ref, total_ref, score_ref
    )
    for query_tile in LATE:
        work.find_best(query_tile, (0, 1))
        work.add_up(query_tile)
    for copy in state:
        copy.wait()
    outward = start_copies(
        (final_ref.at[0:half_blocks],), (out_ref.at[0:half_blocks],), final_sems
    )
    for query_tile in LATE:
        here = work.here(query_tile)
        bests = [best_ref[here, :], bests_ref[0, here, :], bests_ref[1, here, :]]
        totals = [total_ref[here, :], totals_ref[0, here, :], totals_ref[1, here, :]]
        best = functools.reduce(jnp.maximum, bests)
        joined = 0.0
        for one, total in zip(bests, totals):
            shrink = jnp.exp2((one - best) * exponent_scale)
            joined += jnp.concatenate([shrink, shrink], axis=1) * total
        blocks = tile_blocks(query_tile)
        final_ref[blocks] = ratio(joined)
        outward += start_copies(
            (final_ref.at[blocks],),
            (out_ref.at[blocks],),
            final_sems.at[1 + query_tile - LATE.start : 2 + query_tile - LATE.start],
        )
    for copy in outward:
        copy.wait()


def work_space(queries, keys, slots):
    rows_here = len(queries) * TILE_ROWS
    return [
        pltpu.VMEM((rows_here, HEAD_DIM), jnp.float32),
        pltpu.VMEM((rows_here, 2 * HEAD_DIM), jnp.float32),
        pltpu.VMEM((slots * len(tile_pairs(queries, keys)), TILE_ROWS, TILE_ROWS), jnp.float32),
    ]


def final_space(blocks):
    return pltpu.VMEM((blocks, PIECE, HEAD_DIM), jnp.bfloat16)


def attention_space(segments, slots):
    return [
        pltpu.VMEM((segments, BLOCKS // 2, 2 * PIECE, HEAD_DIM), jnp.bfloat16),
        pltpu.VMEM((slots, TILE_ROWS, TILE_ROWS), jnp.float32),
    ]


def lightning_kernel(
    place_ref, query_ref, key_ref, value_ref, decay_ref, mine_ref, other_ref, sibling_ref, out_ref
):
    second = place_ref[CORE] == 1
    endings = join_parts(sibling_ref[HEADS_HERE * HEAD_DIM :, :], HEADS_HERE)
    decay = decay_ref[...]
    causal = lower_triangle()
    running_sum = running_sums(decay)
    later = jnp.where(causal, 0.0, 1.0).astype(jnp.float32)
    shape = (TOKENS, TOKENS)
    upper = lax.broadcasted_iota(jnp.int32, shape, 0) <= lax.broadcasted_iota(jnp.int32, shape, 1)
    upper = jnp.where(upper, 1.0, 0.0).astype(jnp.float32)
    running_row = dot(decay, upper, 0, 0, lax.Precision.HIGHEST)
    for head in range(HEADS_HERE):
        sums = running_sum[:, head : head + 1]
        spread = sums - running_row[head : head + 1, :]
        query = query_ref[:, columns(head)]
        value = value_ref[:, columns(head)]
        scores = dot(query, key_ref[:, columns(head)], 1, 1)
        decayed = jnp.where(causal, jnp.exp(jnp.where(causal, spread, 0.0)), 0.0) * scores
        total = dot(decayed.astype(jnp.bfloat16), value, 1, 0)
        query_scaled = (query.astype(jnp.float32) * jnp.exp(sums)).astype(jnp.bfloat16)
        half, place = head // HALF, head_rows(head % HALF)
        mine = mine_ref[place, :].astype(jnp.float32)
        other = other_ref[place, :].astype(jnp.float32)
        prior = jnp.where(place_ref[CORE] == half, mine, other)
        fade = jnp.exp(endings[head : head + 1, :])
        passed = fade * prior + sibling_ref[head_rows(head), :].astype(jnp.float32)
        prior = jnp.where(second, passed, prior)
        total += dot(query_scaled, prior.astype(jnp.bfloat16), 1, 0)
        mean = jnp.mean(total * total, axis=1, keepdims=True)
        out_ref[:, columns(head)] = (total * lax.rsqrt(mean + norm_eps)).astype(jnp.bfloat16)


def unpack_kernel(moved_ref, order_ref, out_ref):
    for device in range(BLOCKS):
        head, quarter = place_of(device)
        out_ref[rows(quarter), columns(head)] = moved_ref[device]


def exchange(value):
    return lax.all_to_all(value, "ctx", split_axis=0, concat_axis=0, tiled=True)


def swap(value, step):
    return lax.ppermute(value, "ctx", [(d, d ^ step) for d in range(BLOCKS)])


def shards(lin_query, lin_key, lin_value, log_decay, soft_query, soft_key, soft_value):
    half = jnp.bfloat16
    shape = jax.ShapeDtypeStruct
    index = lax.axis_index("ctx").astype(jnp.int32)
    core = index % 2
    place = jnp.stack([2 * (index // X_STEP % 2) + core, core])
    width = HEADS_HERE * HEAD_DIM
    (packed,) = call(
        pack_kernel,
        [shape((BLOCKS, 3 * PIECE, HEAD_DIM), half)],
        (soft_query, soft_key, soft_value),
        1000,
        [pltpu.HBM] * 3,
        [pltpu.HBM],
        (
            pltpu.VMEM((3, TOKENS, width), half),
            pltpu.VMEM((3, BLOCKS, PIECE, HEAD_DIM), half),
            pltpu.SemaphoreType.DMA((2, 3)),
        ),
    )
    kv0 = exchange(packed)
    (states,) = call(
        states_kernel,
        [shape((width + 3 * HEADS_HERE, HEAD_DIM), half)],
        (lin_key, lin_value, log_decay),
        10**8,
    )
    sibling = swap(states, 1)
    on_core = [pltpu.SMEM] + [pltpu.VMEM] * 7
    (chip,) = call(
        chip_kernel,
        [shape((BLOCKS, SLICE + 8, HEAD_DIM), half)],
        (place, states, sibling),
        10**7,
        on_core[:3],
        scratch=(pltpu.VMEM((HALF, HEAD_DIM), jnp.float32),),
    )
    kv0, chip = lax.optimization_barrier((kv0, chip))
    half_blocks = BLOCKS // 2
    kv0a, kv0b, kv0c, kv0d = call(
        slice_kernel,
        [
            shape((blocks, 2 * PIECE, HEAD_DIM), half)
            for blocks in (half_blocks, half_blocks, half_blocks // 2, half_blocks // 2)
        ],
        (kv0,),
        0,
        [pltpu.VMEM],
        [pltpu.HBM] * 4,
        [pltpu.SemaphoreType.DMA((4,))],
    )
    kv2a = swap(kv0a, X_STEP)
    kv1a, kv1b = swap(kv0a, 1), swap(kv0b, 1)
    chips = exchange(chip)

    dma = pltpu.SemaphoreType.DMA
    token_shape = shape((8, HEAD_DIM), jnp.float32)
    state_shapes = [
        shape((len(LATE) * TILE_ROWS, HEAD_DIM), jnp.float32),
        shape((len(LATE) * TILE_ROWS, 2 * HEAD_DIM), jnp.float32),
    ]
    in_hbm, in_vmem, in_smem = pltpu.HBM, pltpu.VMEM, pltpu.SMEM
    best_a, total_a, token = call(
        first_kernel,
        [*state_shapes, token_shape],
        (place, kv0, kv1a, kv1b),
        0,
        [in_smem, in_vmem, in_hbm, in_hbm],
        [in_hbm, in_hbm, in_vmem],
        [*attention_space(2, 2), *work_space(LATE, range(TILES), 2), dma((2,)), dma((2, 2))],
        limit=32,
    )
    token, kv2a, kv0c, kv0d = lax.optimization_barrier((token, kv2a, kv0c, kv0d))
    kv3a = swap(kv2a, 1)
    kv2b = swap(kv0c, X_STEP), swap(kv0d, X_STEP)
    best_b, total_b, first, token = call(
        second_kernel,
        [*state_shapes, shape((half_blocks, PIECE, HEAD_DIM), half), token_shape],
        (place, kv0, kv1a, kv2a, kv3a, token),
        0,
        [in_smem, in_vmem, in_hbm, in_hbm, in_vmem, in_vmem],
        [in_hbm, in_hbm, in_hbm, in_vmem],
        [
            *attention_space(2, 4),
            *work_space(LATE, EARLY, 2),
            *work_space(EARLY, EARLY, 4),
            final_space(half_blocks),
            dma((2,)),
            dma((2,)),
            dma((len(EARLY),)),
        ],
        limit=40,
    )
    token, chips = lax.optimization_barrier((token, chips))
    token, *kv2b = lax.optimization_barrier((token, *kv2b))
    kv3b = [swap(part, 1) for part in kv2b]
    (scanned,) = call(scan_kernel, [shape((BLOCKS, SLICE, HEAD_DIM), half)], (chips,), 10**6)
    prior = exchange(scanned).reshape(HALF * HEAD_DIM, HEAD_DIM)
    (attended,) = call(
        third_kernel,
        [shape((BLOCKS, PIECE, HEAD_DIM), half)],
        (place, kv0, *kv2b, *kv3b, best_a, total_a, best_b, total_b, first, token),
        0,
        [in_smem, in_vmem, in_hbm, in_hbm, in_vmem, in_vmem, *[in_hbm] * 5, in_vmem],
        [in_hbm],
        [
            pltpu.VMEM((half_blocks, 2 * PIECE, HEAD_DIM), half),
            pltpu.VMEM((2, TILE_ROWS, TILE_ROWS), jnp.float32),
            *work_space(LATE, LATE, 2),
            pltpu.VMEM((2, len(LATE) * TILE_ROWS, HEAD_DIM), jnp.float32),
            pltpu.VMEM((2, len(LATE) * TILE_ROWS, 2 * HEAD_DIM), jnp.float32),
            final_space(BLOCKS),
            dma((2,)),
            dma((5,)),
            dma((1 + len(LATE),)),
        ],
        limit=32,
    )
    returned = exchange(attended)
    other_prior = swap(prior, 1)
    whole_out = shape((TOKENS, width), half)
    (lin_out,) = call(
        lightning_kernel,
        [whole_out],
        (place, lin_query, lin_key, lin_value, log_decay, prior, other_prior, sibling),
        2 * 10**8,
        on_core[:8],
    )
    token, returned = lax.optimization_barrier((lin_out[0:8, 0:HEAD_DIM], returned))
    (soft_out,) = call(unpack_kernel, [whole_out], (returned, token), 1000)
    return (lin_out, soft_out)


def solution(mesh):
    spec = P("ctx", "head")
    return jax.shard_map(
        shards, mesh=mesh, in_specs=(spec,) * 7, out_specs=(spec, spec), check_vma=False
    )
```
